32 devices in a mesh: row: 8 (over z, y), col: 4 (over x, core).
Axes of the slice: x: 2, y: 2, z: 4, core: 2. Of those that a mesh axis runs over, the one named last changes fastest.
Arguments:
- tokens: bfloat16 [1600, 8192], P('row', 'col')
- ln1_gain: float32 [1600], P('row'), may hold values from 0.25 to 1.75
- ln1_shift: float32 [1600], P('row'), may hold values from -4 to 4
- weight_qkv: bfloat16 [1600, 4800], P('row', 'col'), may hold values from -0.21875 to 0.21875
- bias_qkv: float32 [4800], P('col'), may hold values from -4 to 4
- weight_out: bfloat16 [1600, 1600], P('row', 'col'), may hold values from -0.625 to 0.625
- bias_out: float32 [1600], P('row'), may hold values from -6 to 6
- ln2_gain: float32 [1600], P('row'), may hold values from 0.25 to 1.75
- ln2_shift: float32 [1600], P('row'), may hold values from -4 to 4
- weight_up: bfloat16 [1600, 6400], P('row', 'col'), may hold values from -0.15625 to 0.15625
- bias_up: float32 [6400], P('col'), may hold values from -6 to 6
- weight_down: bfloat16 [1600, 6400], P('row', 'col'), may hold values from -0.109375 to 0.109375
- bias_down: float32 [1600], P('row'), may hold values from -6 to 6
- cotangent: bfloat16 [1600, 8192], P('row', 'col')
Outputs:
- block_output: bfloat16 [1600, 8192], P('row', 'col')
- grad_tokens: float32 [1600, 8192], P('row', 'col')
- grad_ln1_gain: float32 [1600], P('row')
- grad_ln1_shift: float32 [1600], P('row')
- grad_weight_qkv: float32 [1600, 4800], P('row', 'col')
- grad_bias_qkv: float32 [4800], P('col')
- grad_weight_out: float32 [1600, 1600], P('row', 'col')
- grad_bias_out: float32 [1600], P('row')
- grad_ln2_gain: float32 [1600], P('row')
- grad_ln2_shift: float32 [1600], P('row')
- grad_weight_up: float32 [1600, 6400], P('row', 'col')
- grad_bias_up: float32 [6400], P('col')
- grad_weight_down: float32 [1600, 6400], P('row', 'col')
- grad_bias_down: float32 [1600], P('row')
The draws below stay inside these ranges and needn't reach their ends.
All inputs are finite; a program needn't handle non-finite values.
Results may differ from the reference program's by a relative error of at most 0.012.
The reference program's roundings to bfloat16 on the way count: a program that leaves them out, or rounds other values in their place, can miss the bound.
Values may be sent and summed in bfloat16 or wider, within the bound.
A program may use at most 256 MiB of HBM per device.

```python
import jax
import jax.numpy as jnp
from jax import lax

D = 1600
H = 25
HD = 64
FF = 6400
L = 1024
SEQS = 8
TOKENS = 8192


def scaled_field(key, row_total, col_total):
    row_key, value_key = jax.random.split(key)
    row_scale = jnp.exp(jax.random.uniform(row_key, (row_total, 1), jnp.float32, jnp.log(0.3), jnp.log(3.0)))
    position = jnp.arange(col_total, dtype=jnp.float32)[None, :]
    col_scale = 0.5 + position / col_total
    values = jax.random.normal(value_key, (row_total, col_total), jnp.float32)
    return values * row_scale * col_scale


def draw_tokens(key, part):
    return scaled_field(jax.random.fold_in(key, 11), TOKENS, D).T.astype(jnp.bfloat16)


def draw_cotangent(key, part):
    return scaled_field(jax.random.fold_in(key, 29), TOKENS, D).T.astype(jnp.bfloat16)


def levels(key, extent, cuts, smallest, largest):
    def one(dim, shards_of):
        steps = jax.random.uniform(jax.random.fold_in(jax.random.fold_in(key, 6), dim), (shards_of,), jnp.float32, smallest / len(cuts), largest / len(cuts))
        return jnp.repeat(jnp.exp(steps), extent[dim] // shards_of).reshape((-1,) + (1,) * (len(extent) - dim - 1))

    factor_of = one(*cuts[0])
    for cut in cuts[1:]:
        factor_of = factor_of * one(*cut)
    return factor_of


def gaussian(own_key, shape, width, reach, pieces=(), kind=jnp.bfloat16):
    values = width * jax.random.normal(own_key, shape, jnp.float32)
    if pieces:
        values = values * levels(own_key, shape, pieces, -0.22, 0.18)
    return jnp.clip(values, -reach, reach).astype(kind)


def setup_inputs(seed: int = 0) -> dict:
    seeds = jax.random.split(jax.random.key(seed), 15)
    return {
        "tokens": draw_tokens(jax.random.fold_in(seeds[14], 71), 0),
        "ln1_gain": jnp.clip(1.0 + 0.15 * jax.random.normal(seeds[1], (D,), jnp.float32), 0.25, 1.75),
        "ln1_shift": gaussian(seeds[2], (D,), 0.3, 4.0, ((0, 8),), jnp.float32),
        "weight_qkv": gaussian(seeds[3], (D, 3 * D), (D // 2) ** -0.5, 0.21875, ((0, 8), (1, 4))),
        "bias_qkv": gaussian(seeds[4], (3 * D,), 0.3, 4.0, ((0, 4),), jnp.float32),
        "weight_out": gaussian(seeds[5], (D, D), (D // 16) ** -0.5, 0.625, ((0, 8), (1, 4))),
        "bias_out": gaussian(seeds[6], (D,), 0.5, 6.0, ((0, 8),), jnp.float32),
        "ln2_gain": jnp.clip(1.0 + 0.15 * jax.random.normal(seeds[7], (D,), jnp.float32), 0.25, 1.75),
        "ln2_shift": gaussian(seeds[8], (D,), 0.3, 4.0, ((0, 8),), jnp.float32),
        "weight_up": gaussian(seeds[9], (D, FF), D ** -0.5, 0.15625, ((0, 8), (1, 4))),
        "bias_up": gaussian(seeds[10], (FF,), 0.5, 6.0, ((0, 4),), jnp.float32),
        "weight_down": gaussian(seeds[11], (D, FF), (FF // 2) ** -0.5, 0.109375, ((0, 8), (1, 4))),
        "bias_down": gaussian(seeds[12], (D,), 0.5, 6.0, ((0, 8),), jnp.float32),
        "cotangent": draw_cotangent(jax.random.fold_in(seeds[14], 71), 0),
    }


epsilon = 1e-05
excluded = -1e+30

@jax.custom_vjp
def low(v):
    return lax.optimization_barrier(v.astype(jnp.bfloat16)).astype(jnp.float32)

@jax.custom_vjp
def low_back(v):
    return v

def low_keep(v):
    return (low(v), None)

def low_pass(kept, grad):
    return (grad,)

def back_keep(v):
    return (v, None)

def back_low(kept, grad):
    return (low(grad),)
low.defvjp(low_keep, low_pass)
low_back.defvjp(back_keep, back_low)

def layer_norm(values, norm_gain, norm_shift):
    row_mean = lax.optimization_barrier(jnp.mean(values, axis=-1, keepdims=True))
    centred = values - row_mean
    variance = lax.optimization_barrier(jnp.mean(centred * centred, axis=-1, keepdims=True))
    return centred * lax.rsqrt(variance + epsilon) * norm_gain + norm_shift

def product(left_side, right_side):
    return jnp.dot(left_side, right_side, precision=lax.Precision.HIGHEST)

def attend(block):
    query_rows = block[:, 0]
    key_rows = block[:, 1]
    value_rows = block[:, 2]
    allowed = jnp.arange(L)[:, None] >= jnp.arange(L)[None, :]
    scores = jnp.einsum('qdh,kdh->hqk', query_rows, key_rows, precision=lax.Precision.HIGHEST) * HD ** (-0.5)
    scores = low_back(scores)
    scores = jnp.where(allowed[None], scores, excluded)
    peak = lax.optimization_barrier(jnp.max(scores, axis=-1, keepdims=True))
    weights = jnp.exp(scores - peak)
    weights = low(weights / lax.optimization_barrier(jnp.sum(weights, axis=-1, keepdims=True)))
    attended = jnp.einsum('hqk,kdh->qdh', weights, value_rows, precision=lax.Precision.HIGHEST)
    return attended.reshape(L, HD * H)

def forward(inputs, gain_one, shift_one, weight_qkv, bias_qkv, weight_out, bias_out, gain_two, shift_two, weight_up, bias_up, weight_down, bias_down):
    normed_in = low(layer_norm(inputs, gain_one, shift_one))
    qkv = low_back(low(product(normed_in, weight_qkv) + bias_qkv))
    blocks = qkv.reshape(SEQS, L, 3, HD, H)
    attended = lax.map(jax.checkpoint(attend), blocks).reshape(TOKENS, HD * H)
    attended = low_back(low(attended))
    branch_attn = low_back(product(attended, weight_out) + bias_out)
    residual_mid = inputs + branch_attn
    normed_mid = low(layer_norm(residual_mid, gain_two, shift_two))
    hidden_pre = low_back(product(normed_mid, weight_up) + bias_up)
    hidden = low(jax.nn.gelu(hidden_pre, approximate=True))
    return residual_mid + product(hidden, weight_down) + bias_down

def forward_major(inputs_major, gain_one, shift_one, weight_qkv, bias_qkv, weight_out_major, bias_out, gain_two, shift_two, weight_up, bias_up, weight_down_major, bias_down):
    result = forward(inputs_major.T, gain_one, shift_one, weight_qkv, bias_qkv, weight_out_major.T, bias_out, gain_two, shift_two, weight_up, bias_up, weight_down_major.T, bias_down)
    return result.T

def reference(tokens, ln1_gain, ln1_shift, weight_qkv, bias_qkv, weight_out, bias_out, ln2_gain, ln2_shift, weight_up, bias_up, weight_down, bias_down, cotangent):
    primals = (tokens, ln1_gain, ln1_shift, weight_qkv, bias_qkv, weight_out, bias_out, ln2_gain, ln2_shift, weight_up, bias_up, weight_down, bias_down)
    primals = tuple((array.astype(jnp.float32) for array in primals))
    result, pullback = jax.vjp(forward_major, *primals)
    grads = pullback(cotangent.astype(jnp.float32))
    return (result.astype(jnp.bfloat16), grads[0], grads[1], grads[2], grads[3], grads[4], grads[5], grads[6], grads[7], grads[8], grads[9], grads[10], grads[11], grads[12])
```

```python
import jax
import jax.numpy as jnp
from jax import lax
from jax.sharding import PartitionSpec as P

D = 1600
H = 25
HD = 64
L = 1024
CHANNELS = 3 * HD

epsilon = 1e-05
excluded = -1e30

TN = (((0,), (0,)), ((), ()))
NN = (((1,), (0,)), ((), ()))
NT = (((1,), (1,)), ((), ()))


def product(left, right, dims):
    return lax.dot_general(left, right, dims, preferred_element_type=jnp.float32)


def norm_stats(values):
    mean = jnp.mean(values, axis=0, keepdims=True)
    centred = values - mean
    scale = lax.rsqrt(jnp.mean(centred * centred, axis=0, keepdims=True) + epsilon)
    return centred * scale, scale


def norm_backward(gradient, centred, scale, gain):
    scaled = gradient * gain
    adjusted = (
        scaled
        - jnp.mean(scaled, axis=0, keepdims=True)
        - centred * jnp.mean(scaled * centred, axis=0, keepdims=True)
    )
    return adjusted * scale, jnp.sum(gradient * centred, axis=1), jnp.sum(gradient, axis=1)


def block_order(rows, cols):
    return [(q * cols + c, c * rows + q) for q in range(rows) for c in range(cols)]


def to_blocks(values, rows, cols):
    k, feats, toks = values.shape
    split = values.reshape(k, feats, rows, toks // rows)
    got = lax.all_to_all(split, "row", split_axis=2, concat_axis=1)
    got = got.reshape(k, rows * feats, toks // rows)
    return lax.ppermute(got, ("row", "col"), block_order(rows, cols))


def from_blocks(values, rows, cols):
    back = [(b, a) for a, b in block_order(rows, cols)]
    got = lax.ppermute(values, ("row", "col"), back)
    feats, toks = values.shape
    got = got.reshape(rows, feats // rows, toks)
    got = lax.all_to_all(got, "row", split_axis=0, concat_axis=1)
    return got.reshape(feats // rows, rows * toks)


def regroup_matrix(channels, slots, cols):
    source = jnp.arange(channels * H, dtype=jnp.int32)
    channel, head = source // H, source % H
    target = ((head % cols) * slots + head // cols) * channels + channel
    return (
        target[:, None] == jnp.arange(cols * slots * channels, dtype=jnp.int32)[None, :]
    ).astype(jnp.bfloat16)


def group_heads(weight, matrix, cols):
    moved = product(weight, matrix, NN).astype(jnp.bfloat16)
    moved = moved.reshape(moved.shape[0], cols, -1)
    got = lax.all_to_all(moved, "col", split_axis=1, concat_axis=1, tiled=True)
    return got.reshape(got.shape[0], -1)


def ungroup_heads(gradient, matrix, cols):
    moved = gradient.reshape(gradient.shape[0], cols, -1)
    got = lax.all_to_all(moved, "col", split_axis=1, concat_axis=1, tiled=True)
    return product(got.reshape(got.shape[0], -1), matrix, NT)


def head_rows(values, cols, slots):
    rest = values.shape[1:]
    split = values.reshape(cols, slots, -1, *rest)
    return jnp.moveaxis(split, 0, 1).reshape(slots, -1, *rest)


def flat_rows(values, cols, slots):
    rest = values.shape[2:]
    split = values.reshape(slots, cols, -1, *rest)
    return jnp.moveaxis(split, 0, 1).reshape(-1, *rest)


def attend_forward(heads):
    allowed = jnp.arange(L)[:, None] <= jnp.arange(L)[None, :]
    outs, logs = [], []
    for s in range(heads.shape[0]):
        query, key, value = heads[s, :HD], heads[s, HD : 2 * HD], heads[s, 2 * HD :]
        scores = product(key, query, TN) * HD ** (-0.5)
        scores = jnp.where(allowed, scores, excluded)
        peak = jnp.max(scores, axis=0, keepdims=True)
        weights = jnp.exp(scores - peak)
        total = jnp.sum(weights, axis=0, keepdims=True)
        low = (weights / total).astype(jnp.bfloat16)
        outs.append(product(value, low, NN).astype(jnp.bfloat16))
        logs.append(peak + jnp.log(total))
    return jnp.stack(outs), jnp.stack(logs)


def attend_backward(heads, grads, logs):
    allowed = jnp.arange(L)[:, None] <= jnp.arange(L)[None, :]
    outs = []
    for s in range(heads.shape[0]):
        query, key, value = heads[s, :HD], heads[s, HD : 2 * HD], heads[s, 2 * HD :]
        grad = grads[s]
        scores = product(key, query, TN) * HD ** (-0.5)
        scores = jnp.where(allowed, scores, excluded)
        weights = jnp.exp(scores - logs[s])
        grad_value = product(grad, weights.astype(jnp.bfloat16), NT)
        grad_weights = product(value, grad, TN)
        inner = jnp.sum(weights * grad_weights, axis=0, keepdims=True)
        low = (weights * (grad_weights - inner)).astype(jnp.bfloat16)
        grad_query = product(key, low, NN) * HD ** (-0.5)
        grad_key = product(query, low, NT) * HD ** (-0.5)
        outs.append(jnp.concatenate([grad_query, grad_key, grad_value], axis=0).astype(jnp.bfloat16))
    return jnp.stack(outs)


def spread(values):
    return lax.all_gather(values, "col", axis=1, tiled=True)


def share(values):
    return lax.psum_scatter(
        values.astype(jnp.bfloat16), "col", scatter_dimension=1, tiled=True
    ).astype(jnp.float32)


def whole_weight(weight):
    return lax.all_gather(weight, "row", axis=0, tiled=True)


def share_weight(gradient):
    return lax.psum_scatter(gradient.astype(jnp.bfloat16), "row", scatter_dimension=0, tiled=True)


def body(
    tokens,
    ln1_gain,
    ln1_shift,
    weight_qkv,
    bias_qkv,
    weight_out,
    bias_out,
    ln2_gain,
    ln2_shift,
    weight_up,
    bias_up,
    weight_down,
    bias_down,
    cotangent,
):
    rows, cols = lax.axis_size("row"), lax.axis_size("col")
    row, col = lax.axis_index("row"), lax.axis_index("col")
    slots = (H + cols - 1) // cols
    qkv_channels = CHANNELS // cols
    out_channels = HD // cols

    vectors = lax.all_gather(
        jnp.stack([ln1_gain, ln1_shift, bias_out, ln2_gain, ln2_shift, bias_down]),
        "row",
        axis=1,
        tiled=True,
    )[:, :, None]
    gain_one, shift_one, out_bias, gain_two, shift_two, down_bias = vectors

    biases = lax.all_gather(bias_qkv, "col", axis=0, tiled=True).reshape(CHANNELS, H)
    biases = jnp.pad(biases, ((0, 0), (0, slots * cols - H))).reshape(CHANNELS, slots, cols)
    qkv_bias = lax.dynamic_index_in_dim(biases, col, axis=2, keepdims=False).T[:, :, None]

    qkv_matrix = regroup_matrix(qkv_channels, slots, cols)
    out_matrix = regroup_matrix(out_channels, slots, cols)
    qkv_weight = whole_weight(group_heads(weight_qkv, qkv_matrix, cols))
    out_weight = whole_weight(group_heads(weight_out, out_matrix, cols))
    up_weight = whole_weight(weight_up)
    down_weight = whole_weight(weight_down)

    own = to_blocks(jnp.stack([tokens, cotangent]), rows, cols)
    both = lax.all_gather(own, "col", axis=2, tiled=True)
    residual_own = own[0].astype(jnp.float32)
    cot_own = own[1].astype(jnp.float32)
    cot = both[1]

    normed_in = (norm_stats(both[0].astype(jnp.float32))[0] * gain_one + shift_one).astype(
        jnp.bfloat16
    )
    qkv = product(qkv_weight, normed_in, TN)
    heads = (head_rows(qkv, cols, slots) + qkv_bias).astype(jnp.bfloat16)
    attended, logs = attend_forward(heads)
    attended = flat_rows(attended, cols, slots)
    residual_mid = residual_own + share(product(out_weight, attended, NN)) + out_bias
    centred_mid, scale_mid = norm_stats(residual_mid)
    normed_mid = spread((centred_mid * gain_two + shift_two).astype(jnp.bfloat16))
    hidden_pre = product(up_weight, normed_mid, TN) + bias_up[:, None]
    hidden = jax.nn.gelu(hidden_pre, approximate=True).astype(jnp.bfloat16)
    block_output = (
        residual_mid + share(product(down_weight, hidden, NN)) + down_bias
    ).astype(jnp.bfloat16)
    block_output = from_blocks(block_output, rows, cols)

    grad_hidden = product(down_weight, cot, TN)
    gelu_back = jax.vjp(lambda inner: jax.nn.gelu(inner, approximate=True), hidden_pre)[1]
    grad_pre = gelu_back(grad_hidden)[0].astype(jnp.bfloat16)
    grad_weight_down = share_weight(product(cot, hidden, NT)).astype(jnp.float32)
    grad_normed_mid = share(product(up_weight, grad_pre, NN))
    grad_weight_up = share_weight(product(normed_mid, grad_pre, NT)).astype(jnp.float32)
    up_part = jnp.sum(grad_pre, axis=1, dtype=jnp.float32)
    grad_norm_mid, gain_two_part, shift_two_part = norm_backward(
        grad_normed_mid, centred_mid, scale_mid, gain_two
    )
    grad_residual_mid = cot_own + grad_norm_mid
    grad_branch_own = grad_residual_mid.astype(jnp.bfloat16)
    grad_branch = spread(grad_branch_own)
    grad_attended = product(out_weight, grad_branch, TN).astype(jnp.bfloat16)
    grad_weight_out = ungroup_heads(
        share_weight(product(grad_branch, attended, NT)), out_matrix, cols
    )
    grad_qkv = attend_backward(heads, head_rows(grad_attended, cols, slots), logs)
    grad_qkv = flat_rows(grad_qkv, cols, slots)
    grad_weight_qkv = ungroup_heads(
        share_weight(product(normed_in, grad_qkv, NT)), qkv_matrix, cols
    )
    qkv_part = jnp.sum(grad_qkv, axis=1, dtype=jnp.float32)
    grad_normed_in = share(product(qkv_weight, grad_qkv, NN))
    centred_in, scale_in = norm_stats(residual_own)
    grad_norm_in, gain_one_part, shift_one_part = norm_backward(
        grad_normed_in, centred_in, scale_in, gain_one
    )
    grad_tokens = from_blocks(grad_residual_mid + grad_norm_in, rows, cols)

    features = jnp.stack(
        [
            gain_one_part,
            shift_one_part,
            jnp.sum(grad_branch_own, axis=1, dtype=jnp.float32),
            gain_two_part,
            shift_two_part,
            jnp.sum(cot_own, axis=1),
        ]
    )
    features = lax.psum(features, ("row", "col"))
    features = lax.dynamic_slice_in_dim(features, row * (D // rows), D // rows, axis=1)
    units = lax.psum(jnp.concatenate([up_part, qkv_part]), "row")
    grad_bias_up = units[: up_part.shape[0]]
    spread_bias = lax.all_gather(
        units[up_part.shape[0] :].reshape(cols, slots, qkv_channels), "col", axis=0
    )
    mine = lax.dynamic_index_in_dim(spread_bias, col, axis=1, keepdims=False)
    grad_bias_qkv = mine.transpose(2, 1, 0).reshape(qkv_channels, slots * cols)[:, :H].reshape(-1)
    return (
        block_output,
        grad_tokens,
        features[0],
        features[1],
        grad_weight_qkv,
        grad_bias_qkv,
        grad_weight_out,
        features[2],
        features[3],
        features[4],
        grad_weight_up,
        grad_bias_up,
        grad_weight_down,
        features[5],
    )


def solution(mesh):
    both, row, col = P("row", "col"), P("row"), P("col")
    in_specs = (both, row, row, both, col, both, row, row, row, both, col, both, row, both)
    out_specs = (both, both, row, row, both, col, both, row, row, row, both, col, both, row)
    return jax.shard_map(body, mesh=mesh, in_specs=in_specs, out_specs=out_specs, check_vma=False)
```

```python
import functools

import jax
import jax.numpy as jnp
from jax import lax
from jax.experimental import pallas as pl
from jax.experimental.pallas import tpu as pltpu
from jax.sharding import PartitionSpec as P

D = 1600
H = 25
HD = 64
L = 1024
CHANNELS = 3 * HD
QB = 256

epsilon = 1e-05
excluded = -1e30

TN = (((0,), (0,)), ((), ()))
NN = (((1,), (0,)), ((), ()))
NT = (((1,), (1,)), ((), ()))
MESH = pl.DeviceIdType.MESH
ANY = pl.BlockSpec(memory_space=pl.ANY)
VMEM = pl.BlockSpec(memory_space=pltpu.VMEM)
LIMIT = 60 * 2**20
f32 = jnp.float32
bf16 = jnp.bfloat16


def product(left, right, dims):
    return lax.dot_general(left, right, dims, preferred_element_type=f32)


def remote(src, dst, send, recv, device):
    return pltpu.make_async_remote_copy(
        src_ref=src,
        dst_ref=dst,
        send_sem=send,
        recv_sem=recv,
        device_id=device,
        device_id_type=MESH,
    )


def meet(devices):
    sem = pltpu.get_barrier_semaphore()
    for device in devices:
        pl.semaphore_signal(sem, inc=1, device_id=device, device_id_type=MESH)
    pl.semaphore_wait(sem, len(devices))


def lanes(index, width):
    return pl.ds(pl.multiple_of(index * width, 128), width)


class Place:
    def __init__(self, rows, cols):
        self.R, self.C, self.A, self.X = rows, cols, rows // 2, cols // 2
        self.r, self.c = lax.axis_index("row"), lax.axis_index("col")
        self.a, self.b = self.r // 2, lax.rem(self.r, 2)
        self.x, self.k = self.c // 2, lax.rem(self.c, 2)
        self.core = (self.r, self.x * 2 + 1 - self.k)
        self.pair = (self.a * 2 + 1 - self.b, self.c)

    def ahead(self, o):
        return lax.rem(self.a + o, self.A)

    def behind(self, o):
        return lax.rem(self.a - o + self.A, self.A)

    def line(self, o):
        return (self.ahead(o) * 2 + self.b, self.c)

    def x_ahead(self, o):
        return lax.rem(self.x + o, self.X)

    def x_behind(self, o):
        return lax.rem(self.x - o + self.X, self.X)

    def side(self, o):
        return (self.r, self.x_ahead(o) * 2 + self.k)

    def col_peers(self):
        return [self.core] + [self.side(o) for o in range(1, self.X)]

    def row_peers(self):
        return [self.pair] + [self.line(o) for o in range(1, self.A)]


class Spread:
    def __init__(self, p, own, full, width, send, recv):
        self.p, self.own, self.full, self.width = p, own, full, width
        self.send, self.recv = send, recv

    def part(self, block):
        return self.full.at[..., lanes(block, self.width)]

    def side_copy(self, o):
        return remote(
            self.own, self.part(self.p.c), self.send.at[o], self.recv.at[o], self.p.side(o)
        )

    def core_copy(self, o):
        p = self.p
        block = p.c if o == 0 else p.x_behind(o) * 2 + p.k
        src = self.own if o == 0 else self.part(block)
        i = p.X + o
        return remote(src, self.part(block), self.send.at[i], self.recv.at[i], p.core)

    def local(self):
        i = 2 * self.p.X
        return pltpu.make_async_copy(self.own, self.part(self.p.c), self.send.at[i])

    def start(self):
        for o in range(1, self.p.X):
            self.side_copy(o).start()
        self.core_copy(0).start()
        self.local().start()

    def forward(self):
        for o in range(1, self.p.X):
            self.side_copy(o).wait_recv()
            self.core_copy(o).start()

    def finish(self):
        for o in range(self.p.X):
            self.core_copy(o).wait()
        for o in range(1, self.p.X):
            self.side_copy(o).wait_send()
        self.local().wait()


def spread_sems(cols):
    return [pltpu.SemaphoreType.DMA((cols + 1,)), pltpu.SemaphoreType.DMA((cols + 1,))]


class Share:
    def __init__(self, p, part, core_in, side_out, side_in, send, recv):
        self.p, self.part, self.core_in = p, part, core_in
        self.side_out, self.side_in, self.send, self.recv = side_out, side_in, send, recv

    def core_copy(self, x):
        p = self.p
        return remote(
            self.part.at[x * 2 + 1 - p.k],
            self.core_in.at[x],
            self.send.at[x],
            self.recv.at[x],
            p.core,
        )

    def side_copy(self, o):
        p = self.p
        i = p.X + o - 1
        return remote(
            self.side_out.at[o - 1],
            self.side_in.at[o - 1],
            self.send.at[i],
            self.recv.at[i],
            p.side(o),
        )

    def start(self):
        for x in range(self.p.X):
            self.core_copy(x).start()

    def middle(self):
        p = self.p
        for x in range(p.X):
            self.core_copy(x).wait_recv()
        for o in range(1, p.X):
            x = p.x_ahead(o)

            def add(d, carry, x=x, o=o):
                total = self.part[x * 2 + p.k, d].astype(f32) + self.core_in[x, d].astype(f32)
                self.side_out[o - 1, d] = total.astype(bf16)
                return carry

            lax.fori_loop(0, p.R, add, 0)
            self.side_copy(o).start()

    def arrive(self):
        for o in range(1, self.p.X):
            self.side_copy(o).wait_recv()

    def total(self, d):
        p = self.p
        result = self.part[p.c, d].astype(f32) + self.core_in[p.x, d].astype(f32)
        for o in range(1, p.X):
            result = result + self.side_in[o - 1, d].astype(f32)
        return result

    def finish(self):
        for x in range(self.p.X):
            self.core_copy(x).wait_send()
        for o in range(1, self.p.X):
            self.side_copy(o).wait_send()


def share_scratch(rows, cols, feats, width):
    half = cols // 2
    return [
        pltpu.VMEM((cols, rows, feats, width), bf16),
        pltpu.VMEM((half, rows, feats, width), bf16),
        pltpu.VMEM((half - 1, rows, feats, width), bf16),
        pltpu.VMEM((half - 1, rows, feats, width), bf16),
        pltpu.SemaphoreType.DMA((cols - 1,)),
        pltpu.SemaphoreType.DMA((cols - 1,)),
    ]


def fill_partial(part, weight, act, cols, rows, width):
    def one(d, carry):
        for j in range(cols):
            part[j, d] = product(
                weight[d], act[:, j * width : (j + 1) * width], NN
            ).astype(bf16)
        return carry

    lax.fori_loop(0, rows, one, 0)


class Reduce:
    def __init__(self, p, left, right, pair_out, pair_in, line_in, sems):
        self.p, self.left, self.right = p, left, right
        self.pair_out, self.pair_in, self.line_in = pair_out, pair_in, line_in
        self.psend, self.precv, self.zsend, self.zrecv = sems

    def chunk(self, d):
        return product(self.left[d], self.right[...], NT)

    def pair_copy(self, i):
        return remote(
            self.pair_out.at[i],
            self.pair_in.at[i],
            self.psend.at[i],
            self.precv.at[i],
            self.p.pair,
        )

    def line_copy(self, o):
        return remote(
            self.pair_in.at[self.p.ahead(o)],
            self.line_in.at[o - 1],
            self.zsend.at[o - 1],
            self.zrecv.at[o - 1],
            self.p.line(o),
        )

    def send_pair(self):
        p = self.p

        def one(o, carry):
            i = p.ahead(o + 1)
            self.pair_out[i] = self.chunk(i * 2 + 1 - p.b).astype(bf16)
            self.pair_copy(i).start()
            return carry

        lax.fori_loop(0, p.A, one, 0)

    def send_line(self):
        p = self.p
        for o in range(1, p.A):
            i = p.ahead(o)
            value = self.chunk(i * 2 + p.b)
            self.pair_copy(i).wait_recv()
            self.pair_in[i] = (value + self.pair_in[i].astype(f32)).astype(bf16)
            self.line_copy(o).start()

    def finish(self, out):
        p = self.p
        value = self.chunk(p.r)
        self.pair_copy(p.a).wait_recv()
        value = value + self.pair_in[p.a].astype(f32)
        for o in range(1, p.A):
            self.line_copy(o).wait_recv()
            value = value + self.line_in[o - 1].astype(f32)
        out[...] = value
        for i in range(p.A):
            self.pair_copy(i).wait_send()
        for o in range(1, p.A):
            self.line_copy(o).wait_send()


def reduce_scratch(rows, feats, width):
    half = rows // 2
    return [
        pltpu.VMEM((half, feats, width), bf16),
        pltpu.VMEM((half, feats, width), bf16),
        pltpu.VMEM((half - 1, feats, width), bf16),
        pltpu.SemaphoreType.DMA((half,)),
        pltpu.SemaphoreType.DMA((half,)),
        pltpu.SemaphoreType.DMA((half - 1,)),
        pltpu.SemaphoreType.DMA((half - 1,)),
    ]


def home(p, q):
    block = p.c * p.R + q
    return (block // p.C, lax.rem(block, p.C))


def own_block(p):
    block = p.r * p.C + p.c
    return block // p.R, lax.rem(block, p.R)


def equal(left, right):
    return jnp.logical_and(left[0] == right[0], left[1] == right[1])


def exchange_copies(p, src, dst, send, recv):
    out = []
    for o in range(1, p.C):
        to = lax.rem(p.c + o, p.C)
        out.append(remote(src.at[to], dst.at[p.c], send.at[o], recv.at[o], (p.r, to)))
    return out


def all_col(p):
    return [(p.r, lax.rem(p.c + o, p.C)) for o in range(1, p.C)]


def all_row(p):
    return [(lax.rem(p.r + o, p.R), p.c) for o in range(1, p.R)]


def enter_kernel(
    rows, cols, tokcot, wq, wo, bias, vec, both, own, wq_o, wo_o, bias_o, vec_o,
    send, recv, local, csend, crecv, ssend, srecv, vsend, vrecv,
):
    p = Place(rows, cols)
    me = (p.r, p.c)
    width = own.shape[-1]
    source_col, _ = own_block(p)
    sources = [(q, source_col) for q in range(rows)]
    targets = [home(p, q) for q in range(rows)]
    meet(sources + targets + all_col(p) + all_row(p))

    swaps = []
    for i, (src, dst) in enumerate(((wq, wq_o), (wo, wo_o), (bias, bias_o))):
        swaps += exchange_copies(p, src, dst, csend.at[i], crecv.at[i])
    for copy in swaps:
        copy.start()
    keeps = [
        pltpu.make_async_copy(src.at[p.c], dst.at[p.c], local.at[i])
        for i, (src, dst) in enumerate(((wq, wq_o), (wo, wo_o), (bias, bias_o)))
    ]
    keeps.append(pltpu.make_async_copy(vec, vec_o.at[p.r], local.at[3]))
    for copy in keeps:
        copy.start()

    def outgoing(q):
        return remote(
            tokcot.at[:, :, q * width : (q + 1) * width],
            own.at[:, p.r],
            send.at[q],
            recv.at[p.r],
            targets[q],
        )

    def staying(q):
        return pltpu.make_async_copy(
            tokcot.at[:, :, q * width : (q + 1) * width], own.at[:, p.r], local.at[4]
        )

    for q in range(rows):
        here = equal(targets[q], me)

        @pl.when(here)
        def _():
            staying(q).start()

        @pl.when(jnp.logical_not(here))
        def _():
            outgoing(q).start()

    vecs = [
        remote(vec, vec_o.at[p.r], vsend.at[o], vrecv.at[o], peer)
        for o, peer in enumerate(all_row(p))
    ]
    for copy in vecs:
        copy.start()

    for q in range(rows):
        here = equal(sources[q], me)

        @pl.when(here)
        def _():
            staying(0).wait()

        @pl.when(jnp.logical_not(here))
        def _():
            remote(
                tokcot.at[:, :, 0:width], own.at[:, q], send.at[0], recv.at[q], sources[q]
            ).wait_recv()

    gather = Spread(p, own, both, width, ssend, srecv)
    gather.start()
    gather.forward()
    for copy in swaps + vecs:
        copy.wait()
    for copy in keeps:
        copy.wait()
    gather.finish()
    for q in range(rows):

        @pl.when(jnp.logical_not(equal(targets[q], me)))
        def _():
            outgoing(q).wait_send()


def leave_kernel(
    rows, cols, blocks, gq, go, feat, units, res, gq_o, go_o, feat_o, units_o,
    feat_in, feat_sum, send, recv, local, csend, crecv, fsend, frecv, usend, urecv,
):
    p = Place(rows, cols)
    me = (p.r, p.c)
    width = blocks.shape[-1]
    target_col, place = own_block(p)
    targets = [(q, target_col) for q in range(rows)]
    sources = [home(p, q) for q in range(rows)]
    meet(sources + targets + all_col(p) + all_row(p))

    feats, unit_copies = [], []
    for o in range(1, rows):
        to = lax.rem(p.r + o, rows)
        feats.append(
            remote(feat.at[to], feat_in.at[o], fsend.at[o], frecv.at[o], (to, p.c))
        )
        unit_copies.append(
            remote(units, units_o.at[p.r], usend.at[o], urecv.at[o], (to, p.c))
        )
    for copy in feats + unit_copies:
        copy.start()
    swaps = []
    for i, (src, dst) in enumerate(((gq, gq_o), (go, go_o))):
        swaps += exchange_copies(p, src, dst, csend.at[i], crecv.at[i])
    for copy in swaps:
        copy.start()
    keeps = [
        pltpu.make_async_copy(src.at[p.c], dst.at[p.c], local.at[i])
        for i, (src, dst) in enumerate(((gq, gq_o), (go, go_o)))
    ]
    keeps.append(pltpu.make_async_copy(units, units_o.at[p.r], local.at[2]))
    for copy in keeps:
        copy.start()

    def slot(q):
        return res.at[:, :, lanes(q, width)]

    def outgoing(q):
        return remote(blocks.at[:, q], slot(place), send.at[q], recv.at[place], targets[q])

    def staying(q):
        return pltpu.make_async_copy(blocks.at[:, q], slot(place), local.at[3])

    for q in range(rows):
        here = equal(targets[q], me)

        @pl.when(here)
        def _():
            staying(q).start()

        @pl.when(jnp.logical_not(here))
        def _():
            outgoing(q).start()

    total = feat[p.r]
    for o, copy in enumerate(feats):
        copy.wait_recv()
        total = total + feat_in[o + 1]
    feat_sum[...] = total
    feat_o[p.c] = total
    sums = [
        remote(feat_sum, feat_o.at[p.c], csend.at[2, o + 1], crecv.at[2, o + 1], peer)
        for o, peer in enumerate(all_col(p))
    ]
    for copy in sums:
        copy.start()

    for q in range(rows):
        here = equal(sources[q], me)

        @pl.when(here)
        def _():
            staying(0).wait()

        @pl.when(jnp.logical_not(here))
        def _():
            remote(
                blocks.at[:, 0], slot(q), send.at[0], recv.at[q], sources[q]
            ).wait_recv()

    for copy in swaps + unit_copies + sums:
        copy.wait()
    for copy in feats:
        copy.wait_send()
    for copy in keeps:
        copy.wait()
    for q in range(rows):

        @pl.when(jnp.logical_not(equal(targets[q], me)))
        def _():
            outgoing(q).wait_send()


def masked_scores(key, query, first):
    scores = product(key, query, TN) * HD ** (-0.5)
    keys = lax.broadcasted_iota(jnp.int32, scores.shape, 0)
    queries = lax.broadcasted_iota(jnp.int32, scores.shape, 1) + first
    return jnp.where(keys <= queries, scores, excluded)


def attend_kernel(qkv, out, logs):
    for first in range(0, L, QB):
        last = first + QB
        scores = masked_scores(qkv[HD : 2 * HD, :last], qkv[:HD, first:last], first)
        peak = jnp.max(scores, axis=0, keepdims=True)
        weights = jnp.exp(scores - peak)
        total = jnp.sum(weights, axis=0, keepdims=True)
        low = (weights * (1.0 / total)).astype(bf16)
        out[:, first:last] = product(qkv[2 * HD :, :last], low, NN).astype(bf16)
        logs[0, :, first:last] = peak + jnp.log(total)


def attend(qkv):
    slots = qkv.shape[0] // CHANNELS
    return pl.pallas_call(
        attend_kernel,
        grid=(slots,),
        out_shape=[
            jax.ShapeDtypeStruct((slots * HD, L), bf16),
            jax.ShapeDtypeStruct((slots, 1, L), f32),
        ],
        in_specs=[pl.BlockSpec((CHANNELS, L), lambda s: (s, 0))],
        out_specs=[
            pl.BlockSpec((HD, L), lambda s: (s, 0)),
            pl.BlockSpec((1, 1, L), lambda s: (s, 0, 0)),
        ],
        compiler_params=pltpu.CompilerParams(vmem_limit_bytes=LIMIT),
        cost_estimate=pl.CostEstimate(
            flops=slots * 4 * HD * L * L, bytes_accessed=4 * 2**20, transcendentals=slots * L * L
        ),
    )(qkv)


def attend_back(qkv, grad, logs, out, dkey, dval):
    query, key, value = qkv[:HD], qkv[HD : 2 * HD], qkv[2 * HD :]
    dkey[...] = jnp.zeros_like(dkey)
    dval[...] = jnp.zeros_like(dval)
    for first in range(0, L, QB):
        last = first + QB
        scores = masked_scores(key[:, :last], query[:, first:last], first)
        weights = jnp.exp(scores - logs[:, first:last])
        back = grad[:, first:last]
        dval[:, :last] += product(back, weights.astype(bf16), NT)
        grad_weights = product(value[:, :last], back, TN)
        inner = jnp.sum(weights * grad_weights, axis=0, keepdims=True)
        low = (weights * (grad_weights - inner)).astype(bf16)
        out(0, first, last, product(key[:, :last], low, NN) * HD ** (-0.5))
        dkey[:, :last] += product(query[:, first:last], low, NT)
    out(HD, 0, L, dkey[...] * HD ** (-0.5))
    out(2 * HD, 0, L, dval[...])


def middle_kernel(rows, cols, weight, att, own, vec, resid, full, normed, *scratch):
    p = Place(rows, cols)
    share = Share(p, *scratch[:6])
    width = own.shape[-1]
    gather = Spread(p, normed, full, width, *scratch[6:8])
    meet(p.col_peers())
    fill_partial(share.part, weight, att, cols, rows, width)
    share.start()
    share.middle()
    share.arrive()

    def first(d, total):
        value = own[d].astype(f32) + share.total(d) + vec[d, :, 2:3]
        resid[d] = value
        return total + jnp.sum(value, axis=0, keepdims=True)

    zero = jnp.zeros((1, width), f32)
    mean = lax.fori_loop(0, rows, first, zero) / D

    def second(d, total):
        value = resid[d] - mean
        return total + jnp.sum(value * value, axis=0, keepdims=True)

    scale = lax.rsqrt(lax.fori_loop(0, rows, second, zero) / D + epsilon)

    def third(d, carry):
        value = (resid[d] - mean) * scale
        normed[d] = (value * vec[d, :, 3:4] + vec[d, :, 4:5]).astype(bf16)
        return carry

    lax.fori_loop(0, rows, third, 0)
    gather.start()
    gather.forward()
    share.finish()
    gather.finish()


def norm_back(rows, width, incoming, values, gain, store, parts):
    zero = jnp.zeros((1, width), f32)

    def sums(d, total):
        return total + jnp.sum(values(d), axis=0, keepdims=True)

    mean = lax.fori_loop(0, rows, sums, zero) / D

    def squares(d, total):
        value = values(d) - mean
        return total + jnp.sum(value * value, axis=0, keepdims=True)

    scale = lax.rsqrt(lax.fori_loop(0, rows, squares, zero) / D + epsilon)

    def moments(d, totals):
        centred = (values(d) - mean) * scale
        back = incoming(d)
        parts(d, jnp.sum(back * centred, axis=1, keepdims=True), jnp.sum(back, axis=1, keepdims=True))
        scaled = back * gain(d)
        return (
            totals[0] + jnp.sum(scaled, axis=0, keepdims=True),
            totals[1] + jnp.sum(scaled * centred, axis=0, keepdims=True),
        )

    first, second = lax.fori_loop(0, rows, moments, (zero, zero))

    def last(d, carry):
        centred = (values(d) - mean) * scale
        scaled = incoming(d) * gain(d)
        store(d, scale * (scaled - first / D - centred * (second / D)))
        return carry

    lax.fori_loop(0, rows, last, 0)


def back_one_kernel(
    rows, cols, cot, cot_own, hidden, grad_pre, w_up, w_down, resid, vec,
    grad_down, grad_mid, branch, output, parts, branch_own, *scratch,
):
    p = Place(rows, cols)
    width = resid.shape[-1]
    share = Share(p, *scratch[:6])
    gather = Spread(p, branch_own, branch, width, *scratch[6:8])
    down = Reduce(p, cot, hidden, *scratch[8:11], scratch[11:15])
    share_out = Share(p, *scratch[15:21])
    meet(p.col_peers() + p.row_peers())
    fill_partial(share.part, w_up, grad_pre, cols, rows, width)
    share.start()
    down.send_pair()
    share.middle()
    fill_partial(share_out.part, w_down, hidden, cols, rows, width)
    share_out.start()
    share.arrive()

    def incoming(d):
        return share.total(d)

    def store(d, value):
        total = cot_own[d].astype(f32) + value
        grad_mid[d] = total
        low = total.astype(bf16)
        branch_own[d] = low
        parts[d, :, 2:3] = jnp.sum(low.astype(f32), axis=1, keepdims=True)
        parts[d, :, 3:4] = jnp.sum(cot_own[d].astype(f32), axis=1, keepdims=True)

    def put(d, gain, shift):
        parts[d, :, 0:1] = gain
        parts[d, :, 1:2] = shift

    norm_back(
        rows, width, incoming, lambda d: resid[d], lambda d: vec[d, :, 3:4], store, put
    )
    gather.start()
    share_out.middle()
    down.send_line()
    gather.forward()
    share_out.arrive()

    def result(d, carry):
        output[d] = (resid[d] + share_out.total(d) + vec[d, :, 5:6]).astype(bf16)
        return carry

    lax.fori_loop(0, rows, result, 0)
    down.finish(grad_down)
    share.finish()
    share_out.finish()
    gather.finish()


def back_two_kernel(
    rows, cols, normed_mid, grad_pre, branch, att, w_out, qkv, logs, normed_in, w_qkv,
    own, grad_mid, vec,
    grad_up, grad_out, grad_qkv_w, grad_tok, parts, grad_qkv, grad_att, dkey, dval, *scratch,
):
    p = Place(rows, cols)
    width = own.shape[-1]
    slots = logs.shape[0]
    share = Share(p, *scratch[:6])
    up = Reduce(p, normed_mid, grad_pre, *scratch[6:9], scratch[9:13])
    out = Reduce(p, branch, att, *scratch[13:16], scratch[16:20])
    wide = Reduce(p, normed_in, grad_qkv, *scratch[20:23], scratch[23:27])
    meet(p.col_peers() + p.row_peers())
    up.send_pair()
    for s in range(slots):
        total = product(w_out[0, :, s * HD : (s + 1) * HD], branch[0], TN)
        for d in range(1, rows):
            total = total + product(w_out[d, :, s * HD : (s + 1) * HD], branch[d], TN)
        grad_att[s * HD : (s + 1) * HD] = total.astype(bf16)
    out.send_pair()
    up.send_line()
    out.send_line()

    def head(s, carry):
        base = pl.multiple_of(s * CHANNELS, 64)

        def store(row, first, last, value):
            grad_qkv[pl.ds(base + row, HD), first:last] = value.astype(bf16)

        attend_back(
            qkv[pl.ds(base, CHANNELS)],
            grad_att[pl.ds(pl.multiple_of(s * HD, 64), HD)],
            logs[s],
            store,
            dkey,
            dval,
        )
        return carry

    lax.fori_loop(0, slots, head, 0)
    wide.send_pair()
    fill_partial(share.part, w_qkv, grad_qkv, cols, rows, width)
    share.start()
    wide.send_line()
    share.middle()
    up.finish(grad_up)
    out.finish(grad_out)
    share.arrive()

    def store_tokens(d, value):
        grad_tok[d] = (grad_mid[d] + value).astype(bf16)

    def put(d, gain, shift):
        parts[d, :, 0:1] = gain
        parts[d, :, 1:2] = shift

    norm_back(
        rows,
        width,
        lambda d: share.total(d),
        lambda d: own[d].astype(f32),
        lambda d: vec[d, :, 0:1],
        store_tokens,
        put,
    )
    wide.finish(grad_qkv_w)
    share.finish()


def call(kernel, outs, scratch, args, collective, spec=VMEM, out_specs=None):
    return pl.pallas_call(
        kernel,
        out_shape=[jax.ShapeDtypeStruct(s, t) for s, t in outs],
        in_specs=[spec] * len(args),
        out_specs=[spec] * len(outs) if out_specs is None else out_specs,
        scratch_shapes=scratch,
        compiler_params=pltpu.CompilerParams(
            collective_id=collective, has_side_effects=True, vmem_limit_bytes=LIMIT
        ),
    )(*args)


def one_hot(target, size):
    return (target[:, None] == jnp.arange(size, dtype=jnp.int32)[None, :]).astype(bf16)


def split_matrix(channels, slots, cols):
    source = jnp.arange(channels * H, dtype=jnp.int32)
    channel, head = source // H, source % H
    return one_hot(
        ((head % cols) * slots + head // cols) * channels + channel, cols * slots * channels
    )


def join_matrix(channels, slots, cols):
    source = jnp.arange(cols * slots * channels, dtype=jnp.int32)
    col, slot, channel = source // (slots * channels), source // channels % slots, source % channels
    return one_hot((slot * cols + col) * channels + channel, cols * slots * channels)


def to_owners(weight, matrix, cols):
    moved = product(weight, matrix, NN).astype(bf16)
    return moved.reshape(moved.shape[0], cols, -1).transpose(1, 0, 2)


def joined(blocks, matrix):
    flat = blocks.transpose(1, 0, 2).reshape(blocks.shape[1], -1)
    return product(flat, matrix, NN).astype(bf16)


def from_joined(gradient, matrix, cols):
    moved = product(gradient.astype(bf16), matrix, NT).astype(bf16)
    return moved.reshape(moved.shape[0], cols, -1).transpose(1, 0, 2)


def from_owners(blocks, matrix):
    flat = blocks.transpose(1, 0, 2).reshape(blocks.shape[1], -1)
    return product(flat, matrix, NT)


def whole_weight(weight):
    return lax.all_gather(weight, "row", axis=0, tiled=True)


def body(
    tokens, ln1_gain, ln1_shift, weight_qkv, bias_qkv, weight_out, bias_out, ln2_gain,
    ln2_shift, weight_up, bias_up, weight_down, bias_down, cotangent,
):
    rows, cols = lax.axis_size("row"), lax.axis_size("col")
    slots = (H + cols - 1) // cols
    ch, och = CHANNELS // cols, HD // cols
    feats = D // rows
    width = L // cols
    ffc = weight_up.shape[1]
    dma = pltpu.SemaphoreType.DMA

    qkv_split, out_split = split_matrix(ch, slots, cols), split_matrix(och, slots, cols)
    qkv_join, out_join = join_matrix(ch, slots, cols), join_matrix(och, slots, cols)
    wq = to_owners(weight_qkv, qkv_split, cols)
    wo = to_owners(weight_out, out_split, cols)
    bias = jnp.pad(bias_qkv.reshape(ch, H), ((0, 0), (0, slots * cols - H)))
    bias = bias.reshape(ch, slots, cols).transpose(2, 1, 0)
    zero = jnp.zeros_like(ln1_gain)
    vec = jnp.stack(
        [ln1_gain, ln1_shift, bias_out, ln2_gain, ln2_shift, bias_down, zero, zero]
    )
    both, own, wq, wo, bias, vec = call(
        functools.partial(enter_kernel, rows, cols),
        [
            ((2, rows, feats, L), bf16),
            ((2, rows, feats, width), bf16),
            (wq.shape, bf16),
            (wo.shape, bf16),
            (bias.shape, f32),
            ((rows,) + vec.shape, f32),
        ],
        [dma((rows,)), dma((rows,)), dma((5,)), dma((3, cols)), dma((3, cols))]
        + spread_sems(cols)
        + [dma((rows,)), dma((rows,))],
        (jnp.stack([tokens, cotangent]), wq, wo, bias, vec),
        1,
        ANY,
    )
    vec = vec.transpose(0, 2, 1)
    w_up = whole_weight(weight_up)
    w_qkv = whole_weight(joined(wq, qkv_join))
    w_out = whole_weight(joined(wo, out_join))
    w_down = whole_weight(weight_down)
    qkv_bias = bias.transpose(1, 0, 2).reshape(slots * CHANNELS, 1)

    chunked = lambda array: array.reshape(rows, feats, array.shape[-1])
    flat = lambda array: array.reshape(D, array.shape[-1])

    values = flat(both[0]).astype(f32)
    mean = jnp.mean(values, axis=0, keepdims=True)
    centred = values - mean
    scale = lax.rsqrt(jnp.mean(centred * centred, axis=0, keepdims=True) + epsilon)
    normed_in = (
        centred * scale * flat(vec[:, :, 0:1]) + flat(vec[:, :, 1:2])
    ).astype(bf16)
    qkv = (product(w_qkv, normed_in, TN) + qkv_bias).astype(bf16)
    att, logs = attend(qkv)

    resid, normed_mid = call(
        functools.partial(middle_kernel, rows, cols),
        [((rows, feats, width), f32), ((rows, feats, L), bf16)],
        [pltpu.VMEM((rows, feats, width), bf16)]
        + share_scratch(rows, cols, feats, width)
        + spread_sems(cols),
        (chunked(w_out), att, own[0], vec),
        2,
    )
    hidden_pre = product(w_up, flat(normed_mid), TN) + bias_up[:, None]
    hidden = jax.nn.gelu(hidden_pre, approximate=True).astype(bf16)
    grad_hidden = product(w_down, flat(both[1]), TN)
    gelu_back = jax.vjp(lambda inner: jax.nn.gelu(inner, approximate=True), hidden_pre)[1]
    grad_pre = gelu_back(grad_hidden)[0].astype(bf16)
    up_part = jnp.sum(grad_pre, axis=1, dtype=f32)

    grad_weight_down, grad_mid, branch, output, parts_two = call(
        functools.partial(back_one_kernel, rows, cols),
        [
            ((feats, ffc), f32),
            ((rows, feats, width), f32),
            ((rows, feats, L), bf16),
            ((rows, feats, width), bf16),
            ((rows, feats, 4), f32),
        ],
        [pltpu.VMEM((rows, feats, width), bf16)]
        + share_scratch(rows, cols, feats, width)
        + spread_sems(cols)
        + reduce_scratch(rows, feats, ffc)
        + share_scratch(rows, cols, feats, width),
        (both[1], own[1], hidden, grad_pre, chunked(w_up), chunked(w_down), resid, vec),
        3,
    )
    grad_weight_up, grad_out, grad_qkv_w, grad_tok, parts_one, grad_qkv = call(
        functools.partial(back_two_kernel, rows, cols),
        [
            ((feats, ffc), f32),
            ((feats, slots * HD), f32),
            ((feats, slots * CHANNELS), f32),
            ((rows, feats, width), bf16),
            ((rows, feats, 2), f32),
            ((slots * CHANNELS, L), bf16),
        ],
        [
            pltpu.VMEM((slots * HD, L), bf16),
            pltpu.VMEM((HD, L), f32),
            pltpu.VMEM((HD, L), f32),
        ]
        + share_scratch(rows, cols, feats, width)
        + reduce_scratch(rows, feats, ffc)
        + reduce_scratch(rows, feats, slots * HD)
        + reduce_scratch(rows, feats, slots * CHANNELS),
        (
            normed_mid, grad_pre, branch, att, chunked(w_out), qkv, logs,
            chunked(normed_in), chunked(w_qkv), own[0], grad_mid, vec,
        ),
        4,
    )
    qkv_part = jnp.sum(grad_qkv, axis=1, dtype=f32)

    feat = jnp.concatenate([parts_one, parts_two, jnp.zeros((rows, feats, 2), f32)], axis=2)
    feat = feat.transpose(0, 2, 1)
    units = jnp.concatenate([up_part, qkv_part])[None, :]
    gq = from_joined(grad_qkv_w, qkv_join, cols)
    go = from_joined(grad_out, out_join, cols)
    res, gq, go, feat, units = call(
        functools.partial(leave_kernel, rows, cols),
        [
            ((2, feats, rows * width), bf16),
            (gq.shape, bf16),
            (go.shape, bf16),
            ((cols,) + feat.shape[1:], f32),
            ((rows,) + units.shape, f32),
        ],
        [
            pltpu.VMEM(feat.shape, f32),
            pltpu.VMEM(feat.shape[1:], f32),
            dma((rows,)), dma((rows,)), dma((4,)), dma((3, cols)), dma((3, cols)),
            dma((rows,)), dma((rows,)), dma((rows,)), dma((rows,)),
        ],
        (jnp.stack([output, grad_tok]), gq, go, feat, units),
        5,
    )
    feat = jnp.sum(feat, axis=0)
    units = jnp.sum(units, axis=0)[0]
    grad_weight_qkv = from_owners(gq, qkv_split)
    grad_weight_out = from_owners(go, out_split)
    grads = lax.all_gather(units[ffc:].reshape(slots, cols, ch), "col", axis=0)
    mine = lax.dynamic_index_in_dim(grads, lax.axis_index("col"), axis=2, keepdims=False)
    grad_bias_qkv = mine.transpose(2, 1, 0).reshape(ch, slots * cols)[:, :H].reshape(-1)
    return (
        res[0],
        res[1].astype(f32),
        feat[0],
        feat[1],
        grad_weight_qkv,
        grad_bias_qkv,
        grad_weight_out,
        feat[4],
        feat[2],
        feat[3],
        grad_weight_up,
        units[:ffc],
        grad_weight_down,
        feat[5],
    )


def solution(mesh):
    both, row, col = P("row", "col"), P("row"), P("col")
    in_specs = (both, row, row, both, col, both, row, row, row, both, col, both, row, both)
    out_specs = (both, both, row, row, both, col, both, row, row, row, both, col, both, row)
    return jax.shard_map(body, mesh=mesh, in_specs=in_specs, out_specs=out_specs, check_vma=False)
```

```python
import functools

import jax
import jax.numpy as jnp
from jax import lax
from jax.experimental import pallas as pl
from jax.experimental.pallas import tpu as pltpu
from jax.sharding import PartitionSpec as P

D = 1600
H = 25
HD = 64
L = 1024
CHANNELS = 3 * HD
QB = 256

epsilon = 1e-05
excluded = -1e30

TN = (((0,), (0,)), ((), ()))
NN = (((1,), (0,)), ((), ()))
NT = (((1,), (1,)), ((), ()))
MESH = pl.DeviceIdType.MESH
ANY = pl.BlockSpec(memory_space=pl.ANY)
VMEM = pl.BlockSpec(memory_space=pltpu.VMEM)
LIMIT = 62 * 2**20
f32 = jnp.float32
bf16 = jnp.bfloat16


def product(left, right, dims):
    return lax.dot_general(left, right, dims, preferred_element_type=f32)


def remote(src, dst, send, recv, device):
    return pltpu.make_async_remote_copy(
        src_ref=src,
        dst_ref=dst,
        send_sem=send,
        recv_sem=recv,
        device_id=device,
        device_id_type=MESH,
    )


def meet(devices):
    sem = pltpu.get_barrier_semaphore()
    for device in devices:
        pl.semaphore_signal(sem, inc=1, device_id=device, device_id_type=MESH)
    pl.semaphore_wait(sem, len(devices))


def lanes(index, width):
    return pl.ds(pl.multiple_of(index * width, 128), width)


class Place:
    def __init__(self, rows, cols):
        self.R, self.C, self.A, self.X = rows, cols, rows // 2, cols // 2
        self.r, self.c = lax.axis_index("row"), lax.axis_index("col")
        self.a, self.b = self.r // 2, lax.rem(self.r, 2)
        self.x, self.k = self.c // 2, lax.rem(self.c, 2)
        self.core = (self.r, self.x * 2 + 1 - self.k)
        self.pair = (self.a * 2 + 1 - self.b, self.c)
        self.pos = jnp.where(self.b == 0, self.a, rows - 1 - self.a)
        self.around = [(self.row_at(1), self.c), (self.row_at(-1), self.c)]

    def row_at(self, o):
        at = lax.rem(self.pos + o + self.R, self.R)
        return jnp.where(at < self.A, at * 2, (self.R - 1 - at) * 2 + 1)

    def ahead(self, o):
        return lax.rem(self.a + o, self.A)

    def behind(self, o):
        return lax.rem(self.a - o + self.A, self.A)

    def line(self, o):
        return (self.ahead(o) * 2 + self.b, self.c)

    def x_ahead(self, o):
        return lax.rem(self.x + o, self.X)

    def x_behind(self, o):
        return lax.rem(self.x - o + self.X, self.X)

    def side(self, o):
        return (self.r, self.x_ahead(o) * 2 + self.k)

    def col_peers(self):
        return [self.core] + [self.side(o) for o in range(1, self.X)]

    def row_peers(self):
        return [self.pair] + [self.line(o) for o in range(1, self.A)]


class Spread:
    def __init__(self, p, own, full, width, send, recv):
        self.p, self.own, self.full, self.width = p, own, full, width
        self.send, self.recv = send, recv

    def part(self, block):
        return self.full.at[..., lanes(block, self.width)]

    def side_copy(self, o):
        return remote(
            self.own, self.part(self.p.c), self.send.at[o], self.recv.at[o], self.p.side(o)
        )

    def core_copy(self, o):
        p = self.p
        block = p.c if o == 0 else p.x_behind(o) * 2 + p.k
        src = self.own if o == 0 else self.part(block)
        i = p.X + o
        return remote(src, self.part(block), self.send.at[i], self.recv.at[i], p.core)

    def local(self):
        i = 2 * self.p.X
        return pltpu.make_async_copy(self.own, self.part(self.p.c), self.send.at[i])

    def start(self):
        for o in range(1, self.p.X):
            self.side_copy(o).start()
        self.core_copy(0).start()
        self.local().start()

    def forward(self):
        for o in range(1, self.p.X):
            self.side_copy(o).wait_recv()
            self.core_copy(o).start()

    def finish(self):
        for o in range(self.p.X):
            self.core_copy(o).wait()
        for o in range(1, self.p.X):
            self.side_copy(o).wait_send()
        self.local().wait()


def spread_sems(cols):
    return [pltpu.SemaphoreType.DMA((cols + 1,)), pltpu.SemaphoreType.DMA((cols + 1,))]


class Share:
    def __init__(self, p, part, core_in, side_out, side_in, send, recv):
        self.p, self.part, self.core_in = p, part, core_in
        self.side_out, self.side_in, self.send, self.recv = side_out, side_in, send, recv

    def core_copy(self, x):
        p = self.p
        return remote(
            self.part.at[x * 2 + 1 - p.k],
            self.core_in.at[x],
            self.send.at[x],
            self.recv.at[x],
            p.core,
        )

    def side_copy(self, o):
        p = self.p
        i = p.X + o - 1
        return remote(
            self.side_out.at[o - 1],
            self.side_in.at[o - 1],
            self.send.at[i],
            self.recv.at[i],
            p.side(o),
        )

    def start(self):
        for x in range(self.p.X):
            self.core_copy(x).start()

    def middle(self):
        p = self.p
        for x in range(p.X):
            self.core_copy(x).wait_recv()
        for o in range(1, p.X):
            x = p.x_ahead(o)

            def add(d, carry, x=x, o=o):
                total = self.part[x * 2 + p.k, d].astype(f32) + self.core_in[x, d].astype(f32)
                self.side_out[o - 1, d] = total.astype(bf16)
                return carry

            lax.fori_loop(0, p.R, add, 0)
            self.side_copy(o).start()

    def arrive(self):
        for o in range(1, self.p.X):
            self.side_copy(o).wait_recv()

    def total(self, d):
        p = self.p
        result = self.part[p.c, d].astype(f32) + self.core_in[p.x, d].astype(f32)
        for o in range(1, p.X):
            result = result + self.side_in[o - 1, d].astype(f32)
        return result

    def finish(self):
        for x in range(self.p.X):
            self.core_copy(x).wait_send()
        for o in range(1, self.p.X):
            self.side_copy(o).wait_send()


def share_scratch(rows, cols, feats, width):
    half = cols // 2
    return [
        pltpu.VMEM((cols, rows, feats, width), bf16),
        pltpu.VMEM((half, rows, feats, width), bf16),
        pltpu.VMEM((half - 1, rows, feats, width), bf16),
        pltpu.VMEM((half - 1, rows, feats, width), bf16),
        pltpu.SemaphoreType.DMA((cols - 1,)),
        pltpu.SemaphoreType.DMA((cols - 1,)),
    ]


def fill_partial(part, weight, act, cols, rows, width):
    def one(d, carry):
        for j in range(cols):
            part[j, d] = product(
                weight[d], act[:, j * width : (j + 1) * width], NN
            ).astype(bf16)
        return carry

    lax.fori_loop(0, rows, one, 0)


def middle(size, extra):
    return min((size // 256 + extra) * 128, (size - 1) // 128 * 128)


class Reduce:
    def __init__(self, p, left, right, scratch, cut):
        self.p, self.left, self.right = p, left, right
        self.slots, self.send, self.recv = scratch
        self.parts = (slice(0, cut), slice(cut, self.slots.shape[-1]))

    def copy(self, way, t):
        part = self.parts[way]
        i = way * self.p.R + t
        return remote(
            self.slots.at[t, :, part],
            self.slots.at[t + 1, :, part],
            self.send.at[i],
            self.recv.at[i],
            self.p.around[way],
        )

    def step(self, t):
        p = self.p
        for way in range(2):
            part = self.parts[way]
            row = p.row_at(-1 - t if way == 0 else 1 + t)
            value = product(self.left[row], self.right[part], NT)
            if t > 0:
                self.copy(way, t - 1).wait_recv()
                value = value + self.slots[t, :, part].astype(f32)
            if t < p.R - 1:
                self.slots[t, :, part] = value.astype(bf16)
                self.copy(way, t).start()
            else:
                self.out[:, part] = value.astype(self.out.dtype)

    def into(self, out):
        self.out = out
        return self

    def finish(self):
        for way in range(2):
            for t in range(self.p.R - 1):
                self.copy(way, t).wait_send()


def reduce_scratch(rows, feats, size):
    return [
        pltpu.VMEM((rows, feats, size), bf16),
        pltpu.SemaphoreType.DMA((2 * rows,)),
        pltpu.SemaphoreType.DMA((2 * rows,)),
    ]


def steps(rows, *rings):
    return [(ring, t) for t in range(rows) for ring in rings]


def serve(queue, t):
    while queue and queue[0][1] <= t:
        ring, at = queue.pop(0)
        ring.step(at)


def home(p, q):
    block = p.c * p.R + q
    return (block // p.C, lax.rem(block, p.C))


def own_block(p):
    block = p.r * p.C + p.c
    return block // p.R, lax.rem(block, p.R)


def equal(left, right):
    return jnp.logical_and(left[0] == right[0], left[1] == right[1])


def exchange_copies(p, src, dst, send, recv):
    out = []
    for o in range(1, p.C):
        to = lax.rem(p.c + o, p.C)
        out.append(remote(src.at[to], dst.at[p.c], send.at[o], recv.at[o], (p.r, to)))
    return out


def all_col(p):
    return [(p.r, lax.rem(p.c + o, p.C)) for o in range(1, p.C)]


def all_row(p):
    return [(lax.rem(p.r + o, p.R), p.c) for o in range(1, p.R)]


class Back:
    def __init__(self, p, src, dst, sems):
        self.p, self.src, self.dst = p, src, dst
        self.send, self.recv = sems
        self.width = src.shape[-1]
        self.col, self.place = own_block(p)

    def slot(self, q):
        return self.dst.at[:, lanes(q, self.width)]

    def outgoing(self, q):
        return remote(
            self.src.at[q],
            self.slot(self.place),
            self.send.at[q],
            self.recv.at[self.place],
            (q, self.col),
        )

    def staying(self, q):
        return pltpu.make_async_copy(
            self.src.at[q], self.slot(self.place), self.send.at[self.p.R]
        )

    def start(self):
        p = self.p
        for q in range(p.R):
            here = equal((q, self.col), (p.r, p.c))

            @pl.when(here)
            def _():
                self.staying(q).start()

            @pl.when(jnp.logical_not(here))
            def _():
                self.outgoing(q).start()

    def finish(self):
        p = self.p
        for q in range(p.R):
            source = home(p, q)
            here = equal(source, (p.r, p.c))

            @pl.when(here)
            def _():
                self.staying(0).wait()

            @pl.when(jnp.logical_not(here))
            def _():
                remote(
                    self.src.at[0], self.slot(q), self.send.at[0], self.recv.at[q], source
                ).wait_recv()

        for q in range(p.R):

            @pl.when(jnp.logical_not(equal((q, self.col), (p.r, p.c))))
            def _():
                self.outgoing(q).wait_send()


def masked_scores(key, query, first):
    scores = product(key, query, TN) * HD ** (-0.5)
    keys = lax.broadcasted_iota(jnp.int32, scores.shape, 0)
    queries = lax.broadcasted_iota(jnp.int32, scores.shape, 1) + first
    return jnp.where(keys <= queries, scores, excluded)


def attend_back(qkv, grad, logs, out, dkey, dval):
    query, key, value = qkv[:HD], qkv[HD : 2 * HD], qkv[2 * HD :]
    dkey[...] = jnp.zeros_like(dkey)
    dval[...] = jnp.zeros_like(dval)
    for first in range(0, L, QB):
        last = first + QB
        scores = masked_scores(key[:, :last], query[:, first:last], first)
        weights = jnp.exp(scores - logs[:, first:last])
        back = grad[:, first:last]
        dval[:, :last] += product(back, weights.astype(bf16), NT)
        grad_weights = product(value[:, :last], back, TN)
        inner = jnp.sum(weights * grad_weights, axis=0, keepdims=True)
        low = (weights * (grad_weights - inner)).astype(bf16)
        out(0, first, last, product(key[:, :last], low, NN) * HD ** (-0.5))
        dkey[:, :last] += product(query[:, first:last], low, NT)
    out(HD, 0, L, dkey[...] * HD ** (-0.5))
    out(2 * HD, 0, L, dval[...])


def norm_back(rows, width, incoming, values, gain, store, parts):
    zero = jnp.zeros((1, width), f32)

    def sums(d, total):
        return total + jnp.sum(values(d), axis=0, keepdims=True)

    mean = lax.fori_loop(0, rows, sums, zero) / D

    def squares(d, total):
        value = values(d) - mean
        return total + jnp.sum(value * value, axis=0, keepdims=True)

    scale = lax.rsqrt(lax.fori_loop(0, rows, squares, zero) / D + epsilon)

    def moments(d, totals):
        centred = (values(d) - mean) * scale
        back = incoming(d)
        parts(d, jnp.sum(back * centred, axis=1, keepdims=True), jnp.sum(back, axis=1, keepdims=True))
        scaled = back * gain(d)
        return (
            totals[0] + jnp.sum(scaled, axis=0, keepdims=True),
            totals[1] + jnp.sum(scaled * centred, axis=0, keepdims=True),
        )

    first, second = lax.fori_loop(0, rows, moments, (zero, zero))

    def last(d, carry):
        centred = (values(d) - mean) * scale
        scaled = incoming(d) * gain(d)
        store(d, scale * (scaled - first / D - centred * (second / D)))
        return carry

    lax.fori_loop(0, rows, last, 0)


class Ring:
    def __init__(self, p, own, full, sems, cut):
        self.p, self.own, self.full = p, own, full
        self.send, self.recv = sems
        self.parts = (slice(0, cut), slice(cut, own.shape[1]))

    def copy(self, way, t):
        p = self.p
        row = p.row_at(-t if way == 0 else t)
        part = self.parts[way]
        i = way * p.R + t
        return remote(
            self.own.at[:, part] if t == 0 else self.full.at[row, :, part],
            self.full.at[row, :, part],
            self.send.at[i],
            self.recv.at[i],
            p.around[way],
        )

    def local(self):
        return pltpu.make_async_copy(
            self.own, self.full.at[self.p.r], self.send.at[self.p.R - 1]
        )

    def step(self, t):
        if t == 0:
            self.local().start()
        for way in range(2):
            if t > 0:
                self.copy(way, t - 1).wait_recv()
            if t < self.p.R - 1:
                self.copy(way, t).start()
        if t == self.p.R - 1:
            self.local().wait()

    def finish(self):
        for way in range(2):
            for t in range(self.p.R - 1):
                self.copy(way, t).wait_send()


class Redistribute:
    def __init__(self, p, src, own, sems):
        self.p, self.src, self.own = p, src, own
        self.send, self.recv = sems
        self.width = own.shape[-1]
        self.col, _ = own_block(p)

    def outgoing(self, q, target):
        return remote(
            self.src.at[:, q * self.width : (q + 1) * self.width],
            self.own.at[self.p.r],
            self.send.at[q],
            self.recv.at[self.p.r],
            target,
        )

    def staying(self, q):
        return pltpu.make_async_copy(
            self.src.at[:, q * self.width : (q + 1) * self.width],
            self.own.at[self.p.r],
            self.send.at[self.p.R],
        )

    def start(self):
        p = self.p
        for q in range(p.R):
            target = home(p, q)
            here = equal(target, (p.r, p.c))

            @pl.when(here)
            def _():
                self.staying(q).start()

            @pl.when(jnp.logical_not(here))
            def _():
                self.outgoing(q, target).start()

    def arrive(self):
        p = self.p
        for q in range(p.R):
            here = equal((q, self.col), (p.r, p.c))

            @pl.when(here)
            def _():
                self.staying(0).wait()

            @pl.when(jnp.logical_not(here))
            def _():
                remote(
                    self.src.at[:, 0 : self.width],
                    self.own.at[q],
                    self.send.at[0],
                    self.recv.at[q],
                    (q, self.col),
                ).wait_recv()

    def finish(self):
        p = self.p
        for q in range(p.R):
            target = home(p, q)

            @pl.when(jnp.logical_not(equal(target, (p.r, p.c))))
            def _():
                self.outgoing(q, target).wait_send()


def norm_scale(rows, width, values):
    zero = jnp.zeros((1, width), f32)

    def sums(d, total):
        return total + jnp.sum(values(d), axis=0, keepdims=True)

    mean = lax.fori_loop(0, rows, sums, zero) / D

    def squares(d, total):
        value = values(d) - mean
        return total + jnp.sum(value * value, axis=0, keepdims=True)

    return mean, lax.rsqrt(lax.fori_loop(0, rows, squares, zero) / D + epsilon)


def tiled(size, tile, one):
    count = size // tile

    def step(i, carry):
        one(pl.multiple_of(i * tile, tile), tile)
        return carry

    lax.fori_loop(0, count, step, 0)
    if size % tile:
        one(count * tile, size % tile)


def summed(weight, act, rows, first, size):
    total = product(weight[0, :, pl.ds(first, size)], act[0], TN)
    for d in range(1, rows):
        total = total + product(weight[d, :, pl.ds(first, size)], act[d], TN)
    return total


def forward_kernel(
    rows, cols,
    tok, cot, wq, wo, bias, vec, wu, wd, bias_up,
    wq_f, wo_f, wu_f, wd_f, n1_f, qkv_f, att_f, logs_f, resid_f, n2_f, hidden_f, gp_f,
    cot_f, tok_own_f, cot_own_f, vec_f,
    qfull, ofull, ufull, dfull, qown, oown, qin, oin, bin_, qbias, vin, vecs,
    xfull, n1, qkv, att, logs, resid, normed, n2, hidden, gp, cfull, tok_own, cot_own,
    part, core_in, side_out, side_in, share_s, share_r,
    qs, qr, os_, or_, us, ur, ds0, dr0, ts, tr, cs, cr,
    xs, xr, ys, yr, ns, nr, es, er, vs, vr, loc,
):
    p = Place(rows, cols)
    width = tok_own.shape[-1]
    slots = logs.shape[0]
    ch = CHANNELS // cols
    ffc = hidden.shape[0]
    red_tok = Redistribute(p, tok, tok_own, (ts, tr))
    red_cot = Redistribute(p, cot, cot_own, (cs, cr))
    sources = [(q, red_tok.col) for q in range(rows)]
    targets = [home(p, q) for q in range(rows)]
    meet(sources + targets + all_col(p) + all_row(p))

    groups = ((wq, qin), (wo, oin), (bias, bin_))
    swaps = []
    for i, (src, dst) in enumerate(groups):
        swaps.append(exchange_copies(p, src, dst, es.at[i], er.at[i]))
    for copies in swaps:
        for copy in copies:
            copy.start()
    keeps = [
        pltpu.make_async_copy(src.at[p.c], dst.at[p.c], loc.at[i])
        for i, (src, dst) in enumerate(groups)
    ]
    keeps.append(pltpu.make_async_copy(vec, vin.at[p.r], loc.at[3]))
    for copy in keeps:
        copy.start()
    red_tok.start()
    vec_copies = [
        remote(vec, vin.at[p.r], vs.at[o], vr.at[o], peer)
        for o, peer in enumerate(all_row(p))
    ]
    for copy in vec_copies:
        copy.start()

    for copies, keep in zip(swaps, keeps):
        for copy in copies:
            copy.wait_recv()
        keep.wait()
    och = HD // cols
    for j in range(cols):
        for s in range(slots):
            base = s * CHANNELS + j * ch
            qown[:, base : base + ch] = qin[j, :, s * ch : (s + 1) * ch]
            qbias[:, base : base + ch] = bin_[j, :, s * ch : (s + 1) * ch]
            base = s * HD + j * och
            oown[:, base : base + och] = oin[j, :, s * och : (s + 1) * och]
    ring_q = Ring(p, qown, qfull, (qs, qr), middle(slots * CHANNELS, 0))
    ring_o = Ring(p, oown, ofull, (os_, or_), middle(slots * HD, 1))
    ring_u = Ring(p, wu, ufull, (us, ur), middle(ffc, 0))
    ring_d = Ring(p, wd, dfull, (ds0, dr0), middle(ffc, 1))
    early = steps(rows, ring_q, ring_o)
    late = steps(rows, ring_u, ring_d)
    serve(early, 0)
    red_tok.arrive()
    spread_x = Spread(p, tok_own, xfull, width, xs, xr)
    spread_x.start()
    serve(early, rows * 1 // 8)
    for copy in vec_copies:
        copy.wait_recv()
    keeps[3].wait()
    eye = (
        lax.broadcasted_iota(jnp.int32, (8, 8), 0) == lax.broadcasted_iota(jnp.int32, (8, 8), 1)
    ).astype(f32)
    for d in range(rows):
        vecs[d] = lax.dot_general(
            vin[d], eye, TN, precision=lax.Precision.HIGHEST, preferred_element_type=f32
        )
    spread_x.forward()
    serve(early, rows * 2 // 8)
    spread_x.finish()
    outs = []

    def keep_out(src, dst):
        copy = pltpu.make_async_copy(src, dst, loc.at[4 + len(outs)])
        copy.start()
        outs.append(copy)

    keep_out(tok_own, tok_own_f)
    keep_out(vecs, vec_f)
    mean, scale = norm_scale(rows, L, lambda d: xfull[d].astype(f32))
    serve(early, rows * 3 // 8)

    def normal(d, carry):
        value = (xfull[d].astype(f32) - mean) * scale
        n1[d] = (value * vecs[d, :, 0:1] + vecs[d, :, 1:2]).astype(bf16)
        return carry

    lax.fori_loop(0, rows, normal, 0)
    keep_out(n1, n1_f)

    serve(early, rows - 2)
    serve(late, 0)
    red_cot.start()
    serve(early, rows)
    keep_out(qfull, wq_f)
    keep_out(ofull, wo_f)
    ones = jnp.ones((8, L), bf16)

    def project(first, size):
        total = product(qbias[:, pl.ds(first, size)], ones, TN)
        total = total + summed(qfull, n1, rows, first, size)
        qkv[pl.ds(first, size)] = total.astype(bf16)

    tiled(slots * CHANNELS, 384, project)
    keep_out(qkv, qkv_f)

    def head(s, carry):
        base = s * CHANNELS
        rows_of = lambda part: pl.ds(pl.multiple_of(base + part * HD, HD), HD)
        query, key, value = qkv[rows_of(0)], qkv[rows_of(1)], qkv[rows_of(2)]
        for first in range(0, L, QB):
            last = first + QB
            scores = masked_scores(key[:, :last], query[:, first:last], first)
            peak = jnp.max(scores, axis=0, keepdims=True)
            weights = jnp.exp(scores - peak)
            total = jnp.sum(weights, axis=0, keepdims=True)
            low = (weights * (1.0 / total)).astype(bf16)
            att[pl.ds(pl.multiple_of(s * HD, HD), HD), first:last] = product(
                value[:, :last], low, NN
            ).astype(bf16)
            logs[s, :, first:last] = peak + jnp.log(total)
        return carry

    half = slots * 5 // 7
    lax.fori_loop(0, half, head, 0)
    serve(late, rows * 1 // 8)
    lax.fori_loop(half, slots, head, 0)
    keep_out(att, att_f)
    keep_out(logs, logs_f)

    share = Share(p, part, core_in, side_out, side_in, share_s, share_r)
    fill_partial(part, ofull, att, cols, rows, width)
    share.start()
    share.middle()
    serve(late, rows * 2 // 8)
    share.arrive()

    def first_pass(d, total):
        value = tok_own[d].astype(f32) + share.total(d) + vecs[d, :, 2:3]
        resid[d] = value
        return total

    lax.fori_loop(0, rows, first_pass, 0)
    keep_out(resid, resid_f)
    mean, scale = norm_scale(rows, width, lambda d: resid[d])

    def third(d, carry):
        value = (resid[d] - mean) * scale
        normed[d] = (value * vecs[d, :, 3:4] + vecs[d, :, 4:5]).astype(bf16)
        return carry

    lax.fori_loop(0, rows, third, 0)
    spread_n = Spread(p, normed, n2, width, ns, nr)
    spread_n.start()
    serve(late, rows * 3 // 8)
    red_cot.arrive()
    spread_n.forward()
    spread_c = Spread(p, cot_own, cfull, width, ys, yr)
    spread_c.start()
    serve(late, rows * 4 // 8)
    spread_n.finish()
    keep_out(n2, n2_f)
    keep_out(cot_own, cot_own_f)
    serve(late, rows * 5 // 8)
    spread_c.forward()
    serve(late, rows * 6 // 8)
    spread_c.finish()
    keep_out(cfull, cot_f)
    serve(late, rows)
    keep_out(ufull, wu_f)

    def up(first, size):
        value = summed(ufull, n2, rows, first, size) + bias_up[pl.ds(first, size)]
        cube = 0.7978845608 * (value + 0.044715 * value * value * value)
        bend = jnp.tanh(cube)
        hidden[pl.ds(first, size)] = (0.5 * value * (1.0 + bend)).astype(bf16)
        slope = 0.7978845608 * (1.0 + 3.0 * 0.044715 * value * value)
        gp[pl.ds(first, size)] = (
            0.5 * (1.0 + bend) + 0.5 * value * (1.0 - bend * bend) * slope
        ).astype(bf16)

    tiled(ffc, 256, up)
    keep_out(hidden, hidden_f)

    def down(first, size):
        value = summed(dfull, cfull, rows, first, size)
        value = (value * gp[pl.ds(first, size)].astype(f32)).astype(bf16)
        gp[pl.ds(first, size)] = value

    tiled(ffc, 256, down)
    keep_out(gp, gp_f)
    keep_out(dfull, wd_f)
    for copies in swaps:
        for copy in copies:
            copy.wait_send()
    for copy in vec_copies:
        copy.wait_send()
    for ring in (ring_q, ring_o, ring_u, ring_d):
        ring.finish()
    red_tok.finish()
    red_cot.finish()
    share.finish()
    for copy in outs:
        copy.wait()


def forward(rows, cols, args, shapes):
    feats, width, slots, ffc = shapes
    dma = pltpu.SemaphoreType.DMA
    big = lambda n, t=bf16: pltpu.VMEM((rows, feats, n), t)
    qn, on = slots * CHANNELS, slots * HD
    ch, och = CHANNELS // cols, HD // cols
    outs = [
        ((rows, feats, qn), bf16),
        ((rows, feats, on), bf16),
        ((rows, feats, ffc), bf16),
        ((rows, feats, ffc), bf16),
        ((rows, feats, L), bf16),
        ((qn, L), bf16),
        ((on, L), bf16),
        ((slots, 1, L), f32),
        ((rows, feats, width), f32),
        ((rows, feats, L), bf16),
        ((ffc, L), bf16),
        ((ffc, L), bf16),
        ((rows, feats, L), bf16),
        ((rows, feats, width), bf16),
        ((rows, feats, width), bf16),
        ((rows, feats, 8), f32),
    ]
    scratch = [
        big(qn), big(on), big(ffc), big(ffc),
        pltpu.VMEM((feats, qn), bf16), pltpu.VMEM((feats, on), bf16),
        pltpu.VMEM((cols, feats, slots * ch), bf16),
        pltpu.VMEM((cols, feats, slots * och), bf16),
        pltpu.VMEM((cols, 8, slots * ch), bf16),
        pltpu.VMEM((8, qn), bf16),
        pltpu.VMEM((rows, 8, feats), f32),
        big(8, f32),
        big(L), big(L),
        pltpu.VMEM((qn, L), bf16), pltpu.VMEM((on, L), bf16), pltpu.VMEM((slots, 1, L), f32),
        big(width, f32), big(width), big(L),
        pltpu.VMEM((ffc, L), bf16), pltpu.VMEM((ffc, L), bf16),
        big(L), big(width), big(width),
    ]
    scratch += share_scratch(rows, cols, feats, width)
    scratch += [dma((2 * rows,))] * 8
    scratch += [dma((rows + 1,)), dma((rows,))] * 2
    scratch += spread_sems(cols) * 3
    scratch += [dma((3, cols)), dma((3, cols)), dma((rows,)), dma((rows,)), dma((24,))]
    return call(
        functools.partial(forward_kernel, rows, cols),
        outs,
        scratch,
        args,
        1,
        ANY,
        in_specs=[ANY] * 8 + [VMEM],
        out_specs=[ANY] * 16,
    )


def back_one_kernel(
    rows, cols, ready, w_up, grad_pre, cot, hidden, cot_own, resid, vec, w_down, normed_mid,
    grad_down, grad_up, grad_mid, branch, part_out, parts, branch_own, *scratch,
):
    p = Place(rows, cols)
    width = resid.shape[-1]
    half = grad_up.shape[1]
    share = Share(p, *scratch[:6])
    gather = Spread(p, branch_own, branch, width, *scratch[6:8])
    down = Reduce(p, cot, hidden, scratch[8:11], middle(hidden.shape[0], 0)).into(grad_down)
    up = Reduce(
        p, normed_mid, grad_pre.at[pl.ds(0, half)], scratch[11:14], middle(half, 0)
    ).into(grad_up)
    queue = steps(rows, down, up)
    at = lambda t: rows * t // 8
    meet(p.col_peers() + p.row_peers())
    ready("w_up", "grad_pre")
    fill_partial(share.part, w_up, grad_pre, cols, rows, width)
    share.start()
    ready("cot", "hidden", "normed_mid")
    serve(queue, 0)
    share.middle()
    serve(queue, at(1))
    ready("cot_own", "resid", "vec", "w_down")
    serve(queue, at(2))
    share.arrive()

    def store(d, value):
        total = cot_own[d].astype(f32) + value
        grad_mid[d] = total
        low = total.astype(bf16)
        branch_own[d] = low
        parts[d, :, 4:5] = jnp.sum(low.astype(f32), axis=1, keepdims=True)
        parts[d, :, 5:6] = jnp.sum(cot_own[d].astype(f32), axis=1, keepdims=True)

    parts[...] = jnp.zeros_like(parts)

    def put(d, gain, shift):
        parts[d, :, 2:3] = gain
        parts[d, :, 3:4] = shift

    norm_back(
        rows,
        width,
        lambda d: share.total(d),
        lambda d: resid[d],
        lambda d: vec[d, :, 3:4],
        store,
        put,
    )
    gather.start()
    serve(queue, at(3))
    fill_partial(part_out, w_down, hidden, cols, rows, width)
    serve(queue, at(4))
    gather.forward()
    serve(queue, rows)
    down.finish()
    up.finish()
    share.finish()
    gather.finish()


def back_two_kernel(
    rows, cols, ready, part_out, normed_mid, grad_pre, w_out, branch, att, qkv, logs, resid,
    vec, normed_in, w_qkv, own, late_mid, parts,
    grad_up, wq_o, wo_o, bias_o, units_o, feat_o, res_out, res_tok,
    grad_tok, grad_qkv, grad_att, dkey, dval, lead_sum, rest_sum, out_sum, gq, go, gb,
    units, units_in, qkv_in, output, feat, feat_in, feat_sum, feat_cols,
    bs, br, ts, tr, es, er, fs, fr, us, ur, ws, wr, loc, *scratch,
):
    p = Place(rows, cols)
    width = own.shape[-1]
    slots = logs.shape[0]
    ch, och = CHANNELS // cols, HD // cols
    ffc = grad_pre.shape[0]
    half = grad_up.shape[1]
    qn = slots * CHANNELS
    share = Share(p, *scratch[:6])
    lead = slots * 4 // 7
    up = Reduce(
        p, normed_mid, grad_pre.at[pl.ds(ffc - half, half)], scratch[6:9], middle(half, 0)
    ).into(grad_up)
    out = Reduce(p, branch, att, scratch[9:12], middle(slots * HD, 1)).into(out_sum)
    wide = [
        Reduce(
            p,
            normed_in,
            grad_qkv.at[pl.ds(first * CHANNELS, count * CHANNELS)],
            scratch[i : i + 3],
            middle(count * CHANNELS, 0),
        ).into(total)
        for first, count, i, total in (
            (0, lead, 12, lead_sum),
            (lead, slots - lead, 15, rest_sum),
        )
    ]
    early = steps(rows, up, out)
    late = steps(rows, *wide)
    at = lambda t: rows * t // 8
    share_out = Share(p, scratch[0], scratch[18], scratch[2], *scratch[19:22])
    part_copy = pltpu.make_async_copy(part_out, scratch[0], loc.at[3])
    grad_mid = resid
    mid_copy = pltpu.make_async_copy(late_mid, grad_mid, loc.at[4])
    part_copy.start()
    back_out = Back(p, output, res_out, (bs, br))
    back_tok = Back(p, grad_tok, res_tok, (ts, tr))
    sources = [(q, back_out.col) for q in range(rows)]
    targets = [home(p, q) for q in range(rows)]
    meet(sources + targets + all_col(p) + all_row(p))
    part_copy.wait()
    share_out.start()
    ready("normed_mid", "grad_pre", "branch", "att")
    serve(early, 0)
    share_out.middle()
    ready("w_out", "qkv", "logs")
    for s in range(slots):
        total = product(w_out[0, :, s * HD : (s + 1) * HD], branch[0], TN)
        for d in range(1, rows):
            total = total + product(w_out[d, :, s * HD : (s + 1) * HD], branch[d], TN)
        grad_att[s * HD : (s + 1) * HD] = total.astype(bf16)

    def head(s, carry):
        base = pl.multiple_of(s * CHANNELS, 64)

        def store(row, first, last, value):
            grad_qkv[pl.ds(base + row, HD), first:last] = value.astype(bf16)

        attend_back(
            qkv[pl.ds(base, CHANNELS)],
            grad_att[pl.ds(pl.multiple_of(s * HD, 64), HD)],
            logs[s],
            store,
            dkey,
            dval,
        )
        return carry

    serve(early, at(1))
    lax.fori_loop(0, lead // 2, head, 0)
    serve(early, at(2))
    lax.fori_loop(lead // 2, lead, head, 0)
    serve(early, at(3))
    ready("normed_in")
    wide[0].step(0)
    ready("resid", "vec")
    share_out.arrive()

    def result(d, carry):
        output[d] = (resid[d] + share_out.total(d) + vec[d, :, 5:6]).astype(bf16)
        return carry

    lax.fori_loop(0, rows, result, 0)
    back_out.start()
    share_out.finish()
    mid_copy.start()
    late.pop(0)
    lax.fori_loop(lead, slots, head, 0)
    serve(early, at(4))
    serve(late, 0)
    ready("w_qkv", "own", "parts")
    mid_copy.wait()
    fill_partial(share.part, w_qkv, grad_qkv, cols, rows, width)
    share.start()
    serve(early, at(5))
    serve(late, at(1))
    ones = jnp.ones((8, L), bf16)
    units[:, :ffc] = product(ones, grad_pre[...], NT)[0:1]
    units[:, ffc:] = product(ones, grad_qkv[...], NT)[0:1]
    row_units = []
    for o, peer in enumerate(all_row(p)):
        row_units.append(remote(units, units_in.at[o + 1], us.at[o], ur.at[o], peer))
    for copy in row_units:
        copy.start()
    share.middle()
    serve(early, at(6))
    serve(late, at(2))
    serve(early, rows)
    for j in range(cols):
        for s in range(slots):
            base = s * HD + j * och
            go[j, :, s * och : (s + 1) * och] = out_sum[:, base : base + och]
    swap_o = exchange_copies(p, go, wo_o, es.at[0], er.at[0])
    for copy in swap_o:
        copy.start()
    serve(late, at(3))
    share.arrive()

    def store_tokens(d, value):
        grad_tok[d] = (grad_mid[d] + value).astype(bf16)

    def put(d, gain, shift):
        parts[d, :, 0:1] = gain
        parts[d, :, 1:2] = shift

    norm_back(
        rows,
        width,
        lambda d: share.total(d),
        lambda d: own[d].astype(f32),
        lambda d: vec[d, :, 0:1],
        store_tokens,
        put,
    )
    back_tok.start()
    serve(late, at(4))
    eye = (
        lax.broadcasted_iota(jnp.int32, (8, 8), 0) == lax.broadcasted_iota(jnp.int32, (8, 8), 1)
    ).astype(f32)
    for d in range(rows):
        feat[d] = lax.dot_general(
            eye, parts[d], NT, precision=lax.Precision.HIGHEST, preferred_element_type=f32
        )
    feats = []
    for o in range(1, rows):
        to = lax.rem(p.r + o, rows)
        feats.append(remote(feat.at[to], feat_in.at[o], fs.at[o], fr.at[o], (to, p.c)))
    for copy in feats:
        copy.start()
    serve(late, at(5))
    total = units[...]
    for o, copy in enumerate(row_units):
        copy.wait_recv()
        total = total + units_in[o + 1]
    units_o[...] = total[:, :ffc]
    qkv_in[...] = total[:, ffc:]
    for j in range(cols):
        for s in range(slots):
            base = s * CHANNELS + j * ch
            gb[j, :, s * ch : (s + 1) * ch] = qkv_in[:, base : base + ch]
    swap_b = exchange_copies(p, gb, bias_o, es.at[1], er.at[1])
    for copy in swap_b:
        copy.start()
    serve(late, at(6))
    total = feat[p.r]
    for o, copy in enumerate(feats):
        copy.wait_recv()
        total = total + feat_in[o + 1]
    feat_sum[...] = total
    sums = [
        remote(feat_sum, feat_cols.at[o + 1], ws.at[o], wr.at[o], peer)
        for o, peer in enumerate(all_col(p))
    ]
    for copy in sums:
        copy.start()
    serve(late, rows)
    for j in range(cols):
        for s in range(slots):
            base = (s if s < lead else s - lead) * CHANNELS + j * ch
            source = lead_sum if s < lead else rest_sum
            gq[j, :, s * ch : (s + 1) * ch] = source[:, base : base + ch]
    for ring in [up, out] + wide:
        ring.finish()
    swap_q = exchange_copies(p, gq, wq_o, es.at[2], er.at[2])
    for copy in swap_q:
        copy.start()
    keeps = [
        pltpu.make_async_copy(src.at[p.c], dst.at[p.c], loc.at[i])
        for i, (src, dst) in enumerate(((gq, wq_o), (go, wo_o), (gb, bias_o)))
    ]
    for copy in keeps:
        copy.start()
    for o, copy in enumerate(sums):
        copy.wait_recv()
        total = total + feat_cols[o + 1]
    feat_o[...] = total
    share.finish()
    back_out.finish()
    back_tok.finish()
    for copy in swap_o + swap_b + swap_q:
        copy.wait()
    for copy in keeps:
        copy.wait()
    for copy in row_units + feats + sums:
        copy.wait_send()


RAW = ("part_out", "late_mid")
INPUTS = {
    back_one_kernel: (
        "w_up", "grad_pre", "cot", "hidden", "cot_own", "resid", "vec", "w_down", "normed_mid",
    ),
    back_two_kernel: (
        "part_out", "normed_mid", "grad_pre", "w_out", "branch", "att", "qkv", "logs", "resid",
        "vec", "normed_in", "w_qkv", "own", "late_mid", "parts",
    ),
}


def call(kernel, outs, scratch, args, collective, spec=VMEM, in_specs=None, out_specs=None):
    return pl.pallas_call(
        kernel,
        out_shape=[jax.ShapeDtypeStruct(s, t) for s, t in outs],
        in_specs=[spec] * len(args) if in_specs is None else in_specs,
        out_specs=[spec] * len(outs) if out_specs is None else out_specs,
        scratch_shapes=scratch,
        compiler_params=pltpu.CompilerParams(
            collective_id=collective, has_side_effects=True, vmem_limit_bytes=LIMIT
        ),
    )(*args)


def staged(kernel, count, *refs):
    rows, cols, outs = count
    names = INPUTS[kernel]
    ins = len(names)
    rest = list(refs[ins + outs :])
    buffers = [refs[i] if name in RAW else rest.pop(0) for i, name in enumerate(names)]
    sem = rest.pop(0)
    copies = {
        name: pltpu.make_async_copy(refs[i], buffers[i], sem.at[i])
        for i, name in enumerate(names)
        if name not in RAW
    }
    for name in copies:
        copies[name].start()

    def ready(*names):
        for name in names:
            copies[name].wait()

    kernel(rows, cols, ready, *buffers, *refs[ins : ins + outs], *rest)


def call_staged(kernel, rows, cols, outs, scratch, args, collective):
    return call(
        functools.partial(staged, kernel, (rows, cols, len(outs))),
        outs,
        [
            pltpu.VMEM(arg.shape, arg.dtype)
            for name, arg in zip(INPUTS[kernel], args)
            if name not in RAW
        ]
        + [pltpu.SemaphoreType.DMA((len(args),))]
        + scratch,
        args,
        collective,
        in_specs=[ANY] * len(args),
    )


def one_hot(target, size):
    return (target[:, None] == jnp.arange(size, dtype=jnp.int32)[None, :]).astype(bf16)


def split_matrix(channels, slots, cols):
    source = jnp.arange(channels * H, dtype=jnp.int32)
    channel, head = source // H, source % H
    return one_hot(
        ((head % cols) * slots + head // cols) * channels + channel, cols * slots * channels
    )


def to_owners(weight, matrix, cols):
    moved = product(weight, matrix, NN).astype(bf16)
    return moved.reshape(moved.shape[0], cols, -1).transpose(1, 0, 2)


def from_owners(blocks, matrix):
    flat = blocks.transpose(1, 0, 2).reshape(blocks.shape[1], -1)
    return product(flat, matrix, NT)


def body(
    tokens, ln1_gain, ln1_shift, weight_qkv, bias_qkv, weight_out, bias_out, ln2_gain,
    ln2_shift, weight_up, bias_up, weight_down, bias_down, cotangent,
):
    rows, cols = lax.axis_size("row"), lax.axis_size("col")
    slots = (H + cols - 1) // cols
    ch, och = CHANNELS // cols, HD // cols
    feats = D // rows
    width = L // cols
    ffc = weight_up.shape[1]
    dma = pltpu.SemaphoreType.DMA

    qkv_split, out_split = split_matrix(ch, slots, cols), split_matrix(och, slots, cols)
    wq = to_owners(weight_qkv, qkv_split, cols)
    wo = to_owners(weight_out, out_split, cols)
    bias = jnp.pad(bias_qkv.reshape(ch, H), ((0, 0), (0, slots * cols - H)))
    bias = bias.reshape(ch, slots, cols).transpose(2, 1, 0).reshape(cols, 1, slots * ch)
    terms = []
    for _ in range(3):
        terms.append(lax.reduce_precision(bias, 8, 7))
        bias = bias - terms[-1]
    bias = jnp.concatenate(terms + [jnp.zeros_like(bias)] * 5, axis=1).astype(bf16)
    zero = jnp.zeros_like(ln1_gain)
    vec = jnp.stack(
        [ln1_gain, ln1_shift, bias_out, ln2_gain, ln2_shift, bias_down, zero, zero]
    )
    (
        w_qkv, w_out, w_up, w_down, normed_in, qkv, att, logs, resid, normed_mid, hidden,
        grad_pre, cot, tok_own, cot_own, vec,
    ) = forward(
        rows,
        cols,
        (tokens, cotangent, wq, wo, bias, vec, weight_up, weight_down, bias_up[:, None]),
        (feats, width, slots, ffc),
    )
    half = ffc // 2 // 128 * 128
    grad_weight_down, grad_up_one, grad_mid, branch, part_out, parts = call_staged(
        back_one_kernel,
        rows,
        cols,
        [
            ((feats, ffc), f32),
            ((feats, half), f32),
            ((rows, feats, width), f32),
            ((rows, feats, L), bf16),
            ((cols, rows, feats, width), bf16),
            ((rows, feats, 8), f32),
        ],
        [pltpu.VMEM((rows, feats, width), bf16)]
        + share_scratch(rows, cols, feats, width)
        + spread_sems(cols)
        + reduce_scratch(rows, feats, ffc)
        + reduce_scratch(rows, feats, half),
        (w_up, grad_pre, cot, hidden, cot_own, resid, vec, w_down, normed_mid),
        3,
    )
    qn, on = slots * CHANNELS, slots * HD
    vm = pltpu.VMEM
    lead = slots * 4 // 7 * CHANNELS
    (
        grad_up_two, gq, go, gb, grad_bias_up, feat, res_out, res_tok
    ) = call_staged(
        back_two_kernel,
        rows,
        cols,
        [
            ((feats, ffc - half), f32),
            ((cols, feats, slots * ch), bf16),
            ((cols, feats, slots * och), bf16),
            ((cols, 1, slots * ch), f32),
            ((1, ffc), f32),
            ((8, feats), f32),
            ((feats, rows * width), bf16),
            ((feats, rows * width), bf16),
        ],
        [
            vm((rows, feats, width), bf16),
            vm((qn, L), bf16),
            vm((on, L), bf16),
            vm((HD, L), f32),
            vm((HD, L), f32),
            vm((feats, lead), bf16),
            vm((feats, qn - lead), bf16),
            vm((feats, on), bf16),
            vm((cols, feats, slots * ch), bf16),
            vm((cols, feats, slots * och), bf16),
            vm((cols, 1, slots * ch), f32),
            vm((1, ffc + qn), f32),
            vm((rows, 1, ffc + qn), f32),
            vm((1, qn), f32),
            vm((rows, feats, width), bf16),
            vm((rows, 8, feats), f32),
            vm((rows, 8, feats), f32),
            vm((8, feats), f32),
            vm((cols, 8, feats), f32),
        ]
        + [dma((rows + 1,)), dma((rows,))] * 2
        + [dma((3, cols)), dma((3, cols))]
        + [dma((rows,))] * 4
        + [dma((cols,))] * 2
        + [dma((5,))]
        + share_scratch(rows, cols, feats, width)
        + reduce_scratch(rows, feats, ffc - half)
        + reduce_scratch(rows, feats, on)
        + reduce_scratch(rows, feats, lead)
        + reduce_scratch(rows, feats, qn - lead)
        + [share_scratch(rows, cols, feats, width)[i] for i in (1, 3, 4, 5)],
        (
            part_out, normed_mid, grad_pre, w_out, branch, att, qkv, logs, resid,
            vec, normed_in, w_qkv, tok_own, grad_mid, parts,
        ),
        4,
    )
    grad_weight_up = jnp.concatenate([grad_up_one, grad_up_two], axis=1)
    grad_weight_qkv = from_owners(gq, qkv_split)
    grad_weight_out = from_owners(go, out_split)
    grad_bias_qkv = gb.reshape(cols, slots, ch).transpose(2, 1, 0)
    grad_bias_qkv = grad_bias_qkv.reshape(ch, slots * cols)[:, :H].reshape(-1)
    return (
        res_out,
        res_tok.astype(f32),
        feat[0],
        feat[1],
        grad_weight_qkv,
        grad_bias_qkv,
        grad_weight_out,
        feat[4],
        feat[2],
        feat[3],
        grad_weight_up,
        grad_bias_up[0],
        grad_weight_down,
        feat[5],
    )


def solution(mesh):
    both, row, col = P("row", "col"), P("row"), P("col")
    in_specs = (both, row, row, both, col, both, row, row, row, both, col, both, row, both)
    out_specs = (both, both, row, row, both, col, both, row, row, row, both, col, both, row)
    return jax.shard_map(body, mesh=mesh, in_specs=in_specs, out_specs=out_specs, check_vma=False)
```

```python
import functools

import jax
import jax.numpy as jnp
from jax import lax
from jax.experimental import pallas as pl
from jax.experimental.pallas import tpu as pltpu
from jax.sharding import PartitionSpec as P

D = 1600
H = 25
HD = 64
L = 1024
CHANNELS = 3 * HD
QB = 256

epsilon = 1e-05
excluded = -1e30

TN = (((0,), (0,)), ((), ()))
NN = (((1,), (0,)), ((), ()))
NT = (((1,), (1,)), ((), ()))
MESH = pl.DeviceIdType.MESH
ANY = pl.BlockSpec(memory_space=pl.ANY)
VMEM = pl.BlockSpec(memory_space=pltpu.VMEM)
LIMIT = 62 * 2**20
f32 = jnp.float32
bf16 = jnp.bfloat16


def product(left, right, dims):
    return lax.dot_general(left, right, dims, preferred_element_type=f32)


def remote(src, dst, send, recv, device):
    return pltpu.make_async_remote_copy(
        src_ref=src,
        dst_ref=dst,
        send_sem=send,
        recv_sem=recv,
        device_id=device,
        device_id_type=MESH,
    )


def meet(devices):
    sem = pltpu.get_barrier_semaphore()
    for device in devices:
        pl.semaphore_signal(sem, inc=1, device_id=device, device_id_type=MESH)
    pl.semaphore_wait(sem, len(devices))


def lanes(index, width):
    return pl.ds(pl.multiple_of(index * width, 128), width)


class Place:
    def __init__(self, rows, cols):
        self.R, self.C, self.A, self.X = rows, cols, rows // 2, cols // 2
        self.r, self.c = lax.axis_index("row"), lax.axis_index("col")
        self.a, self.b = self.r // 2, lax.rem(self.r, 2)
        self.x, self.k = self.c // 2, lax.rem(self.c, 2)
        self.core = (self.r, self.x * 2 + 1 - self.k)
        self.pair = (self.a * 2 + 1 - self.b, self.c)
        self.pos = jnp.where(self.b == 0, self.a, rows - 1 - self.a)
        self.around = [(self.row_at(1), self.c), (self.row_at(-1), self.c)]

    def row_at(self, o):
        at = lax.rem(self.pos + o + self.R, self.R)
        return jnp.where(at < self.A, at * 2, (self.R - 1 - at) * 2 + 1)

    def ahead(self, o):
        return lax.rem(self.a + o, self.A)

    def behind(self, o):
        return lax.rem(self.a - o + self.A, self.A)

    def line(self, o):
        return (self.ahead(o) * 2 + self.b, self.c)

    def x_ahead(self, o):
        return lax.rem(self.x + o, self.X)

    def x_behind(self, o):
        return lax.rem(self.x - o + self.X, self.X)

    def side(self, o):
        return (self.r, self.x_ahead(o) * 2 + self.k)

    def col_peers(self):
        return [self.core] + [self.side(o) for o in range(1, self.X)]

    def row_peers(self):
        return [self.pair] + [self.line(o) for o in range(1, self.A)]


class Spread:
    def __init__(self, p, own, full, width, send, recv):
        self.p, self.own, self.full, self.width = p, own, full, width
        self.send, self.recv = send, recv

    def part(self, block):
        return self.full.at[..., lanes(block, self.width)]

    def side_copy(self, o):
        return remote(
            self.own, self.part(self.p.c), self.send.at[o], self.recv.at[o], self.p.side(o)
        )

    def core_copy(self, o):
        p = self.p
        block = p.c if o == 0 else p.x_behind(o) * 2 + p.k
        src = self.own if o == 0 else self.part(block)
        i = p.X + o
        return remote(src, self.part(block), self.send.at[i], self.recv.at[i], p.core)

    def local(self):
        i = 2 * self.p.X
        return pltpu.make_async_copy(self.own, self.part(self.p.c), self.send.at[i])

    def start(self):
        for o in range(1, self.p.X):
            self.side_copy(o).start()
        self.core_copy(0).start()
        self.local().start()

    def forward(self):
        for o in range(1, self.p.X):
            self.side_copy(o).wait_recv()
            self.core_copy(o).start()

    def finish(self):
        for o in range(self.p.X):
            self.core_copy(o).wait()
        for o in range(1, self.p.X):
            self.side_copy(o).wait_send()
        self.local().wait()


def spread_sems(cols):
    return [pltpu.SemaphoreType.DMA((cols + 1,)), pltpu.SemaphoreType.DMA((cols + 1,))]


class Share:
    def __init__(self, p, part, core_in, side_out, side_in, send, recv):
        self.p, self.part, self.core_in = p, part, core_in
        self.side_out, self.side_in, self.send, self.recv = side_out, side_in, send, recv

    def core_copy(self, x):
        p = self.p
        return remote(
            self.part.at[x * 2 + 1 - p.k],
            self.core_in.at[x],
            self.send.at[x],
            self.recv.at[x],
            p.core,
        )

    def side_copy(self, o):
        p = self.p
        i = p.X + o - 1
        return remote(
            self.side_out.at[o - 1],
            self.side_in.at[o - 1],
            self.send.at[i],
            self.recv.at[i],
            p.side(o),
        )

    def start(self):
        for x in range(self.p.X):
            self.core_copy(x).start()

    def middle(self):
        p = self.p
        for x in range(p.X):
            self.core_copy(x).wait_recv()
        for o in range(1, p.X):
            x = p.x_ahead(o)

            def add(d, carry, x=x, o=o):
                total = self.part[x * 2 + p.k, d].astype(f32) + self.core_in[x, d].astype(f32)
                self.side_out[o - 1, d] = total.astype(bf16)
                return carry

            lax.fori_loop(0, p.R, add, 0)
            self.side_copy(o).start()

    def arrive(self):
        for o in range(1, self.p.X):
            self.side_copy(o).wait_recv()

    def total(self, d):
        p = self.p
        result = self.part[p.c, d].astype(f32) + self.core_in[p.x, d].astype(f32)
        for o in range(1, p.X):
            result = result + self.side_in[o - 1, d].astype(f32)
        return result

    def finish(self):
        for x in range(self.p.X):
            self.core_copy(x).wait_send()
        for o in range(1, self.p.X):
            self.side_copy(o).wait_send()


def share_scratch(rows, cols, feats, width):
    half = cols // 2
    return [
        pltpu.VMEM((cols, rows, feats, width), bf16),
        pltpu.VMEM((half, rows, feats, width), bf16),
        pltpu.VMEM((half - 1, rows, feats, width), bf16),
        pltpu.VMEM((half - 1, rows, feats, width), bf16),
        pltpu.SemaphoreType.DMA((cols - 1,)),
        pltpu.SemaphoreType.DMA((cols - 1,)),
    ]


def fill_partial(part, weight, act, cols, rows, width, between=lambda: None):
    def one(d, carry):
        for j in range(cols):
            part[j, d] = product(
                weight[d], act[:, j * width : (j + 1) * width], NN
            ).astype(bf16)
        return carry

    lax.fori_loop(0, rows // 2, one, 0)
    between()
    lax.fori_loop(rows // 2, rows, one, 0)


def middle(size, extra):
    return min((size // 256 + extra) * 128, (size - 1) // 128 * 128)


class Reduce:
    def __init__(self, p, left, right, scratch, cut):
        self.p, self.left, self.right = p, left, right
        self.slots, self.send, self.recv = scratch
        self.parts = (slice(0, cut), slice(cut, self.slots.shape[-1]))

    def copy(self, way, t):
        part = self.parts[way]
        i = way * self.p.R + t
        return remote(
            self.slots.at[t, :, part],
            self.slots.at[t + 1, :, part],
            self.send.at[i],
            self.recv.at[i],
            self.p.around[way],
        )

    def step(self, t):
        p = self.p
        for way in range(2):
            part = self.parts[way]
            row = p.row_at(-1 - t if way == 0 else 1 + t)
            value = product(self.left[row], self.right[part], NT)
            if t > 0:
                self.copy(way, t - 1).wait_recv()
                value = value + self.slots[t, :, part].astype(f32)
            if t < p.R - 1:
                self.slots[t, :, part] = value.astype(bf16)
                self.copy(way, t).start()
            else:
                self.out[:, part] = value.astype(self.out.dtype)

    def into(self, out):
        self.out = out
        return self

    def finish(self):
        for way in range(2):
            for t in range(self.p.R - 1):
                self.copy(way, t).wait_send()


def reduce_scratch(rows, feats, size):
    return [
        pltpu.VMEM((rows, feats, size), bf16),
        pltpu.SemaphoreType.DMA((2 * rows,)),
        pltpu.SemaphoreType.DMA((2 * rows,)),
    ]


def steps(rows, *rings):
    return [(ring, t) for t in range(rows) for ring in rings]


def serve(queue, t):
    while queue and queue[0][1] <= t:
        ring, at = queue.pop(0)
        ring.step(at)


def take(queue, count):
    for ring, at in queue[:count]:
        ring.step(at)
    del queue[:count]


def home(p, q):
    block = p.c * p.R + q
    return (block // p.C, lax.rem(block, p.C))


def own_block(p):
    block = p.r * p.C + p.c
    return block // p.R, lax.rem(block, p.R)


def equal(left, right):
    return jnp.logical_and(left[0] == right[0], left[1] == right[1])


def exchange_copies(p, src, dst, send, recv):
    out = []
    for o in range(1, p.C):
        to = lax.rem(p.c + o, p.C)
        out.append(remote(src.at[to], dst.at[p.c], send.at[o], recv.at[o], (p.r, to)))
    return out


def all_col(p):
    return [(p.r, lax.rem(p.c + o, p.C)) for o in range(1, p.C)]


def all_row(p):
    return [(lax.rem(p.r + o, p.R), p.c) for o in range(1, p.R)]


class Back:
    def __init__(self, p, src, dst, sems):
        self.p, self.src, self.dst = p, src, dst
        self.send, self.recv = sems
        self.width = src.shape[-1]
        self.col, self.place = own_block(p)

    def slot(self, q):
        return self.dst.at[:, lanes(q, self.width)]

    def outgoing(self, q):
        return remote(
            self.src.at[q],
            self.slot(self.place),
            self.send.at[q],
            self.recv.at[self.place],
            (q, self.col),
        )

    def staying(self, q):
        return pltpu.make_async_copy(
            self.src.at[q], self.slot(self.place), self.send.at[self.p.R]
        )

    def start(self):
        p = self.p
        for q in range(p.R):
            here = equal((q, self.col), (p.r, p.c))

            @pl.when(here)
            def _():
                self.staying(q).start()

            @pl.when(jnp.logical_not(here))
            def _():
                self.outgoing(q).start()

    def finish(self):
        p = self.p
        for q in range(p.R):
            source = home(p, q)
            here = equal(source, (p.r, p.c))

            @pl.when(here)
            def _():
                self.staying(0).wait()

            @pl.when(jnp.logical_not(here))
            def _():
                remote(
                    self.src.at[0], self.slot(q), self.send.at[0], self.recv.at[q], source
                ).wait_recv()

        for q in range(p.R):

            @pl.when(jnp.logical_not(equal((q, self.col), (p.r, p.c))))
            def _():
                self.outgoing(q).wait_send()


def masked_scores(key, query, first):
    scores = product(key, query, TN) * HD ** (-0.5)
    keys = lax.broadcasted_iota(jnp.int32, scores.shape, 0)
    queries = lax.broadcasted_iota(jnp.int32, scores.shape, 1) + first
    return jnp.where(keys <= queries, scores, excluded)


def attend_back(qkv, grad, logs, out, dkey, dval):
    query, key, value = qkv[:HD], qkv[HD : 2 * HD], qkv[2 * HD :]
    dkey[...] = jnp.zeros_like(dkey)
    dval[...] = jnp.zeros_like(dval)
    for first in range(0, L, QB):
        last = first + QB
        scores = masked_scores(key[:, :last], query[:, first:last], first)
        weights = jnp.exp(scores - logs[:, first:last])
        back = grad[:, first:last]
        dval[:, :last] += product(back, weights.astype(bf16), NT)
        grad_weights = product(value[:, :last], back, TN)
        inner = jnp.sum(weights * grad_weights, axis=0, keepdims=True)
        low = (weights * (grad_weights - inner)).astype(bf16)
        out(0, first, last, product(key[:, :last], low, NN) * HD ** (-0.5))
        dkey[:, :last] += product(query[:, first:last], low, NT)
    out(HD, 0, L, dkey[...] * HD ** (-0.5))
    out(2 * HD, 0, L, dval[...])


def norm_back(rows, width, incoming, values, gain, store, parts):
    zero = jnp.zeros((1, width), f32)

    def sums(d, total):
        return total + jnp.sum(values(d), axis=0, keepdims=True)

    mean = lax.fori_loop(0, rows, sums, zero) / D

    def squares(d, total):
        value = values(d) - mean
        return total + jnp.sum(value * value, axis=0, keepdims=True)

    scale = lax.rsqrt(lax.fori_loop(0, rows, squares, zero) / D + epsilon)

    def moments(d, totals):
        centred = (values(d) - mean) * scale
        back = incoming(d)
        parts(d, jnp.sum(back * centred, axis=1, keepdims=True), jnp.sum(back, axis=1, keepdims=True))
        scaled = back * gain(d)
        return (
            totals[0] + jnp.sum(scaled, axis=0, keepdims=True),
            totals[1] + jnp.sum(scaled * centred, axis=0, keepdims=True),
        )

    first, second = lax.fori_loop(0, rows, moments, (zero, zero))

    def last(d, carry):
        centred = (values(d) - mean) * scale
        scaled = incoming(d) * gain(d)
        store(d, scale * (scaled - first / D - centred * (second / D)))
        return carry

    lax.fori_loop(0, rows, last, 0)


class Ring:
    def __init__(self, p, own, full, sems, cut):
        self.p, self.own, self.full = p, own, full
        self.send, self.recv = sems
        self.parts = (slice(0, cut), slice(cut, own.shape[1]))

    def copy(self, way, t):
        p = self.p
        row = p.row_at(-t if way == 0 else t)
        part = self.parts[way]
        i = way * p.R + t
        return remote(
            self.own.at[:, part] if t == 0 else self.full.at[row, :, part],
            self.full.at[row, :, part],
            self.send.at[i],
            self.recv.at[i],
            p.around[way],
        )

    def local(self):
        return pltpu.make_async_copy(
            self.own, self.full.at[self.p.r], self.send.at[self.p.R - 1]
        )

    def step(self, t):
        if t == 0:
            self.local().start()
        for way in range(2):
            if t > 0:
                self.copy(way, t - 1).wait_recv()
            if t < self.p.R - 1:
                self.copy(way, t).start()
        if t == self.p.R - 1:
            self.local().wait()

    def finish(self):
        for way in range(2):
            for t in range(self.p.R - 1):
                self.copy(way, t).wait_send()


class Redistribute:
    def __init__(self, p, src, own, sems):
        self.p, self.src, self.own = p, src, own
        self.send, self.recv = sems
        self.width = own.shape[-1]
        self.col, _ = own_block(p)

    def outgoing(self, q, target):
        return remote(
            self.src.at[:, q * self.width : (q + 1) * self.width],
            self.own.at[self.p.r],
            self.send.at[q],
            self.recv.at[self.p.r],
            target,
        )

    def staying(self, q):
        return pltpu.make_async_copy(
            self.src.at[:, q * self.width : (q + 1) * self.width],
            self.own.at[self.p.r],
            self.send.at[self.p.R],
        )

    def start(self):
        p = self.p
        for q in range(p.R):
            target = home(p, q)
            here = equal(target, (p.r, p.c))

            @pl.when(here)
            def _():
                self.staying(q).start()

            @pl.when(jnp.logical_not(here))
            def _():
                self.outgoing(q, target).start()

    def arrive(self):
        p = self.p
        for q in range(p.R):
            here = equal((q, self.col), (p.r, p.c))

            @pl.when(here)
            def _():
                self.staying(0).wait()

            @pl.when(jnp.logical_not(here))
            def _():
                remote(
                    self.src.at[:, 0 : self.width],
                    self.own.at[q],
                    self.send.at[0],
                    self.recv.at[q],
                    (q, self.col),
                ).wait_recv()

    def finish(self):
        p = self.p
        for q in range(p.R):
            target = home(p, q)

            @pl.when(jnp.logical_not(equal(target, (p.r, p.c))))
            def _():
                self.outgoing(q, target).wait_send()


def norm_scale(rows, width, values):
    zero = jnp.zeros((1, width), f32)

    def sums(d, total):
        return total + jnp.sum(values(d), axis=0, keepdims=True)

    mean = lax.fori_loop(0, rows, sums, zero) / D

    def squares(d, total):
        value = values(d) - mean
        return total + jnp.sum(value * value, axis=0, keepdims=True)

    return mean, lax.rsqrt(lax.fori_loop(0, rows, squares, zero) / D + epsilon)


def tiled(size, tile, one):
    count = size // tile

    def step(i, carry):
        one(pl.multiple_of(i * tile, tile), tile)
        return carry

    lax.fori_loop(0, count, step, 0)
    if size % tile:
        one(count * tile, size % tile)


def summed(weight, act, rows, first, size):
    total = product(weight[0, :, pl.ds(first, size)], act[0], TN)
    for d in range(1, rows):
        total = total + product(weight[d, :, pl.ds(first, size)], act[d], TN)
    return total


def forward_kernel(
    rows, cols,
    tok, cot, wq, wo, bias, vec, wu, wd, bias_up,
    wq_f, wo_f, wu_f, wd_f, n1_f, qkv_f, att_f, logs_f, resid_f, n2_f, hidden_f, gp_f,
    cot_f, tok_own_f, cot_own_f, vec_f,
    qfull, ofull, ufull, dfull, qown, oown, qin, oin, bin_, qbias, vin, vecs,
    xfull, n1, qkv, att, logs, resid, normed, n2, hidden, gp, cfull, tok_own, cot_own,
    part, core_in, side_out, side_in, share_s, share_r,
    qs, qr, os_, or_, us, ur, ds0, dr0, ts, tr, cs, cr,
    xs, xr, ys, yr, ns, nr, es, er, vs, vr, loc,
):
    p = Place(rows, cols)
    width = tok_own.shape[-1]
    slots = logs.shape[0]
    ch = CHANNELS // cols
    ffc = hidden.shape[0]
    red_tok = Redistribute(p, tok, tok_own, (ts, tr))
    red_cot = Redistribute(p, cot, cot_own, (cs, cr))
    sources = [(q, red_tok.col) for q in range(rows)]
    targets = [home(p, q) for q in range(rows)]
    meet(sources + targets + all_col(p) + all_row(p))

    groups = ((wq, qin), (wo, oin), (bias, bin_))
    swaps = []
    for i, (src, dst) in enumerate(groups):
        swaps.append(exchange_copies(p, src, dst, es.at[i], er.at[i]))
    for copies in swaps:
        for copy in copies:
            copy.start()
    keeps = [
        pltpu.make_async_copy(src.at[p.c], dst.at[p.c], loc.at[i])
        for i, (src, dst) in enumerate(groups)
    ]
    keeps.append(pltpu.make_async_copy(vec, vin.at[p.r], loc.at[3]))
    for copy in keeps:
        copy.start()
    red_tok.start()
    vec_copies = [
        remote(vec, vin.at[p.r], vs.at[o], vr.at[o], peer)
        for o, peer in enumerate(all_row(p))
    ]
    for copy in vec_copies:
        copy.start()

    for copies, keep in zip(swaps, keeps):
        for copy in copies:
            copy.wait_recv()
        keep.wait()
    och = HD // cols
    for j in range(cols):
        for s in range(slots):
            base = s * CHANNELS + j * ch
            qown[:, base : base + ch] = qin[j, :, s * ch : (s + 1) * ch]
            qbias[:, base : base + ch] = bin_[j, :, s * ch : (s + 1) * ch]
            base = s * HD + j * och
            oown[:, base : base + och] = oin[j, :, s * och : (s + 1) * och]
    ring_q = Ring(p, qown, qfull, (qs, qr), middle(slots * CHANNELS, 0))
    ring_o = Ring(p, oown, ofull, (os_, or_), middle(slots * HD, 1))
    ring_u = Ring(p, wu, ufull, (us, ur), middle(ffc, 0))
    ring_d = Ring(p, wd, dfull, (ds0, dr0), middle(ffc, 1))
    early = steps(rows, ring_q, ring_o)
    late = steps(rows, ring_u, ring_d)
    serve(early, 0)
    red_tok.arrive()
    spread_x = Spread(p, tok_own, xfull, width, xs, xr)
    spread_x.start()
    serve(early, rows * 1 // 8)
    for copy in vec_copies:
        copy.wait_recv()
    keeps[3].wait()
    eye = (
        lax.broadcasted_iota(jnp.int32, (8, 8), 0) == lax.broadcasted_iota(jnp.int32, (8, 8), 1)
    ).astype(f32)
    for d in range(rows):
        vecs[d] = lax.dot_general(
            vin[d], eye, TN, precision=lax.Precision.HIGHEST, preferred_element_type=f32
        )
    serve(early, rows * 2 // 8)
    serve(early, rows * 3 // 8)
    spread_x.forward()
    spread_x.finish()
    outs = []

    def keep_out(src, dst):
        copy = pltpu.make_async_copy(src, dst, loc.at[4 + len(outs)])
        copy.start()
        outs.append(copy)

    keep_out(tok_own, tok_own_f)
    keep_out(vecs, vec_f)
    mean, scale = norm_scale(rows, L, lambda d: xfull[d].astype(f32))
    serve(early, rows * 4 // 8)

    def normal(d, carry):
        value = (xfull[d].astype(f32) - mean) * scale
        n1[d] = (value * vecs[d, :, 0:1] + vecs[d, :, 1:2]).astype(bf16)
        return carry

    lax.fori_loop(0, rows, normal, 0)
    keep_out(n1, n1_f)

    serve(early, rows - 2)
    red_cot.start()
    serve(late, 0)
    serve(early, rows)
    keep_out(qfull, wq_f)
    keep_out(ofull, wo_f)
    ones = jnp.ones((8, L), bf16)

    def project(first, size):
        total = product(qbias[:, pl.ds(first, size)], ones, TN)
        total = total + summed(qfull, n1, rows, first, size)
        qkv[pl.ds(first, size)] = total.astype(bf16)

    tiled(slots * CHANNELS, 384, project)
    keep_out(qkv, qkv_f)

    def head(s, carry):
        base = s * CHANNELS
        rows_of = lambda part: pl.ds(pl.multiple_of(base + part * HD, HD), HD)
        query, key, value = qkv[rows_of(0)], qkv[rows_of(1)], qkv[rows_of(2)]
        for first in range(0, L, QB):
            last = first + QB
            scores = masked_scores(key[:, :last], query[:, first:last], first)
            peak = jnp.max(scores, axis=0, keepdims=True)
            weights = jnp.exp(scores - peak)
            total = jnp.sum(weights, axis=0, keepdims=True)
            low = (weights * (1.0 / total)).astype(bf16)
            att[pl.ds(pl.multiple_of(s * HD, HD), HD), first:last] = product(
                value[:, :last], low, NN
            ).astype(bf16)
            logs[s, :, first:last] = peak + jnp.log(total)
        return carry

    half = slots * 5 // 7
    lax.fori_loop(0, half, head, 0)
    red_cot.arrive()
    spread_c = Spread(p, cot_own, cfull, width, ys, yr)
    spread_c.start()
    lax.fori_loop(half, slots, head, 0)
    take(late, 1)
    keep_out(att, att_f)
    keep_out(logs, logs_f)

    share = Share(p, part, core_in, side_out, side_in, share_s, share_r)
    fill_partial(part, ofull, att, cols, rows, width)
    share.start()
    take(late, 1)
    share.middle()
    spread_c.forward()
    take(late, 1)
    keep_out(cot_own, cot_own_f)
    spread_c.finish()
    keep_out(cfull, cot_f)
    take(late, 2)
    share.arrive()

    def first_pass(d, total):
        value = tok_own[d].astype(f32) + share.total(d) + vecs[d, :, 2:3]
        resid[d] = value
        return total

    lax.fori_loop(0, rows, first_pass, 0)
    keep_out(resid, resid_f)
    mean, scale = norm_scale(rows, width, lambda d: resid[d])

    def third(d, carry):
        value = (resid[d] - mean) * scale
        normed[d] = (value * vecs[d, :, 3:4] + vecs[d, :, 4:5]).astype(bf16)
        return carry

    lax.fori_loop(0, rows, third, 0)
    spread_n = Spread(p, normed, n2, width, ns, nr)
    spread_n.start()
    take(late, 3)
    spread_n.forward()
    spread_n.finish()
    keep_out(n2, n2_f)
    take(late, len(late) - 1)
    keep_out(ufull, wu_f)

    def up(first, size):
        value = summed(ufull, n2, rows, first, size) + bias_up[pl.ds(first, size)]
        cube = 0.7978845608 * (value + 0.044715 * value * value * value)
        bend = jnp.tanh(cube)
        hidden[pl.ds(first, size)] = (0.5 * value * (1.0 + bend)).astype(bf16)
        slope = 0.7978845608 * (1.0 + 3.0 * 0.044715 * value * value)
        gp[pl.ds(first, size)] = (
            0.5 * (1.0 + bend) + 0.5 * value * (1.0 - bend * bend) * slope
        ).astype(bf16)

    tiled(ffc, 256, up)
    take(late, 1)
    keep_out(dfull, wd_f)
    keep_out(hidden, hidden_f)

    def down(first, size):
        value = summed(dfull, cfull, rows, first, size)
        value = (value * gp[pl.ds(first, size)].astype(f32)).astype(bf16)
        gp[pl.ds(first, size)] = value

    tiled(ffc, 256, down)
    keep_out(gp, gp_f)
    for copies in swaps:
        for copy in copies:
            copy.wait_send()
    for copy in vec_copies:
        copy.wait_send()
    for ring in (ring_q, ring_o, ring_u, ring_d):
        ring.finish()
    red_tok.finish()
    red_cot.finish()
    share.finish()
    for copy in outs:
        copy.wait()


def forward(rows, cols, args, shapes):
    feats, width, slots, ffc = shapes
    dma = pltpu.SemaphoreType.DMA
    big = lambda n, t=bf16: pltpu.VMEM((rows, feats, n), t)
    qn, on = slots * CHANNELS, slots * HD
    ch, och = CHANNELS // cols, HD // cols
    outs = [
        ((rows, feats, qn), bf16),
        ((rows, feats, on), bf16),
        ((rows, feats, ffc), bf16),
        ((rows, feats, ffc), bf16),
        ((rows, feats, L), bf16),
        ((qn, L), bf16),
        ((on, L), bf16),
        ((slots, 1, L), f32),
        ((rows, feats, width), f32),
        ((rows, feats, L), bf16),
        ((ffc, L), bf16),
        ((ffc, L), bf16),
        ((rows, feats, L), bf16),
        ((rows, feats, width), bf16),
        ((rows, feats, width), bf16),
        ((rows, feats, 8), f32),
    ]
    scratch = [
        big(qn), big(on), big(ffc), big(ffc),
        pltpu.VMEM((feats, qn), bf16), pltpu.VMEM((feats, on), bf16),
        pltpu.VMEM((cols, feats, slots * ch), bf16),
        pltpu.VMEM((cols, feats, slots * och), bf16),
        pltpu.VMEM((cols, 8, slots * ch), bf16),
        pltpu.VMEM((8, qn), bf16),
        pltpu.VMEM((rows, 8, feats), f32),
        big(8, f32),
        big(L), big(L),
        pltpu.VMEM((qn, L), bf16), pltpu.VMEM((on, L), bf16), pltpu.VMEM((slots, 1, L), f32),
        big(width, f32), big(width), big(L),
        pltpu.VMEM((ffc, L), bf16), pltpu.VMEM((ffc, L), bf16),
        big(L), big(width), big(width),
    ]
    scratch += share_scratch(rows, cols, feats, width)
    scratch += [dma((2 * rows,))] * 8
    scratch += [dma((rows + 1,)), dma((rows,))] * 2
    scratch += spread_sems(cols) * 3
    scratch += [dma((3, cols)), dma((3, cols)), dma((rows,)), dma((rows,)), dma((24,))]
    return call(
        functools.partial(forward_kernel, rows, cols),
        outs,
        scratch,
        args,
        1,
        ANY,
        in_specs=[ANY] * 8 + [VMEM],
        out_specs=[ANY] * 16,
    )


def back_one_kernel(
    rows, cols, ready, cot, hidden, normed_mid, grad_pre, w_up, cot_own, resid, vec, w_down,
    grad_down, grad_up, grad_mid, branch, output, parts, branch_own, *scratch,
):
    p = Place(rows, cols)
    width = resid.shape[-1]
    half = grad_up.shape[1]
    share = Share(p, *scratch[:6])
    gather = Spread(p, branch_own, branch, width, *scratch[6:8])
    down = Reduce(p, cot, hidden, scratch[8:11], middle(hidden.shape[0], 0)).into(grad_down)
    up = Reduce(
        p, normed_mid, grad_pre.at[pl.ds(0, half)], scratch[11:14], middle(half, 0)
    ).into(grad_up)
    share_out = Share(p, scratch[0], scratch[14], scratch[2], *scratch[15:18])
    queue = steps(rows, down, up)
    at = lambda t: rows * t // 8
    meet(p.col_peers() + p.row_peers())
    ready("cot", "hidden", "normed_mid", "grad_pre")
    take(queue, 2)
    ready("w_up")
    fill_partial(
        share.part, w_up, grad_pre, cols, rows, width, lambda: take(queue, 1)
    )
    share.start()
    take(queue, 1)
    share.middle()
    ready("cot_own", "resid", "vec", "w_down")
    serve(queue, at(2))
    serve(queue, at(3))
    share.arrive()

    def store(d, value):
        total = cot_own[d].astype(f32) + value
        grad_mid[d] = total
        low = total.astype(bf16)
        branch_own[d] = low
        parts[d, :, 4:5] = jnp.sum(low.astype(f32), axis=1, keepdims=True)
        parts[d, :, 5:6] = jnp.sum(cot_own[d].astype(f32), axis=1, keepdims=True)

    parts[...] = jnp.zeros_like(parts)

    def put(d, gain, shift):
        parts[d, :, 2:3] = gain
        parts[d, :, 3:4] = shift

    norm_back(
        rows,
        width,
        lambda d: share.total(d),
        lambda d: resid[d],
        lambda d: vec[d, :, 3:4],
        store,
        put,
    )
    gather.start()
    share.finish()
    serve(queue, at(4))
    fill_partial(share_out.part, w_down, hidden, cols, rows, width)
    share_out.start()
    serve(queue, at(5))
    share_out.middle()
    gather.forward()
    serve(queue, rows)
    share_out.arrive()

    def result(d, carry):
        output[d] = (resid[d] + share_out.total(d) + vec[d, :, 5:6]).astype(bf16)
        return carry

    lax.fori_loop(0, rows, result, 0)
    down.finish()
    up.finish()
    share_out.finish()
    gather.finish()


def back_two_kernel(
    rows, cols, ready, output, normed_mid, grad_pre, w_out, branch, att, qkv, logs,
    vec, normed_in, w_qkv, own, grad_mid, parts,
    grad_up, wq_o, wo_o, bias_o, units_o, feat_o, res_out, res_tok,
    grad_tok, grad_qkv, grad_att, dkey, dval, lead_sum, rest_sum, out_sum, gq, go, gb,
    units, units_in, qkv_in, feat, feat_in, feat_sum, feat_cols,
    bs, br, ts, tr, es, er, fs, fr, us, ur, ws, wr, loc, *scratch,
):
    p = Place(rows, cols)
    width = own.shape[-1]
    slots = logs.shape[0]
    ch, och = CHANNELS // cols, HD // cols
    ffc = grad_pre.shape[0]
    half = grad_up.shape[1]
    qn = slots * CHANNELS
    share = Share(p, *scratch[:6])
    lead = slots * 4 // 7
    up = Reduce(
        p, normed_mid, grad_pre.at[pl.ds(ffc - half, half)], scratch[6:9], middle(half, 0)
    ).into(grad_up)
    out = Reduce(p, branch, att, scratch[9:12], middle(slots * HD, 1)).into(out_sum)
    wide = [
        Reduce(
            p,
            normed_in,
            grad_qkv.at[pl.ds(first * CHANNELS, count * CHANNELS)],
            scratch[i : i + 3],
            middle(count * CHANNELS, 0),
        ).into(total)
        for first, count, i, total in (
            (0, lead, 12, lead_sum),
            (lead, slots - lead, 15, rest_sum),
        )
    ]
    early = steps(rows, up, out)
    late = steps(rows, *wide)
    at = lambda t: rows * t // 8
    back_out = Back(p, output, res_out, (bs, br))
    back_tok = Back(p, grad_tok, res_tok, (ts, tr))
    sources = [(q, back_out.col) for q in range(rows)]
    targets = [home(p, q) for q in range(rows)]
    meet(sources + targets + all_col(p) + all_row(p))
    back_out.start()
    ready("normed_mid", "grad_pre", "branch", "att")
    serve(early, 0)
    ready("w_out", "qkv", "logs")
    for s in range(slots):
        total = product(w_out[0, :, s * HD : (s + 1) * HD], branch[0], TN)
        for d in range(1, rows):
            total = total + product(w_out[d, :, s * HD : (s + 1) * HD], branch[d], TN)
        grad_att[s * HD : (s + 1) * HD] = total.astype(bf16)

    def head(s, carry):
        base = pl.multiple_of(s * CHANNELS, 64)

        def store(row, first, last, value):
            grad_qkv[pl.ds(base + row, HD), first:last] = value.astype(bf16)

        attend_back(
            qkv[pl.ds(base, CHANNELS)],
            grad_att[pl.ds(pl.multiple_of(s * HD, 64), HD)],
            logs[s],
            store,
            dkey,
            dval,
        )
        return carry

    third = lead * 3 // 4
    lax.fori_loop(0, third, head, 0)
    serve(early, at(1))
    lax.fori_loop(third, lead, head, 0)
    ready("normed_in")
    take(late, 1)
    serve(early, at(2))
    most = lead + (slots - lead) // 2
    lax.fori_loop(lead, most, head, 0)
    serve(early, at(3))
    lax.fori_loop(most, slots, head, 0)
    serve(early, at(4))
    take(late, 1)
    ready("w_qkv", "own", "parts", "vec", "grad_mid")
    fill_partial(
        share.part, w_qkv, grad_qkv, cols, rows, width, lambda: serve(early, at(5))
    )
    share.start()
    serve(early, at(6))
    take(late, 1)
    share.middle()
    serve(early, rows)
    take(late, 1)
    ones = jnp.ones((8, L), bf16)
    units[:, :ffc] = product(ones, grad_pre[...], NT)[0:1]
    units[:, ffc:] = product(ones, grad_qkv[...], NT)[0:1]
    row_units = []
    for o, peer in enumerate(all_row(p)):
        row_units.append(remote(units, units_in.at[o + 1], us.at[o], ur.at[o], peer))
    for copy in row_units:
        copy.start()
    serve(late, at(2))
    serve(late, at(3))
    for j in range(cols):
        for s in range(slots):
            base = s * HD + j * och
            go[j, :, s * och : (s + 1) * och] = out_sum[:, base : base + och]
    swap_o = exchange_copies(p, go, wo_o, es.at[0], er.at[0])
    for copy in swap_o:
        copy.start()
    serve(late, at(4))
    share.arrive()

    def store_tokens(d, value):
        grad_tok[d] = (grad_mid[d] + value).astype(bf16)

    def put(d, gain, shift):
        parts[d, :, 0:1] = gain
        parts[d, :, 1:2] = shift

    norm_back(
        rows,
        width,
        lambda d: share.total(d),
        lambda d: own[d].astype(f32),
        lambda d: vec[d, :, 0:1],
        store_tokens,
        put,
    )
    eye = (
        lax.broadcasted_iota(jnp.int32, (8, 8), 0) == lax.broadcasted_iota(jnp.int32, (8, 8), 1)
    ).astype(f32)
    for d in range(rows):
        feat[d] = lax.dot_general(
            eye, parts[d], NT, precision=lax.Precision.HIGHEST, preferred_element_type=f32
        )
    feats = []
    for o in range(1, rows):
        to = lax.rem(p.r + o, rows)
        feats.append(remote(feat.at[to], feat_in.at[o], fs.at[o], fr.at[o], (to, p.c)))
    for copy in feats:
        copy.start()
    serve(late, at(5))
    serve(late, rows - 2)
    back_tok.start()
    total = units[...]
    for o, copy in enumerate(row_units):
        copy.wait_recv()
        total = total + units_in[o + 1]
    units_o[...] = total[:, :ffc]
    qkv_in[...] = total[:, ffc:]
    for j in range(cols):
        for s in range(slots):
            base = s * CHANNELS + j * ch
            gb[j, :, s * ch : (s + 1) * ch] = qkv_in[:, base : base + ch]
    swap_b = exchange_copies(p, gb, bias_o, es.at[1], er.at[1])
    for copy in swap_b:
        copy.start()
    total = feat[p.r]
    for o, copy in enumerate(feats):
        copy.wait_recv()
        total = total + feat_in[o + 1]
    feat_sum[...] = total
    sums = [
        remote(feat_sum, feat_cols.at[o + 1], ws.at[o], wr.at[o], peer)
        for o, peer in enumerate(all_col(p))
    ]
    for copy in sums:
        copy.start()
    serve(late, rows)
    for j in range(cols):
        for s in range(slots):
            base = (s if s < lead else s - lead) * CHANNELS + j * ch
            source = lead_sum if s < lead else rest_sum
            gq[j, :, s * ch : (s + 1) * ch] = source[:, base : base + ch]
    for ring in [up, out] + wide:
        ring.finish()
    swap_q = exchange_copies(p, gq, wq_o, es.at[2], er.at[2])
    for copy in swap_q:
        copy.start()
    keeps = [
        pltpu.make_async_copy(src.at[p.c], dst.at[p.c], loc.at[i])
        for i, (src, dst) in enumerate(((gq, wq_o), (go, wo_o), (gb, bias_o)))
    ]
    for copy in keeps:
        copy.start()
    for o, copy in enumerate(sums):
        copy.wait_recv()
        total = total + feat_cols[o + 1]
    feat_o[...] = total
    share.finish()
    back_out.finish()
    back_tok.finish()
    for copy in swap_o + swap_b + swap_q:
        copy.wait()
    for copy in keeps:
        copy.wait()
    for copy in row_units + feats + sums:
        copy.wait_send()


RAW = ("output",)
INPUTS = {
    back_one_kernel: (
        "cot", "hidden", "normed_mid", "grad_pre", "w_up", "cot_own", "resid", "vec", "w_down",
    ),
    back_two_kernel: (
        "output", "normed_mid", "grad_pre", "w_out", "branch", "att", "qkv", "logs",
        "vec", "normed_in", "w_qkv", "own", "grad_mid", "parts",
    ),
}


def call(kernel, outs, scratch, args, collective, spec=VMEM, in_specs=None, out_specs=None):
    return pl.pallas_call(
        kernel,
        out_shape=[jax.ShapeDtypeStruct(s, t) for s, t in outs],
        in_specs=[spec] * len(args) if in_specs is None else in_specs,
        out_specs=[spec] * len(outs) if out_specs is None else out_specs,
        scratch_shapes=scratch,
        compiler_params=pltpu.CompilerParams(
            collective_id=collective, has_side_effects=True, vmem_limit_bytes=LIMIT
        ),
    )(*args)


def staged(kernel, count, *refs):
    rows, cols, outs = count
    names = INPUTS[kernel]
    ins = len(names)
    rest = list(refs[ins + outs :])
    buffers = [refs[i] if name in RAW else rest.pop(0) for i, name in enumerate(names)]
    sem = rest.pop(0)
    copies = {
        name: pltpu.make_async_copy(refs[i], buffers[i], sem.at[i])
        for i, name in enumerate(names)
        if name not in RAW
    }
    for name in copies:
        copies[name].start()

    def ready(*names):
        for name in names:
            copies[name].wait()

    kernel(rows, cols, ready, *buffers, *refs[ins : ins + outs], *rest)


def call_staged(kernel, rows, cols, outs, scratch, args, collective):
    return call(
        functools.partial(staged, kernel, (rows, cols, len(outs))),
        outs,
        [
            pltpu.VMEM(arg.shape, arg.dtype)
            for name, arg in zip(INPUTS[kernel], args)
            if name not in RAW
        ]
        + [pltpu.SemaphoreType.DMA((len(args),))]
        + scratch,
        args,
        collective,
        in_specs=[ANY] * len(args),
    )


def one_hot(target, size):
    return (target[:, None] == jnp.arange(size, dtype=jnp.int32)[None, :]).astype(bf16)


def split_matrix(channels, slots, cols):
    source = jnp.arange(channels * H, dtype=jnp.int32)
    channel, head = source // H, source % H
    return one_hot(
        ((head % cols) * slots + head // cols) * channels + channel, cols * slots * channels
    )


def to_owners(weight, matrix, cols):
    moved = product(weight, matrix, NN).astype(bf16)
    return moved.reshape(moved.shape[0], cols, -1).transpose(1, 0, 2)


def from_owners(blocks, matrix):
    flat = blocks.transpose(1, 0, 2).reshape(blocks.shape[1], -1)
    return product(flat, matrix, NT)


def body(
    tokens, ln1_gain, ln1_shift, weight_qkv, bias_qkv, weight_out, bias_out, ln2_gain,
    ln2_shift, weight_up, bias_up, weight_down, bias_down, cotangent,
):
    rows, cols = lax.axis_size("row"), lax.axis_size("col")
    slots = (H + cols - 1) // cols
    ch, och = CHANNELS // cols, HD // cols
    feats = D // rows
    width = L // cols
    ffc = weight_up.shape[1]
    dma = pltpu.SemaphoreType.DMA

    qkv_split, out_split = split_matrix(ch, slots, cols), split_matrix(och, slots, cols)
    wq = to_owners(weight_qkv, qkv_split, cols)
    wo = to_owners(weight_out, out_split, cols)
    bias = jnp.pad(bias_qkv.reshape(ch, H), ((0, 0), (0, slots * cols - H)))
    bias = bias.reshape(ch, slots, cols).transpose(2, 1, 0).reshape(cols, 1, slots * ch)
    terms = []
    for _ in range(3):
        terms.append(lax.reduce_precision(bias, 8, 7))
        bias = bias - terms[-1]
    bias = jnp.concatenate(terms + [jnp.zeros_like(bias)] * 5, axis=1).astype(bf16)
    zero = jnp.zeros_like(ln1_gain)
    vec = jnp.stack(
        [ln1_gain, ln1_shift, bias_out, ln2_gain, ln2_shift, bias_down, zero, zero]
    )
    (
        w_qkv, w_out, w_up, w_down, normed_in, qkv, att, logs, resid, normed_mid, hidden,
        grad_pre, cot, tok_own, cot_own, vec,
    ) = forward(
        rows,
        cols,
        (tokens, cotangent, wq, wo, bias, vec, weight_up, weight_down, bias_up[:, None]),
        (feats, width, slots, ffc),
    )
    half = ffc // 2 // 128 * 128
    grad_weight_down, grad_up_one, grad_mid, branch, output, parts = call_staged(
        back_one_kernel,
        rows,
        cols,
        [
            ((feats, ffc), f32),
            ((feats, half), f32),
            ((rows, feats, width), f32),
            ((rows, feats, L), bf16),
            ((rows, feats, width), bf16),
            ((rows, feats, 8), f32),
        ],
        [pltpu.VMEM((rows, feats, width), bf16)]
        + share_scratch(rows, cols, feats, width)
        + spread_sems(cols)
        + reduce_scratch(rows, feats, ffc)
        + reduce_scratch(rows, feats, half)
        + [share_scratch(rows, cols, feats, width)[i] for i in (1, 3, 4, 5)],
        (cot, hidden, normed_mid, grad_pre, w_up, cot_own, resid, vec, w_down),
        3,
    )
    qn, on = slots * CHANNELS, slots * HD
    vm = pltpu.VMEM
    lead = slots * 4 // 7 * CHANNELS
    (
        grad_up_two, gq, go, gb, grad_bias_up, feat, res_out, res_tok
    ) = call_staged(
        back_two_kernel,
        rows,
        cols,
        [
            ((feats, ffc - half), f32),
            ((cols, feats, slots * ch), bf16),
            ((cols, feats, slots * och), bf16),
            ((cols, 1, slots * ch), f32),
            ((1, ffc), f32),
            ((8, feats), f32),
            ((feats, rows * width), bf16),
            ((feats, rows * width), bf16),
        ],
        [
            vm((rows, feats, width), bf16),
            vm((qn, L), bf16),
            vm((on, L), bf16),
            vm((HD, L), f32),
            vm((HD, L), f32),
            vm((feats, lead), bf16),
            vm((feats, qn - lead), bf16),
            vm((feats, on), bf16),
            vm((cols, feats, slots * ch), bf16),
            vm((cols, feats, slots * och), bf16),
            vm((cols, 1, slots * ch), f32),
            vm((1, ffc + qn), f32),
            vm((rows, 1, ffc + qn), f32),
            vm((1, qn), f32),
            vm((rows, 8, feats), f32),
            vm((rows, 8, feats), f32),
            vm((8, feats), f32),
            vm((cols, 8, feats), f32),
        ]
        + [dma((rows + 1,)), dma((rows,))] * 2
        + [dma((3, cols)), dma((3, cols))]
        + [dma((rows,))] * 4
        + [dma((cols,))] * 2
        + [dma((3,))]
        + share_scratch(rows, cols, feats, width)
        + reduce_scratch(rows, feats, ffc - half)
        + reduce_scratch(rows, feats, on)
        + reduce_scratch(rows, feats, lead)
        + reduce_scratch(rows, feats, qn - lead),
        (
            output, normed_mid, grad_pre, w_out, branch, att, qkv, logs,
            vec, normed_in, w_qkv, tok_own, grad_mid, parts,
        ),
        4,
    )
    grad_weight_up = jnp.concatenate([grad_up_one, grad_up_two], axis=1)
    grad_weight_qkv = from_owners(gq, qkv_split)
    grad_weight_out = from_owners(go, out_split)
    grad_bias_qkv = gb.reshape(cols, slots, ch).transpose(2, 1, 0)
    grad_bias_qkv = grad_bias_qkv.reshape(ch, slots * cols)[:, :H].reshape(-1)
    return (
        res_out,
        res_tok.astype(f32),
        feat[0],
        feat[1],
        grad_weight_qkv,
        grad_bias_qkv,
        grad_weight_out,
        feat[4],
        feat[2],
        feat[3],
        grad_weight_up,
        grad_bias_up[0],
        grad_weight_down,
        feat[5],
    )


def solution(mesh):
    both, row, col = P("row", "col"), P("row"), P("col")
    in_specs = (both, row, row, both, col, both, row, row, row, both, col, both, row, both)
    out_specs = (both, both, row, row, both, col, both, row, row, row, both, col, both, row)
    return jax.shard_map(body, mesh=mesh, in_specs=in_specs, out_specs=out_specs, check_vma=False)
```

```python
import functools

import jax
import jax.numpy as jnp
from jax import lax
from jax.experimental import pallas as pl
from jax.experimental.pallas import tpu as pltpu
from jax.sharding import PartitionSpec as P

D = 1600
H = 25
HD = 64
L = 1024
CHANNELS = 3 * HD
QB = 256

epsilon = 1e-05
excluded = -1e30

TN = (((0,), (0,)), ((), ()))
NN = (((1,), (0,)), ((), ()))
NT = (((1,), (1,)), ((), ()))
MESH = pl.DeviceIdType.MESH
ANY = pl.BlockSpec(memory_space=pl.ANY)
VMEM = pl.BlockSpec(memory_space=pltpu.VMEM)
LIMIT = 62 * 2**20
f32 = jnp.float32
bf16 = jnp.bfloat16


def product(left, right, dims):
    return lax.dot_general(left, right, dims, preferred_element_type=f32)


def remote(src, dst, send, recv, device):
    return pltpu.make_async_remote_copy(
        src_ref=src,
        dst_ref=dst,
        send_sem=send,
        recv_sem=recv,
        device_id=device,
        device_id_type=MESH,
    )


def meet(devices):
    sem = pltpu.get_barrier_semaphore()
    for device in devices:
        pl.semaphore_signal(sem, inc=1, device_id=device, device_id_type=MESH)
    pl.semaphore_wait(sem, len(devices))


def lanes(index, width):
    return pl.ds(pl.multiple_of(index * width, 128), width)


class Place:
    def __init__(self, rows, cols):
        self.R, self.C, self.A, self.X = rows, cols, rows // 2, cols // 2
        self.r, self.c = lax.axis_index("row"), lax.axis_index("col")
        self.a, self.b = self.r // 2, lax.rem(self.r, 2)
        self.x, self.k = self.c // 2, lax.rem(self.c, 2)
        self.core = (self.r, self.x * 2 + 1 - self.k)
        self.pair = (self.a * 2 + 1 - self.b, self.c)
        self.pos = jnp.where(self.b == 0, self.a, rows - 1 - self.a)
        self.around = [(self.row_at(1), self.c), (self.row_at(-1), self.c)]

    def row_at(self, o):
        at = lax.rem(self.pos + o + self.R, self.R)
        return jnp.where(at < self.A, at * 2, (self.R - 1 - at) * 2 + 1)

    def ahead(self, o):
        return lax.rem(self.a + o, self.A)

    def behind(self, o):
        return lax.rem(self.a - o + self.A, self.A)

    def line(self, o):
        return (self.ahead(o) * 2 + self.b, self.c)

    def x_ahead(self, o):
        return lax.rem(self.x + o, self.X)

    def x_behind(self, o):
        return lax.rem(self.x - o + self.X, self.X)

    def side(self, o):
        return (self.r, self.x_ahead(o) * 2 + self.k)

    def col_peers(self):
        return [self.core] + [self.side(o) for o in range(1, self.X)]

    def row_peers(self):
        return [self.pair] + [self.line(o) for o in range(1, self.A)]


class Spread:
    def __init__(self, p, own, full, width, send, recv):
        self.p, self.own, self.full, self.width = p, own, full, width
        self.send, self.recv = send, recv

    def part(self, block):
        return self.full.at[..., lanes(block, self.width)]

    def side_copy(self, o):
        return remote(
            self.own, self.part(self.p.c), self.send.at[o], self.recv.at[o], self.p.side(o)
        )

    def core_copy(self, o):
        p = self.p
        block = p.c if o == 0 else p.x_behind(o) * 2 + p.k
        src = self.own if o == 0 else self.part(block)
        i = p.X + o
        return remote(src, self.part(block), self.send.at[i], self.recv.at[i], p.core)

    def local(self):
        i = 2 * self.p.X
        return pltpu.make_async_copy(self.own, self.part(self.p.c), self.send.at[i])

    def start(self):
        for o in range(1, self.p.X):
            self.side_copy(o).start()
        self.core_copy(0).start()
        self.local().start()

    def forward(self):
        for o in range(1, self.p.X):
            self.side_copy(o).wait_recv()
            self.core_copy(o).start()

    def finish(self):
        for o in range(self.p.X):
            self.core_copy(o).wait()
        for o in range(1, self.p.X):
            self.side_copy(o).wait_send()
        self.local().wait()


def spread_sems(cols):
    return [pltpu.SemaphoreType.DMA((cols + 1,)), pltpu.SemaphoreType.DMA((cols + 1,))]


class Share:
    def __init__(self, p, part, core_in, side_out, side_in, send, recv):
        self.p, self.part, self.core_in = p, part, core_in
        self.side_out, self.side_in, self.send, self.recv = side_out, side_in, send, recv

    def core_copy(self, x):
        p = self.p
        return remote(
            self.part.at[x * 2 + 1 - p.k],
            self.core_in.at[x],
            self.send.at[x],
            self.recv.at[x],
            p.core,
        )

    def side_copy(self, o):
        p = self.p
        i = p.X + o - 1
        return remote(
            self.side_out.at[o - 1],
            self.side_in.at[o - 1],
            self.send.at[i],
            self.recv.at[i],
            p.side(o),
        )

    def start(self):
        for x in range(self.p.X):
            self.core_copy(x).start()

    def middle(self):
        p = self.p
        for x in range(p.X):
            self.core_copy(x).wait_recv()
        for o in range(1, p.X):
            x = p.x_ahead(o)

            def add(d, carry, x=x, o=o):
                total = self.part[x * 2 + p.k, d].astype(f32) + self.core_in[x, d].astype(f32)
                self.side_out[o - 1, d] = total.astype(bf16)
                return carry

            lax.fori_loop(0, p.R, add, 0)
            self.side_copy(o).start()

    def arrive(self):
        for o in range(1, self.p.X):
            self.side_copy(o).wait_recv()

    def total(self, d):
        p = self.p
        result = self.part[p.c, d].astype(f32) + self.core_in[p.x, d].astype(f32)
        for o in range(1, p.X):
            result = result + self.side_in[o - 1, d].astype(f32)
        return result

    def finish(self):
        for x in range(self.p.X):
            self.core_copy(x).wait_send()
        for o in range(1, self.p.X):
            self.side_copy(o).wait_send()


def share_scratch(rows, cols, feats, width):
    half = cols // 2
    return [
        pltpu.VMEM((cols, rows, feats, width), bf16),
        pltpu.VMEM((half, rows, feats, width), bf16),
        pltpu.VMEM((half - 1, rows, feats, width), bf16),
        pltpu.VMEM((half - 1, rows, feats, width), bf16),
        pltpu.SemaphoreType.DMA((cols - 1,)),
        pltpu.SemaphoreType.DMA((cols - 1,)),
    ]


def fill_partial(part, weight, act, cols, rows, width, between=lambda: None):
    def one(d, carry):
        for j in range(cols):
            part[j, d] = product(
                weight[d], act[:, j * width : (j + 1) * width], NN
            ).astype(bf16)
        return carry

    lax.fori_loop(0, rows // 2, one, 0)
    between()
    lax.fori_loop(rows // 2, rows, one, 0)


def middle(size, extra):
    return min((size // 256 + extra) * 128, (size - 1) // 128 * 128)


class Reduce:
    def __init__(self, p, left, right, scratch, cut):
        self.p, self.left, self.right = p, left, right
        self.slots, self.send, self.recv = scratch
        self.parts = (slice(0, cut), slice(cut, self.slots.shape[-1]))

    def copy(self, way, t):
        part = self.parts[way]
        i = way * self.p.R + t
        return remote(
            self.slots.at[t, :, part],
            self.slots.at[t + 1, :, part],
            self.send.at[i],
            self.recv.at[i],
            self.p.around[way],
        )

    def step(self, t):
        p = self.p
        for way in range(2):
            part = self.parts[way]
            row = p.row_at(-1 - t if way == 0 else 1 + t)
            value = product(self.left[row], self.right[part], NT)
            if t > 0:
                self.copy(way, t - 1).wait_recv()
                value = value + self.slots[t, :, part].astype(f32)
            if t < p.R - 1:
                self.slots[t, :, part] = value.astype(bf16)
                self.copy(way, t).start()
            else:
                self.out[:, part] = value.astype(self.out.dtype)

    def into(self, out):
        self.out = out
        return self

    def finish(self):
        for way in range(2):
            for t in range(self.p.R - 1):
                self.copy(way, t).wait_send()


def reduce_scratch(rows, feats, size):
    return [
        pltpu.VMEM((rows, feats, size), bf16),
        pltpu.SemaphoreType.DMA((2 * rows,)),
        pltpu.SemaphoreType.DMA((2 * rows,)),
    ]


def steps(rows, *rings):
    return [(ring, t) for t in range(rows) for ring in rings]


def serve(queue, t):
    while queue and queue[0][1] <= t:
        ring, at = queue.pop(0)
        ring.step(at)


def take(queue, count):
    for ring, at in queue[:count]:
        ring.step(at)
    del queue[:count]


def home(p, q):
    half = p.X // 2
    place = (q // p.C * half + p.x // 2) * 2 + p.k
    return (place * 2 + lax.rem(p.k + p.x, 2), lax.rem(q, p.C))


def own_block(p):
    half = p.X // 2
    k = lax.rem(p.a, 2)
    pair = p.a // 2
    x = lax.rem(pair, half) * 2 + lax.rem(p.b + k, 2)
    return x * 2 + k, pair // half * p.C + p.c


def equal(left, right):
    return jnp.logical_and(left[0] == right[0], left[1] == right[1])


def exchange_copies(p, src, dst, send, recv):
    out = []
    for o in range(1, p.C):
        to = lax.rem(p.c + o, p.C)
        out.append(remote(src.at[to], dst.at[p.c], send.at[o], recv.at[o], (p.r, to)))
    return out


def all_col(p):
    return [(p.r, lax.rem(p.c + o, p.C)) for o in range(1, p.C)]


def all_row(p):
    return [(lax.rem(p.r + o, p.R), p.c) for o in range(1, p.R)]


class Back:
    def __init__(self, p, src, dst, sems):
        self.p, self.src, self.dst = p, src, dst
        self.send, self.recv = sems
        self.width = src.shape[-1]
        self.col, self.place = own_block(p)

    def slot(self, q):
        return self.dst.at[:, lanes(q, self.width)]

    def outgoing(self, q):
        return remote(
            self.src.at[q],
            self.slot(self.place),
            self.send.at[q],
            self.recv.at[self.place],
            (q, self.col),
        )

    def staying(self, q):
        return pltpu.make_async_copy(
            self.src.at[q], self.slot(self.place), self.send.at[self.p.R]
        )

    def start(self):
        p = self.p
        for q in range(p.R):
            here = equal((q, self.col), (p.r, p.c))

            @pl.when(here)
            def _():
                self.staying(q).start()

            @pl.when(jnp.logical_not(here))
            def _():
                self.outgoing(q).start()

    def finish(self):
        p = self.p
        for q in range(p.R):
            source = home(p, q)
            here = equal(source, (p.r, p.c))

            @pl.when(here)
            def _():
                self.staying(0).wait()

            @pl.when(jnp.logical_not(here))
            def _():
                remote(
                    self.src.at[0], self.slot(q), self.send.at[0], self.recv.at[q], source
                ).wait_recv()

        for q in range(p.R):

            @pl.when(jnp.logical_not(equal((q, self.col), (p.r, p.c))))
            def _():
                self.outgoing(q).wait_send()


def masked_scores(key, query, first):
    scores = product(key, query, TN) * HD ** (-0.5)
    keys = lax.broadcasted_iota(jnp.int32, scores.shape, 0)
    queries = lax.broadcasted_iota(jnp.int32, scores.shape, 1) + first
    return jnp.where(keys <= queries, scores, excluded)


def attend_back(qkv, grad, logs, out, dkey, dval):
    query, key, value = qkv[:HD], qkv[HD : 2 * HD], qkv[2 * HD :]
    dkey[...] = jnp.zeros_like(dkey)
    dval[...] = jnp.zeros_like(dval)
    for first in range(0, L, QB):
        last = first + QB
        scores = masked_scores(key[:, :last], query[:, first:last], first)
        weights = jnp.exp(scores - logs[:, first:last])
        back = grad[:, first:last]
        dval[:, :last] += product(back, weights.astype(bf16), NT)
        grad_weights = product(value[:, :last], back, TN)
        inner = jnp.sum(weights * grad_weights, axis=0, keepdims=True)
        low = (weights * (grad_weights - inner)).astype(bf16)
        out(0, first, last, product(key[:, :last], low, NN) * HD ** (-0.5))
        dkey[:, :last] += product(query[:, first:last], low, NT)
    out(HD, 0, L, dkey[...] * HD ** (-0.5))
    out(2 * HD, 0, L, dval[...])


def norm_back(rows, width, incoming, values, gain, store, parts):
    zero = jnp.zeros((1, width), f32)

    def sums(d, total):
        return total + jnp.sum(values(d), axis=0, keepdims=True)

    mean = lax.fori_loop(0, rows, sums, zero) / D

    def squares(d, total):
        value = values(d) - mean
        return total + jnp.sum(value * value, axis=0, keepdims=True)

    scale = lax.rsqrt(lax.fori_loop(0, rows, squares, zero) / D + epsilon)

    def moments(d, totals):
        centred = (values(d) - mean) * scale
        back = incoming(d)
        parts(d, jnp.sum(back * centred, axis=1, keepdims=True), jnp.sum(back, axis=1, keepdims=True))
        scaled = back * gain(d)
        return (
            totals[0] + jnp.sum(scaled, axis=0, keepdims=True),
            totals[1] + jnp.sum(scaled * centred, axis=0, keepdims=True),
        )

    first, second = lax.fori_loop(0, rows, moments, (zero, zero))

    def last(d, carry):
        centred = (values(d) - mean) * scale
        scaled = incoming(d) * gain(d)
        store(d, scale * (scaled - first / D - centred * (second / D)))
        return carry

    lax.fori_loop(0, rows, last, 0)


class Ring:
    def __init__(self, p, own, full, sems, cut):
        self.p, self.own, self.full = p, own, full
        self.send, self.recv = sems
        self.parts = (slice(0, cut), slice(cut, own.shape[1]))

    def copy(self, way, t):
        p = self.p
        row = p.row_at(-t if way == 0 else t)
        part = self.parts[way]
        i = way * p.R + t
        return remote(
            self.own.at[:, part] if t == 0 else self.full.at[row, :, part],
            self.full.at[row, :, part],
            self.send.at[i],
            self.recv.at[i],
            p.around[way],
        )

    def local(self):
        return pltpu.make_async_copy(
            self.own, self.full.at[self.p.r], self.send.at[self.p.R - 1]
        )

    def step(self, t):
        if t == 0:
            self.local().start()
        for way in range(2):
            if t > 0:
                self.copy(way, t - 1).wait_recv()
            if t < self.p.R - 1:
                self.copy(way, t).start()
        if t == self.p.R - 1:
            self.local().wait()

    def finish(self):
        for way in range(2):
            for t in range(self.p.R - 1):
                self.copy(way, t).wait_send()


class Redistribute:
    def __init__(self, p, src, own, sems):
        self.p, self.src, self.own = p, src, own
        self.send, self.recv = sems
        self.width = own.shape[-1]
        self.col, _ = own_block(p)

    def outgoing(self, q, target):
        return remote(
            self.src.at[:, q * self.width : (q + 1) * self.width],
            self.own.at[self.p.r],
            self.send.at[q],
            self.recv.at[self.p.r],
            target,
        )

    def staying(self, q):
        return pltpu.make_async_copy(
            self.src.at[:, q * self.width : (q + 1) * self.width],
            self.own.at[self.p.r],
            self.send.at[self.p.R],
        )

    def start(self):
        p = self.p
        for q in range(p.R):
            target = home(p, q)
            here = equal(target, (p.r, p.c))

            @pl.when(here)
            def _():
                self.staying(q).start()

            @pl.when(jnp.logical_not(here))
            def _():
                self.outgoing(q, target).start()

    def arrive(self):
        p = self.p
        for q in range(p.R):
            here = equal((q, self.col), (p.r, p.c))

            @pl.when(here)
            def _():
                self.staying(0).wait()

            @pl.when(jnp.logical_not(here))
            def _():
                remote(
                    self.src.at[:, 0 : self.width],
                    self.own.at[q],
                    self.send.at[0],
                    self.recv.at[q],
                    (q, self.col),
                ).wait_recv()

    def finish(self):
        p = self.p
        for q in range(p.R):
            target = home(p, q)

            @pl.when(jnp.logical_not(equal(target, (p.r, p.c))))
            def _():
                self.outgoing(q, target).wait_send()


def norm_scale(rows, width, values):
    zero = jnp.zeros((1, width), f32)

    def sums(d, total):
        return total + jnp.sum(values(d), axis=0, keepdims=True)

    mean = lax.fori_loop(0, rows, sums, zero) / D

    def squares(d, total):
        value = values(d) - mean
        return total + jnp.sum(value * value, axis=0, keepdims=True)

    return mean, lax.rsqrt(lax.fori_loop(0, rows, squares, zero) / D + epsilon)


def tiled(size, tile, one):
    count = size // tile

    def step(i, carry):
        one(pl.multiple_of(i * tile, tile), tile)
        return carry

    lax.fori_loop(0, count, step, 0)
    if size % tile:
        one(count * tile, size % tile)


def summed(weight, act, rows, first, size):
    total = product(weight[0, :, pl.ds(first, size)], act[0], TN)
    for d in range(1, rows):
        total = total + product(weight[d, :, pl.ds(first, size)], act[d], TN)
    return total


def forward_kernel(
    rows, cols,
    tok, cot, wq, wo, bias, vec, wu, wd, bias_up,
    wq_f, wo_f, wu_f, wd_f, n1_f, qkv_f, att_f, logs_f, resid_f, n2_f, hidden_f, gp_f,
    cot_f, tok_own_f, cot_own_f, vec_f,
    qfull, ofull, ufull, dfull, qown, oown, qout, oout, qin, oin, bin_, qbias, vin, vecs,
    xfull, n1, qkv, att, logs, resid, normed, n2, hidden, gp, cfull, tok_own, cot_own,
    part, core_in, side_out, side_in, share_s, share_r,
    qs, qr, os_, or_, us, ur, ds0, dr0, ts, tr, cs, cr,
    xs, xr, ys, yr, ns, nr, es, er, vs, vr, loc,
):
    p = Place(rows, cols)
    width = tok_own.shape[-1]
    slots = logs.shape[0]
    ch = CHANNELS // cols
    ffc = hidden.shape[0]
    red_tok = Redistribute(p, tok, tok_own, (ts, tr))
    red_cot = Redistribute(p, cot, cot_own, (cs, cr))
    sources = [(q, red_tok.col) for q in range(rows)]
    targets = [home(p, q) for q in range(rows)]
    meet(sources + targets + all_col(p) + all_row(p))
    red_tok.start()
    for src, dst in ((wq, qout), (wo, oout)):
        block = dst.shape[-1]
        for j in range(cols):
            dst[j] = src[:, j * block : (j + 1) * block]
    groups = ((qout, qin), (oout, oin), (bias, bin_))
    swaps = []
    for i, (src, dst) in enumerate(groups):
        swaps.append(exchange_copies(p, src, dst, es.at[i], er.at[i]))
    for copies in swaps:
        for copy in copies:
            copy.start()
    keeps = [
        pltpu.make_async_copy(src.at[p.c], dst.at[p.c], loc.at[i])
        for i, (src, dst) in enumerate(groups)
    ]
    keeps.append(pltpu.make_async_copy(vec, vin.at[p.r], loc.at[3]))
    for copy in keeps:
        copy.start()
    vec_copies = [
        remote(vec, vin.at[p.r], vs.at[o], vr.at[o], peer)
        for o, peer in enumerate(all_row(p))
    ]
    for copy in vec_copies:
        copy.start()

    for copies, keep in zip(swaps, keeps):
        for copy in copies:
            copy.wait_recv()
        keep.wait()
    och = HD // cols
    for j in range(cols):
        for s in range(slots):
            base = s * CHANNELS + j * ch
            qown[:, base : base + ch] = qin[j, :, s * ch : (s + 1) * ch]
            qbias[:, base : base + ch] = bin_[j, :, s * ch : (s + 1) * ch]
            base = s * HD + j * och
            oown[:, base : base + och] = oin[j, :, s * och : (s + 1) * och]
    ring_q = Ring(p, qown, qfull, (qs, qr), middle(slots * CHANNELS, 0))
    ring_o = Ring(p, oown, ofull, (os_, or_), middle(slots * HD, 1))
    ring_u = Ring(p, wu, ufull, (us, ur), middle(ffc, 0))
    ring_d = Ring(p, wd, dfull, (ds0, dr0), middle(ffc, 1))
    early = steps(rows, ring_q, ring_o)
    late = steps(rows, ring_u, ring_d)
    serve(early, 0)
    red_tok.arrive()
    spread_x = Spread(p, tok_own, xfull, width, xs, xr)
    spread_x.start()
    serve(early, rows * 1 // 8)
    for copy in vec_copies:
        copy.wait_recv()
    keeps[3].wait()
    eye = (
        lax.broadcasted_iota(jnp.int32, (8, 8), 0) == lax.broadcasted_iota(jnp.int32, (8, 8), 1)
    ).astype(f32)
    for d in range(rows):
        vecs[d] = lax.dot_general(
            vin[d], eye, TN, precision=lax.Precision.HIGHEST, preferred_element_type=f32
        )
    serve(early, rows * 2 // 8)
    serve(early, rows * 3 // 8)
    spread_x.forward()
    spread_x.finish()
    outs = []

    def keep_out(src, dst):
        copy = pltpu.make_async_copy(src, dst, loc.at[4 + len(outs)])
        copy.start()
        outs.append(copy)

    keep_out(tok_own, tok_own_f)
    keep_out(vecs, vec_f)
    mean, scale = norm_scale(rows, L, lambda d: xfull[d].astype(f32))
    serve(early, rows * 4 // 8)

    def normal(d, carry):
        value = (xfull[d].astype(f32) - mean) * scale
        n1[d] = (value * vecs[d, :, 0:1] + vecs[d, :, 1:2]).astype(bf16)
        return carry

    lax.fori_loop(0, rows, normal, 0)
    keep_out(n1, n1_f)

    serve(early, rows - 2)
    red_cot.start()
    serve(late, 0)
    serve(early, rows)
    keep_out(qfull, wq_f)
    keep_out(ofull, wo_f)
    ones = jnp.ones((8, L), bf16)

    def project(first, size):
        total = product(qbias[:, pl.ds(first, size)], ones, TN)
        total = total + summed(qfull, n1, rows, first, size)
        qkv[pl.ds(first, size)] = total.astype(bf16)

    tiled(slots * CHANNELS, 384, project)
    keep_out(qkv, qkv_f)

    def head(s, carry):
        base = s * CHANNELS
        rows_of = lambda part: pl.ds(pl.multiple_of(base + part * HD, HD), HD)
        query, key, value = qkv[rows_of(0)], qkv[rows_of(1)], qkv[rows_of(2)]
        for first in range(0, L, QB):
            last = first + QB
            scores = masked_scores(key[:, :last], query[:, first:last], first)
            peak = jnp.max(scores, axis=0, keepdims=True)
            weights = jnp.exp(scores - peak)
            total = jnp.sum(weights, axis=0, keepdims=True)
            low = (weights * (1.0 / total)).astype(bf16)
            att[pl.ds(pl.multiple_of(s * HD, HD), HD), first:last] = product(
                value[:, :last], low, NN
            ).astype(bf16)
            logs[s, :, first:last] = peak + jnp.log(total)
        return carry

    half = slots * 5 // 7
    lax.fori_loop(0, half, head, 0)
    red_cot.arrive()
    spread_c = Spread(p, cot_own, cfull, width, ys, yr)
    spread_c.start()
    lax.fori_loop(half, slots, head, 0)
    take(late, 1)
    keep_out(att, att_f)
    keep_out(logs, logs_f)

    share = Share(p, part, core_in, side_out, side_in, share_s, share_r)
    fill_partial(part, ofull, att, cols, rows, width)
    share.start()
    take(late, 1)
    share.middle()
    spread_c.forward()
    take(late, 1)
    keep_out(cot_own, cot_own_f)
    spread_c.finish()
    keep_out(cfull, cot_f)
    take(late, 2)
    share.arrive()

    def first_pass(d, total):
        value = tok_own[d].astype(f32) + share.total(d) + vecs[d, :, 2:3]
        resid[d] = value
        return total

    lax.fori_loop(0, rows, first_pass, 0)
    keep_out(resid, resid_f)
    mean, scale = norm_scale(rows, width, lambda d: resid[d])

    def third(d, carry):
        value = (resid[d] - mean) * scale
        normed[d] = (value * vecs[d, :, 3:4] + vecs[d, :, 4:5]).astype(bf16)
        return carry

    lax.fori_loop(0, rows, third, 0)
    spread_n = Spread(p, normed, n2, width, ns, nr)
    spread_n.start()
    take(late, 3)
    spread_n.forward()
    spread_n.finish()
    keep_out(n2, n2_f)
    take(late, len(late) - 1)
    keep_out(ufull, wu_f)

    def up(first, size):
        value = summed(ufull, n2, rows, first, size) + bias_up[pl.ds(first, size)]
        cube = 0.7978845608 * (value + 0.044715 * value * value * value)
        bend = jnp.tanh(cube)
        hidden[pl.ds(first, size)] = (0.5 * value * (1.0 + bend)).astype(bf16)
        slope = 0.7978845608 * (1.0 + 3.0 * 0.044715 * value * value)
        gp[pl.ds(first, size)] = (
            0.5 * (1.0 + bend) + 0.5 * value * (1.0 - bend * bend) * slope
        ).astype(bf16)

    tiled(ffc, 256, up)
    take(late, 1)
    keep_out(dfull, wd_f)
    keep_out(hidden, hidden_f)

    def down(first, size):
        value = summed(dfull, cfull, rows, first, size)
        value = (value * gp[pl.ds(first, size)].astype(f32)).astype(bf16)
        gp[pl.ds(first, size)] = value

    tiled(ffc, 256, down)
    keep_out(gp, gp_f)
    for copies in swaps:
        for copy in copies:
            copy.wait_send()
    for copy in vec_copies:
        copy.wait_send()
    for ring in (ring_q, ring_o, ring_u, ring_d):
        ring.finish()
    red_tok.finish()
    red_cot.finish()
    share.finish()
    for copy in outs:
        copy.wait()


def forward(rows, cols, args, shapes):
    feats, width, slots, ffc = shapes
    dma = pltpu.SemaphoreType.DMA
    big = lambda n, t=bf16: pltpu.VMEM((rows, feats, n), t)
    qn, on = slots * CHANNELS, slots * HD
    ch, och = CHANNELS // cols, HD // cols
    outs = [
        ((rows, feats, qn), bf16),
        ((rows, feats, on), bf16),
        ((rows, feats, ffc), bf16),
        ((rows, feats, ffc), bf16),
        ((rows, feats, L), bf16),
        ((qn, L), bf16),
        ((on, L), bf16),
        ((slots, 1, L), f32),
        ((rows, feats, width), f32),
        ((rows, feats, L), bf16),
        ((ffc, L), bf16),
        ((ffc, L), bf16),
        ((rows, feats, L), bf16),
        ((rows, feats, width), bf16),
        ((rows, feats, width), bf16),
        ((rows, feats, 8), f32),
    ]
    scratch = [
        big(qn), big(on), big(ffc), big(ffc),
        pltpu.VMEM((feats, qn), bf16), pltpu.VMEM((feats, on), bf16),
        pltpu.VMEM((cols, feats, slots * ch), bf16),
        pltpu.VMEM((cols, feats, slots * och), bf16),
        pltpu.VMEM((cols, feats, slots * ch), bf16),
        pltpu.VMEM((cols, feats, slots * och), bf16),
        pltpu.VMEM((cols, 8, slots * ch), bf16),
        pltpu.VMEM((8, qn), bf16),
        pltpu.VMEM((rows, 8, feats), f32),
        big(8, f32),
        big(L), big(L),
        pltpu.VMEM((qn, L), bf16), pltpu.VMEM((on, L), bf16), pltpu.VMEM((slots, 1, L), f32),
        big(width, f32), big(width), big(L),
        pltpu.VMEM((ffc, L), bf16), pltpu.VMEM((ffc, L), bf16),
        big(L), big(width), big(width),
    ]
    scratch += share_scratch(rows, cols, feats, width)
    scratch += [dma((2 * rows,))] * 8
    scratch += [dma((rows + 1,)), dma((rows,))] * 2
    scratch += spread_sems(cols) * 3
    scratch += [dma((3, cols)), dma((3, cols)), dma((rows,)), dma((rows,)), dma((24,))]
    return call(
        functools.partial(forward_kernel, rows, cols),
        outs,
        scratch,
        args,
        1,
        ANY,
        in_specs=[ANY, ANY, VMEM, VMEM, ANY, ANY, ANY, ANY, VMEM],
        out_specs=[ANY] * 16,
    )


def back_one_kernel(
    rows, cols, ready, cot, hidden, normed_mid, grad_pre, w_up, cot_own, resid, vec, w_down,
    grad_down, grad_up, grad_mid, branch, output, parts, branch_own, *scratch,
):
    p = Place(rows, cols)
    width = resid.shape[-1]
    half = grad_up.shape[1]
    share = Share(p, *scratch[:6])
    gather = Spread(p, branch_own, branch, width, *scratch[6:8])
    down = Reduce(p, cot, hidden, scratch[8:11], middle(hidden.shape[0], 0)).into(grad_down)
    up = Reduce(
        p, normed_mid, grad_pre.at[pl.ds(0, half)], scratch[11:14], middle(half, 0)
    ).into(grad_up)
    share_out = Share(p, scratch[0], scratch[14], scratch[2], *scratch[15:18])
    queue = steps(rows, down, up)
    at = lambda t: rows * t // 8
    meet(p.col_peers() + p.row_peers())
    ready("cot", "hidden", "normed_mid", "grad_pre")
    take(queue, 2)
    ready("w_up")
    fill_partial(
        share.part, w_up, grad_pre, cols, rows, width, lambda: take(queue, 1)
    )
    share.start()
    take(queue, 1)
    share.middle()
    ready("cot_own", "resid", "vec", "w_down")
    serve(queue, at(2))
    serve(queue, at(3))
    share.arrive()

    def store(d, value):
        total = cot_own[d].astype(f32) + value
        grad_mid[d] = total
        low = total.astype(bf16)
        branch_own[d] = low
        parts[d, :, 4:5] = jnp.sum(low.astype(f32), axis=1, keepdims=True)
        parts[d, :, 5:6] = jnp.sum(cot_own[d].astype(f32), axis=1, keepdims=True)

    parts[...] = jnp.zeros_like(parts)

    def put(d, gain, shift):
        parts[d, :, 2:3] = gain
        parts[d, :, 3:4] = shift

    norm_back(
        rows,
        width,
        lambda d: share.total(d),
        lambda d: resid[d],
        lambda d: vec[d, :, 3:4],
        store,
        put,
    )
    gather.start()
    share.finish()
    serve(queue, at(4))
    fill_partial(share_out.part, w_down, hidden, cols, rows, width)
    share_out.start()
    serve(queue, at(5))
    share_out.middle()
    gather.forward()
    serve(queue, rows)
    share_out.arrive()

    def result(d, carry):
        output[d] = (resid[d] + share_out.total(d) + vec[d, :, 5:6]).astype(bf16)
        return carry

    lax.fori_loop(0, rows, result, 0)
    down.finish()
    up.finish()
    share_out.finish()
    gather.finish()


def back_two_kernel(
    rows, cols, ready, output, up_one, normed_mid, grad_pre, w_out, branch, att, qkv, logs,
    vec, normed_in, w_qkv, own, grad_mid, parts,
    grad_up_all, wq_o, wo_o, bias_o, units_o, feat_o, res_out, res_f32,
    grad_up, res_tok, grad_tok, grad_qkv, grad_att, dkey, dval, lead_sum, rest_sum, out_sum, gq, go, gb,
    units, units_in, qkv_in, feat, feat_in, feat_sum, feat_cols,
    bs, br, ts, tr, es, er, fs, fr, us, ur, ws, wr, loc, *scratch,
):
    p = Place(rows, cols)
    width = own.shape[-1]
    slots = logs.shape[0]
    ch, och = CHANNELS // cols, HD // cols
    ffc = grad_pre.shape[0]
    half = grad_up.shape[1]
    qn = slots * CHANNELS
    share = Share(p, *scratch[:6])
    lead = slots * 4 // 7
    up = Reduce(
        p, normed_mid, grad_pre.at[pl.ds(ffc - half, half)], scratch[6:9], middle(half, 0)
    ).into(grad_up)
    out = Reduce(p, branch, att, scratch[9:12], middle(slots * HD, 1)).into(out_sum)
    wide = [
        Reduce(
            p,
            normed_in,
            grad_qkv.at[pl.ds(first * CHANNELS, count * CHANNELS)],
            scratch[i : i + 3],
            middle(count * CHANNELS, 0),
        ).into(total)
        for first, count, i, total in (
            (0, lead, 12, lead_sum),
            (lead, slots - lead, 15, rest_sum),
        )
    ]
    early = steps(rows, up, out)
    late = steps(rows, *wide)
    at = lambda t: rows * t // 8
    back_out = Back(p, output, res_out, (bs, br))
    back_tok = Back(p, grad_tok, res_tok, (ts, tr))
    sources = [(q, back_out.col) for q in range(rows)]
    targets = [home(p, q) for q in range(rows)]
    meet(sources + targets + all_col(p) + all_row(p))
    back_out.start()
    one_copy = pltpu.make_async_copy(
        up_one, grad_up_all.at[:, : ffc - half], loc.at[3]
    )
    one_copy.start()
    ready("normed_mid", "grad_pre", "branch", "att")
    serve(early, 0)
    ready("w_out", "qkv", "logs")
    for s in range(slots):
        total = product(w_out[0, :, s * HD : (s + 1) * HD], branch[0], TN)
        for d in range(1, rows):
            total = total + product(w_out[d, :, s * HD : (s + 1) * HD], branch[d], TN)
        grad_att[s * HD : (s + 1) * HD] = total.astype(bf16)

    def head(s, carry):
        base = pl.multiple_of(s * CHANNELS, 64)

        def store(row, first, last, value):
            grad_qkv[pl.ds(base + row, HD), first:last] = value.astype(bf16)

        attend_back(
            qkv[pl.ds(base, CHANNELS)],
            grad_att[pl.ds(pl.multiple_of(s * HD, 64), HD)],
            logs[s],
            store,
            dkey,
            dval,
        )
        return carry

    third = lead * 3 // 4
    lax.fori_loop(0, third, head, 0)
    serve(early, at(1))
    lax.fori_loop(third, lead, head, 0)
    ready("normed_in")
    take(late, 1)
    serve(early, at(2))
    most = lead + (slots - lead) // 2
    lax.fori_loop(lead, most, head, 0)
    serve(early, at(3))
    lax.fori_loop(most, slots, head, 0)
    serve(early, at(4))
    take(late, 1)
    ready("w_qkv", "own", "parts", "vec", "grad_mid")
    fill_partial(
        share.part, w_qkv, grad_qkv, cols, rows, width, lambda: serve(early, at(5))
    )
    share.start()
    serve(early, at(6))
    take(late, 1)
    share.middle()
    serve(early, rows)
    take(late, 1)
    ones = jnp.ones((8, L), bf16)
    units[:, :ffc] = product(ones, grad_pre[...], NT)[0:1]
    units[:, ffc:] = product(ones, grad_qkv[...], NT)[0:1]
    row_units = []
    for o, peer in enumerate(all_row(p)):
        row_units.append(remote(units, units_in.at[o + 1], us.at[o], ur.at[o], peer))
    for copy in row_units:
        copy.start()
    serve(late, at(2))
    serve(late, at(3))
    for j in range(cols):
        for s in range(slots):
            base = s * HD + j * och
            go[j, :, s * och : (s + 1) * och] = out_sum[:, base : base + och]
    swap_o = exchange_copies(p, go, wo_o, es.at[0], er.at[0])
    for copy in swap_o:
        copy.start()
    serve(late, at(4))
    share.arrive()

    def store_tokens(d, value):
        grad_tok[d] = (grad_mid[d] + value).astype(bf16)

    def put(d, gain, shift):
        parts[d, :, 0:1] = gain
        parts[d, :, 1:2] = shift

    norm_back(
        rows,
        width,
        lambda d: share.total(d),
        lambda d: own[d].astype(f32),
        lambda d: vec[d, :, 0:1],
        store_tokens,
        put,
    )
    eye = (
        lax.broadcasted_iota(jnp.int32, (8, 8), 0) == lax.broadcasted_iota(jnp.int32, (8, 8), 1)
    ).astype(f32)
    for d in range(rows):
        feat[d] = lax.dot_general(
            eye, parts[d], NT, precision=lax.Precision.HIGHEST, preferred_element_type=f32
        )
    feats = []
    for o in range(1, rows):
        to = lax.rem(p.r + o, rows)
        feats.append(remote(feat.at[to], feat_in.at[o], fs.at[o], fr.at[o], (to, p.c)))
    for copy in feats:
        copy.start()
    serve(late, at(5))
    serve(late, rows - 2)
    back_tok.start()
    total = units[...]
    for o, copy in enumerate(row_units):
        copy.wait_recv()
        total = total + units_in[o + 1]
    units_o[...] = total[:, :ffc]
    qkv_in[...] = total[:, ffc:]
    for j in range(cols):
        for s in range(slots):
            base = s * CHANNELS + j * ch
            gb[j, :, s * ch : (s + 1) * ch] = qkv_in[:, base : base + ch]
    swap_b = exchange_copies(p, gb, bias_o, es.at[1], er.at[1])
    for copy in swap_b:
        copy.start()
    total = feat[p.r]
    for o, copy in enumerate(feats):
        copy.wait_recv()
        total = total + feat_in[o + 1]
    feat_sum[...] = total
    sums = [
        remote(feat_sum, feat_cols.at[o + 1], ws.at[o], wr.at[o], peer)
        for o, peer in enumerate(all_col(p))
    ]
    for copy in sums:
        copy.start()
    serve(late, rows)
    for j in range(cols):
        for s in range(slots):
            base = (s if s < lead else s - lead) * CHANNELS + j * ch
            source = lead_sum if s < lead else rest_sum
            gq[j, :, s * ch : (s + 1) * ch] = source[:, base : base + ch]
    for ring in [up, out] + wide:
        ring.finish()
    swap_q = exchange_copies(p, gq, wq_o, es.at[2], er.at[2])
    for copy in swap_q:
        copy.start()
    two_copy = pltpu.make_async_copy(
        grad_up, grad_up_all.at[:, ffc - half :], loc.at[4]
    )
    two_copy.start()
    keeps = [
        pltpu.make_async_copy(src.at[p.c], dst.at[p.c], loc.at[i])
        for i, (src, dst) in enumerate(((gq, wq_o), (go, wo_o), (gb, bias_o)))
    ]
    for copy in keeps:
        copy.start()
    for o, copy in enumerate(sums):
        copy.wait_recv()
        total = total + feat_cols[o + 1]
    feat_o[...] = total
    share.finish()
    back_out.finish()
    back_tok.finish()
    res_f32[...] = res_tok[...].astype(f32)
    one_copy.wait()
    two_copy.wait()
    for copy in swap_o + swap_b + swap_q:
        copy.wait()
    for copy in keeps:
        copy.wait()
    for copy in row_units + feats + sums:
        copy.wait_send()


RAW = ("output", "up_one")
INPUTS = {
    back_one_kernel: (
        "cot", "hidden", "normed_mid", "grad_pre", "w_up", "cot_own", "resid", "vec", "w_down",
    ),
    back_two_kernel: (
        "output", "up_one", "normed_mid", "grad_pre", "w_out", "branch", "att", "qkv", "logs",
        "vec", "normed_in", "w_qkv", "own", "grad_mid", "parts",
    ),
}


def call(kernel, outs, scratch, args, collective, spec=VMEM, in_specs=None, out_specs=None):
    return pl.pallas_call(
        kernel,
        out_shape=[jax.ShapeDtypeStruct(s, t) for s, t in outs],
        in_specs=[spec] * len(args) if in_specs is None else in_specs,
        out_specs=[spec] * len(outs) if out_specs is None else out_specs,
        scratch_shapes=scratch,
        compiler_params=pltpu.CompilerParams(
            collective_id=collective, has_side_effects=True, vmem_limit_bytes=LIMIT
        ),
    )(*args)


def staged(kernel, count, *refs):
    rows, cols, outs = count
    names = INPUTS[kernel]
    ins = len(names)
    rest = list(refs[ins + outs :])
    buffers = [refs[i] if name in RAW else rest.pop(0) for i, name in enumerate(names)]
    sem = rest.pop(0)
    copies = {
        name: pltpu.make_async_copy(refs[i], buffers[i], sem.at[i])
        for i, name in enumerate(names)
        if name not in RAW
    }
    for name in copies:
        copies[name].start()

    def ready(*names):
        for name in names:
            copies[name].wait()

    kernel(rows, cols, ready, *buffers, *refs[ins : ins + outs], *rest)


def call_staged(kernel, rows, cols, outs, scratch, args, collective, out_specs=None):
    return call(
        functools.partial(staged, kernel, (rows, cols, len(outs))),
        outs,
        [
            pltpu.VMEM(arg.shape, arg.dtype)
            for name, arg in zip(INPUTS[kernel], args)
            if name not in RAW
        ]
        + [pltpu.SemaphoreType.DMA((len(args),))]
        + scratch,
        args,
        collective,
        in_specs=[ANY] * len(args),
        out_specs=out_specs,
    )


def one_hot(target, size):
    return (target[:, None] == jnp.arange(size, dtype=jnp.int32)[None, :]).astype(bf16)


def split_matrix(channels, slots, cols):
    source = jnp.arange(channels * H, dtype=jnp.int32)
    channel, head = source // H, source % H
    return one_hot(
        ((head % cols) * slots + head // cols) * channels + channel, cols * slots * channels
    )


def to_owners(weight, matrix):
    return product(weight, matrix, NN).astype(bf16)


def from_owners(blocks, matrix):
    flat = blocks.transpose(1, 0, 2).reshape(blocks.shape[1], -1)
    return product(flat, matrix, NT)


def body(
    tokens, ln1_gain, ln1_shift, weight_qkv, bias_qkv, weight_out, bias_out, ln2_gain,
    ln2_shift, weight_up, bias_up, weight_down, bias_down, cotangent,
):
    rows, cols = lax.axis_size("row"), lax.axis_size("col")
    slots = (H + cols - 1) // cols
    ch, och = CHANNELS // cols, HD // cols
    feats = D // rows
    width = L // cols
    ffc = weight_up.shape[1]
    dma = pltpu.SemaphoreType.DMA

    qkv_split, out_split = split_matrix(ch, slots, cols), split_matrix(och, slots, cols)
    wq = to_owners(weight_qkv, qkv_split)
    wo = to_owners(weight_out, out_split)
    bias = jnp.pad(bias_qkv.reshape(ch, H), ((0, 0), (0, slots * cols - H)))
    bias = bias.reshape(ch, slots, cols).transpose(2, 1, 0).reshape(cols, 1, slots * ch)
    terms = []
    for _ in range(3):
        terms.append(lax.reduce_precision(bias, 8, 7))
        bias = bias - terms[-1]
    bias = jnp.concatenate(terms + [jnp.zeros_like(bias)] * 5, axis=1).astype(bf16)
    zero = jnp.zeros_like(ln1_gain)
    vec = jnp.stack(
        [ln1_gain, ln1_shift, bias_out, ln2_gain, ln2_shift, bias_down, zero, zero]
    )
    (
        w_qkv, w_out, w_up, w_down, normed_in, qkv, att, logs, resid, normed_mid, hidden,
        grad_pre, cot, tok_own, cot_own, vec,
    ) = forward(
        rows,
        cols,
        (tokens, cotangent, wq, wo, bias, vec, weight_up, weight_down, bias_up[:, None]),
        (feats, width, slots, ffc),
    )
    half = ffc // 2 // 128 * 128
    grad_weight_down, grad_up_one, grad_mid, branch, output, parts = call_staged(
        back_one_kernel,
        rows,
        cols,
        [
            ((feats, ffc), f32),
            ((feats, half), f32),
            ((rows, feats, width), f32),
            ((rows, feats, L), bf16),
            ((rows, feats, width), bf16),
            ((rows, feats, 8), f32),
        ],
        [pltpu.VMEM((rows, feats, width), bf16)]
        + share_scratch(rows, cols, feats, width)
        + spread_sems(cols)
        + reduce_scratch(rows, feats, ffc)
        + reduce_scratch(rows, feats, half)
        + [share_scratch(rows, cols, feats, width)[i] for i in (1, 3, 4, 5)],
        (cot, hidden, normed_mid, grad_pre, w_up, cot_own, resid, vec, w_down),
        3,
    )
    qn, on = slots * CHANNELS, slots * HD
    vm = pltpu.VMEM
    lead = slots * 4 // 7 * CHANNELS
    (
        grad_weight_up, gq, go, gb, grad_bias_up, feat, res_out, res_tok
    ) = call_staged(
        back_two_kernel,
        rows,
        cols,
        [
            ((feats, ffc), f32),
            ((cols, feats, slots * ch), bf16),
            ((cols, feats, slots * och), bf16),
            ((cols, 1, slots * ch), f32),
            ((1, ffc), f32),
            ((8, feats), f32),
            ((feats, rows * width), bf16),
            ((feats, rows * width), f32),
        ],
        [
            vm((feats, ffc - half), f32),
            vm((feats, rows * width), bf16),
            vm((rows, feats, width), bf16),
            vm((qn, L), bf16),
            vm((on, L), bf16),
            vm((HD, L), f32),
            vm((HD, L), f32),
            vm((feats, lead), bf16),
            vm((feats, qn - lead), bf16),
            vm((feats, on), bf16),
            vm((cols, feats, slots * ch), bf16),
            vm((cols, feats, slots * och), bf16),
            vm((cols, 1, slots * ch), f32),
            vm((1, ffc + qn), f32),
            vm((rows, 1, ffc + qn), f32),
            vm((1, qn), f32),
            vm((rows, 8, feats), f32),
            vm((rows, 8, feats), f32),
            vm((8, feats), f32),
            vm((cols, 8, feats), f32),
        ]
        + [dma((rows + 1,)), dma((rows,))] * 2
        + [dma((3, cols)), dma((3, cols))]
        + [dma((rows,))] * 4
        + [dma((cols,))] * 2
        + [dma((5,))]
        + share_scratch(rows, cols, feats, width)
        + reduce_scratch(rows, feats, ffc - half)
        + reduce_scratch(rows, feats, on)
        + reduce_scratch(rows, feats, lead)
        + reduce_scratch(rows, feats, qn - lead),
        (
            output, grad_up_one, normed_mid, grad_pre, w_out, branch, att, qkv, logs,
            vec, normed_in, w_qkv, tok_own, grad_mid, parts,
        ),
        4,
        [ANY] + [VMEM] * 5 + [ANY, VMEM],
    )
    grad_weight_qkv = from_owners(gq, qkv_split)
    grad_weight_out = from_owners(go, out_split)
    grad_bias_qkv = gb.reshape(cols, slots, ch).transpose(2, 1, 0)
    grad_bias_qkv = grad_bias_qkv.reshape(ch, slots * cols)[:, :H].reshape(-1)
    return (
        res_out,
        res_tok,
        feat[0],
        feat[1],
        grad_weight_qkv,
        grad_bias_qkv,
        grad_weight_out,
        feat[4],
        feat[2],
        feat[3],
        grad_weight_up,
        grad_bias_up[0],
        grad_weight_down,
        feat[5],
    )


def solution(mesh):
    both, row, col = P("row", "col"), P("row"), P("col")
    in_specs = (both, row, row, both, col, both, row, row, row, both, col, both, row, both)
    out_specs = (both, both, row, row, both, col, both, row, row, row, both, col, both, row)
    return jax.shard_map(body, mesh=mesh, in_specs=in_specs, out_specs=out_specs, check_vma=False)
```

```python
import functools

import jax
import jax.numpy as jnp
from jax import lax
from jax.experimental import pallas as pl
from jax.experimental.pallas import tpu as pltpu
from jax.sharding import PartitionSpec as P

D = 1600
H = 25
HD = 64
L = 1024
CHANNELS = 3 * HD
QB = 256

epsilon = 1e-05
excluded = -1e30

TN = (((0,), (0,)), ((), ()))
NN = (((1,), (0,)), ((), ()))
NT = (((1,), (1,)), ((), ()))
MESH = pl.DeviceIdType.MESH
ANY = pl.BlockSpec(memory_space=pl.ANY)
VMEM = pl.BlockSpec(memory_space=pltpu.VMEM)
LIMIT = 62 * 2**20
f32 = jnp.float32
bf16 = jnp.bfloat16


def product(left, right, dims):
    return lax.dot_general(left, right, dims, preferred_element_type=f32)


def remote(src, dst, send, recv, device):
    return pltpu.make_async_remote_copy(
        src_ref=src,
        dst_ref=dst,
        send_sem=send,
        recv_sem=recv,
        device_id=device,
        device_id_type=MESH,
    )


def meet(devices):
    sem = pltpu.get_barrier_semaphore()
    for device in devices:
        pl.semaphore_signal(sem, inc=1, device_id=device, device_id_type=MESH)
    pl.semaphore_wait(sem, len(devices))


def lanes(index, width):
    return pl.ds(pl.multiple_of(index * width, 128), width)


class Place:
    def __init__(self, rows, cols):
        self.R, self.C, self.A, self.X = rows, cols, rows // 2, cols // 2
        self.r, self.c = lax.axis_index("row"), lax.axis_index("col")
        self.a, self.b = self.r // 2, lax.rem(self.r, 2)
        self.x, self.k = self.c // 2, lax.rem(self.c, 2)
        self.core = (self.r, self.x * 2 + 1 - self.k)
        self.pair = (self.a * 2 + 1 - self.b, self.c)
        self.pos = jnp.where(self.b == 0, self.a, rows - 1 - self.a)
        self.around = [(self.row_at(1), self.c), (self.row_at(-1), self.c)]

    def row_at(self, o):
        at = lax.rem(self.pos + o + self.R, self.R)
        return jnp.where(at < self.A, at * 2, (self.R - 1 - at) * 2 + 1)

    def ahead(self, o):
        return lax.rem(self.a + o, self.A)

    def behind(self, o):
        return lax.rem(self.a - o + self.A, self.A)

    def line(self, o):
        return (self.ahead(o) * 2 + self.b, self.c)

    def x_ahead(self, o):
        return lax.rem(self.x + o, self.X)

    def x_behind(self, o):
        return lax.rem(self.x - o + self.X, self.X)

    def side(self, o):
        return (self.r, self.x_ahead(o) * 2 + self.k)

    def col_peers(self):
        return [self.core] + [self.side(o) for o in range(1, self.X)]

    def row_peers(self):
        return [self.pair] + [self.line(o) for o in range(1, self.A)]


class Spread:
    def __init__(self, p, own, full, width, send, recv):
        self.p, self.own, self.full, self.width = p, own, full, width
        self.send, self.recv = send, recv

    def part(self, block):
        return self.full.at[..., lanes(block, self.width)]

    def side_copy(self, o):
        return remote(
            self.own, self.part(self.p.c), self.send.at[o], self.recv.at[o], self.p.side(o)
        )

    def core_copy(self, o):
        p = self.p
        block = p.c if o == 0 else p.x_behind(o) * 2 + p.k
        src = self.own if o == 0 else self.part(block)
        i = p.X + o
        return remote(src, self.part(block), self.send.at[i], self.recv.at[i], p.core)

    def local(self):
        i = 2 * self.p.X
        return pltpu.make_async_copy(self.own, self.part(self.p.c), self.send.at[i])

    def start(self):
        for o in range(1, self.p.X):
            self.side_copy(o).start()
        self.core_copy(0).start()
        self.local().start()

    def forward(self):
        for o in range(1, self.p.X):
            self.side_copy(o).wait_recv()
            self.core_copy(o).start()

    def finish(self):
        for o in range(self.p.X):
            self.core_copy(o).wait()
        for o in range(1, self.p.X):
            self.side_copy(o).wait_send()
        self.local().wait()


def spread_sems(cols):
    return [pltpu.SemaphoreType.DMA((cols + 1,)), pltpu.SemaphoreType.DMA((cols + 1,))]


class Share:
    def __init__(self, p, part, core_in, side_out, side_in, send, recv):
        self.p, self.part, self.core_in = p, part, core_in
        self.side_out, self.side_in, self.send, self.recv = side_out, side_in, send, recv

    def core_copy(self, x):
        p = self.p
        return remote(
            self.part.at[x * 2 + 1 - p.k],
            self.core_in.at[x],
            self.send.at[x],
            self.recv.at[x],
            p.core,
        )

    def side_copy(self, o):
        p = self.p
        i = p.X + o - 1
        return remote(
            self.side_out.at[o - 1],
            self.side_in.at[o - 1],
            self.send.at[i],
            self.recv.at[i],
            p.side(o),
        )

    def start(self):
        for x in range(self.p.X):
            self.core_copy(x).start()

    def middle(self):
        p = self.p
        for x in range(p.X):
            self.core_copy(x).wait_recv()
        for o in range(1, p.X):
            x = p.x_ahead(o)

            def add(d, carry, x=x, o=o):
                total = self.part[x * 2 + p.k, d].astype(f32) + self.core_in[x, d].astype(f32)
                self.side_out[o - 1, d] = total.astype(bf16)
                return carry

            lax.fori_loop(0, p.R, add, 0)
            self.side_copy(o).start()

    def arrive(self):
        for o in range(1, self.p.X):
            self.side_copy(o).wait_recv()

    def total(self, d):
        p = self.p
        result = self.part[p.c, d].astype(f32) + self.core_in[p.x, d].astype(f32)
        for o in range(1, p.X):
            result = result + self.side_in[o - 1, d].astype(f32)
        return result

    def finish(self):
        for x in range(self.p.X):
            self.core_copy(x).wait_send()
        for o in range(1, self.p.X):
            self.side_copy(o).wait_send()


def share_scratch(rows, cols, feats, width):
    half = cols // 2
    return [
        pltpu.VMEM((cols, rows, feats, width), bf16),
        pltpu.VMEM((half, rows, feats, width), bf16),
        pltpu.VMEM((half - 1, rows, feats, width), bf16),
        pltpu.VMEM((half - 1, rows, feats, width), bf16),
        pltpu.SemaphoreType.DMA((cols - 1,)),
        pltpu.SemaphoreType.DMA((cols - 1,)),
    ]


def fill_partial(part, weight, act, cols, rows, width, between=lambda: None):
    def one(d, carry):
        for j in range(cols):
            part[j, d] = product(
                weight[d], act[:, j * width : (j + 1) * width], NN
            ).astype(bf16)
        return carry

    lax.fori_loop(0, rows // 2, one, 0)
    between()
    lax.fori_loop(rows // 2, rows, one, 0)


def middle(size, extra):
    return min(max((size // 256 + extra) * 128, 128), (size - 1) // 128 * 128)


def where(condition, act):
    if condition is None:
        act()
    else:
        pl.when(condition)(act)


class Reduce:
    def __init__(self, p, left, right, scratch, cut, only=None):
        self.p, self.left, self.right, self.only = p, left, right, only
        self.slots, self.send, self.recv = scratch
        self.parts = (slice(0, cut), slice(cut, self.slots.shape[-1]))

    def copy(self, way, t):
        part = self.parts[way]
        i = way * self.p.R + t
        return remote(
            self.slots.at[t, :, part],
            self.slots.at[t + 1, :, part],
            self.send.at[i],
            self.recv.at[i],
            self.p.around[way],
        )

    def step(self, t):
        where(self.only, lambda: self.run(t))

    def run(self, t):
        p = self.p
        for way in range(2):
            part = self.parts[way]
            row = p.row_at(-1 - t if way == 0 else 1 + t)
            value = product(self.left[row], self.right[part], NT)
            if t > 0:
                self.copy(way, t - 1).wait_recv()
                value = value + self.slots[t, :, part].astype(f32)
            if t < p.R - 1:
                self.slots[t, :, part] = value.astype(bf16)
                self.copy(way, t).start()
            else:
                self.out[:, part] = value.astype(self.out.dtype)

    def into(self, out):
        self.out = out
        return self

    def finish(self):
        where(self.only, self.end)

    def end(self):
        for way in range(2):
            for t in range(self.p.R - 1):
                self.copy(way, t).wait_send()


def reduce_scratch(rows, feats, size):
    return [
        pltpu.VMEM((rows, feats, size), bf16),
        pltpu.SemaphoreType.DMA((2 * rows,)),
        pltpu.SemaphoreType.DMA((2 * rows,)),
    ]


def steps(rows, *rings):
    return [(ring, t) for t in range(rows) for ring in rings]


def serve(queue, t):
    while queue and queue[0][1] <= t:
        ring, at = queue.pop(0)
        ring.step(at)


def take(queue, count):
    for ring, at in queue[:count]:
        ring.step(at)
    del queue[:count]


def home(p, q):
    half = p.X // 2
    place = (q // p.C * half + p.x // 2) * 2 + p.k
    return (place * 2 + lax.rem(p.k + p.x, 2), lax.rem(q, p.C))


def own_block(p):
    half = p.X // 2
    k = lax.rem(p.a, 2)
    pair = p.a // 2
    x = lax.rem(pair, half) * 2 + lax.rem(p.b + k, 2)
    return x * 2 + k, pair // half * p.C + p.c


def equal(left, right):
    return jnp.logical_and(left[0] == right[0], left[1] == right[1])


def exchange_copies(p, src, dst, send, recv):
    out = []
    for o in range(1, p.C):
        to = lax.rem(p.c + o, p.C)
        out.append(remote(src.at[to], dst.at[p.c], send.at[o], recv.at[o], (p.r, to)))
    return out


def all_col(p):
    return [(p.r, lax.rem(p.c + o, p.C)) for o in range(1, p.C)]


def all_row(p):
    return [(lax.rem(p.r + o, p.R), p.c) for o in range(1, p.R)]


class Back:
    def __init__(self, p, src, dst, sems):
        self.p, self.src, self.dst = p, src, dst
        self.send, self.recv = sems
        self.width = src.shape[-1]
        self.col, self.place = own_block(p)

    def slot(self, q):
        return self.dst.at[:, lanes(q, self.width)]

    def outgoing(self, q):
        return remote(
            self.src.at[q],
            self.slot(self.place),
            self.send.at[q],
            self.recv.at[self.place],
            (q, self.col),
        )

    def staying(self, q):
        return pltpu.make_async_copy(
            self.src.at[q], self.slot(self.place), self.send.at[self.p.R]
        )

    def start(self):
        p = self.p
        for q in range(p.R):
            here = equal((q, self.col), (p.r, p.c))

            @pl.when(here)
            def _():
                self.staying(q).start()

            @pl.when(jnp.logical_not(here))
            def _():
                self.outgoing(q).start()

    def finish(self):
        p = self.p
        for q in range(p.R):
            source = home(p, q)
            here = equal(source, (p.r, p.c))

            @pl.when(here)
            def _():
                self.staying(0).wait()

            @pl.when(jnp.logical_not(here))
            def _():
                remote(
                    self.src.at[0], self.slot(q), self.send.at[0], self.recv.at[q], source
                ).wait_recv()

        for q in range(p.R):

            @pl.when(jnp.logical_not(equal((q, self.col), (p.r, p.c))))
            def _():
                self.outgoing(q).wait_send()


def masked_scores(key, query, first):
    scores = product(key, query, TN) * HD ** (-0.5)
    keys = lax.broadcasted_iota(jnp.int32, scores.shape, 0)
    queries = lax.broadcasted_iota(jnp.int32, scores.shape, 1) + first
    return jnp.where(keys <= queries, scores, excluded)


def attend_back(qkv, grad, logs, out, dkey, dval):
    query, key, value = qkv[:HD], qkv[HD : 2 * HD], qkv[2 * HD :]
    dkey[...] = jnp.zeros_like(dkey)
    dval[...] = jnp.zeros_like(dval)
    for first in range(0, L, QB):
        last = first + QB
        scores = masked_scores(key[:, :last], query[:, first:last], first)
        weights = jnp.exp(scores - logs[:, first:last])
        back = grad[:, first:last]
        dval[:, :last] += product(back, weights.astype(bf16), NT)
        grad_weights = product(value[:, :last], back, TN)
        inner = jnp.sum(weights * grad_weights, axis=0, keepdims=True)
        low = (weights * (grad_weights - inner)).astype(bf16)
        out(0, first, last, product(key[:, :last], low, NN) * HD ** (-0.5))
        dkey[:, :last] += product(query[:, first:last], low, NT)
    out(HD, 0, L, dkey[...] * HD ** (-0.5))
    out(2 * HD, 0, L, dval[...])


def norm_back(rows, width, incoming, values, gain, store, parts):
    zero = jnp.zeros((1, width), f32)

    def sums(d, total):
        return total + jnp.sum(values(d), axis=0, keepdims=True)

    mean = lax.fori_loop(0, rows, sums, zero) / D

    def squares(d, total):
        value = values(d) - mean
        return total + jnp.sum(value * value, axis=0, keepdims=True)

    scale = lax.rsqrt(lax.fori_loop(0, rows, squares, zero) / D + epsilon)

    def moments(d, totals):
        centred = (values(d) - mean) * scale
        back = incoming(d)
        parts(d, jnp.sum(back * centred, axis=1, keepdims=True), jnp.sum(back, axis=1, keepdims=True))
        scaled = back * gain(d)
        return (
            totals[0] + jnp.sum(scaled, axis=0, keepdims=True),
            totals[1] + jnp.sum(scaled * centred, axis=0, keepdims=True),
        )

    first, second = lax.fori_loop(0, rows, moments, (zero, zero))

    def last(d, carry):
        centred = (values(d) - mean) * scale
        scaled = incoming(d) * gain(d)
        store(d, scale * (scaled - first / D - centred * (second / D)))
        return carry

    lax.fori_loop(0, rows, last, 0)


class Ring:
    def __init__(self, p, own, full, sems, cut, first=0, last=None, only=None):
        self.p, self.own, self.full, self.only = p, own, full, only
        self.send, self.recv = sems
        last = own.shape[1] if last is None else last
        self.span = slice(first, last)
        self.parts = (slice(first, cut), slice(cut, last))

    def copy(self, way, t):
        p = self.p
        row = p.row_at(-t if way == 0 else t)
        part = self.parts[way]
        i = way * p.R + t
        return remote(
            self.own.at[:, part] if t == 0 else self.full.at[row, :, part],
            self.full.at[row, :, part],
            self.send.at[i],
            self.recv.at[i],
            p.around[way],
        )

    def local(self):
        return pltpu.make_async_copy(
            self.own.at[:, self.span],
            self.full.at[self.p.r, :, self.span],
            self.send.at[self.p.R - 1],
        )

    def step(self, t):
        where(self.only, lambda: self.run(t))

    def run(self, t):
        if t == 0:
            self.local().start()
        for way in range(2):
            if t > 0:
                self.copy(way, t - 1).wait_recv()
            if t < self.p.R - 1:
                self.copy(way, t).start()
        if t == self.p.R - 1:
            self.local().wait()

    def finish(self):
        where(self.only, self.end)

    def end(self):
        for way in range(2):
            for t in range(self.p.R - 1):
                self.copy(way, t).wait_send()


class Redistribute:
    def __init__(self, p, src, own, sems):
        self.p, self.src, self.own = p, src, own
        self.send, self.recv = sems
        self.width = own.shape[-1]
        self.col, _ = own_block(p)

    def outgoing(self, q, target):
        return remote(
            self.src.at[:, q * self.width : (q + 1) * self.width],
            self.own.at[self.p.r],
            self.send.at[q],
            self.recv.at[self.p.r],
            target,
        )

    def staying(self, q):
        return pltpu.make_async_copy(
            self.src.at[:, q * self.width : (q + 1) * self.width],
            self.own.at[self.p.r],
            self.send.at[self.p.R],
        )

    def start(self):
        p = self.p
        for q in range(p.R):
            target = home(p, q)
            here = equal(target, (p.r, p.c))

            @pl.when(here)
            def _():
                self.staying(q).start()

            @pl.when(jnp.logical_not(here))
            def _():
                self.outgoing(q, target).start()

    def arrive(self):
        p = self.p
        for q in range(p.R):
            here = equal((q, self.col), (p.r, p.c))

            @pl.when(here)
            def _():
                self.staying(0).wait()

            @pl.when(jnp.logical_not(here))
            def _():
                remote(
                    self.src.at[:, 0 : self.width],
                    self.own.at[q],
                    self.send.at[0],
                    self.recv.at[q],
                    (q, self.col),
                ).wait_recv()

    def finish(self):
        p = self.p
        for q in range(p.R):
            target = home(p, q)

            @pl.when(jnp.logical_not(equal(target, (p.r, p.c))))
            def _():
                self.outgoing(q, target).wait_send()


def norm_scale(rows, width, values):
    zero = jnp.zeros((1, width), f32)

    def sums(d, total):
        return total + jnp.sum(values(d), axis=0, keepdims=True)

    mean = lax.fori_loop(0, rows, sums, zero) / D

    def squares(d, total):
        value = values(d) - mean
        return total + jnp.sum(value * value, axis=0, keepdims=True)

    return mean, lax.rsqrt(lax.fori_loop(0, rows, squares, zero) / D + epsilon)


def tiled(size, tile, one):
    count = size // tile

    def step(i, carry):
        one(pl.multiple_of(i * tile, tile), tile)
        return carry

    lax.fori_loop(0, count, step, 0)
    if size % tile:
        one(count * tile, size % tile)


def summed(weight, act, rows, first, size):
    total = product(weight[0, :, pl.ds(first, size)], act[0], TN)
    for d in range(1, rows):
        total = total + product(weight[d, :, pl.ds(first, size)], act[d], TN)
    return total


def forward_kernel(
    rows, cols,
    tok, cot, wq, wo, bias, vec, wu, wd, bias_up,
    wq_f, wo_f, wu_f, wd_f, n1_f, qkv_f, att_f, logs_f, resid_f, n2_f, hidden_f, gp_f,
    cot_f, tok_own_f, cot_own_f, vec_f,
    qfull, ofull, ufull, dfull, qown, oown, qout, oout, qin, oin, bin_, qbias, vin, vecs,
    xfull, n1, qkv, att, logs, resid, normed, n2, hidden, gp, cfull, tok_own, cot_own,
    part, core_in, side_out, side_in, share_s, share_r,
    qs, qr, zs, zr, os_, or_, us, ur, ds0, dr0, ts, tr, cs, cr,
    xs, xr, ys, yr, ns, nr, es, er, vs, vr, loc,
):
    p = Place(rows, cols)
    width = tok_own.shape[-1]
    slots = logs.shape[0]
    ch = CHANNELS // cols
    ffc = hidden.shape[0]
    red_tok = Redistribute(p, tok, tok_own, (ts, tr))
    red_cot = Redistribute(p, cot, cot_own, (cs, cr))
    sources = [(q, red_tok.col) for q in range(rows)]
    targets = [home(p, q) for q in range(rows)]
    meet(sources + targets + all_col(p) + all_row(p))
    red_tok.start()
    for src, dst in ((wq, qout), (wo, oout)):
        block = dst.shape[-1]
        for j in range(cols):
            dst[j] = src[:, j * block : (j + 1) * block]
    groups = ((qout, qin), (oout, oin), (bias, bin_))
    swaps = []
    for i, (src, dst) in enumerate(groups):
        swaps.append(exchange_copies(p, src, dst, es.at[i], er.at[i]))
    for copies in swaps:
        for copy in copies:
            copy.start()
    keeps = [
        pltpu.make_async_copy(src.at[p.c], dst.at[p.c], loc.at[i])
        for i, (src, dst) in enumerate(groups)
    ]
    keeps.append(pltpu.make_async_copy(vec, vin.at[p.r], loc.at[3]))
    for copy in keeps:
        copy.start()
    vec_copies = [
        remote(vec, vin.at[p.r], vs.at[o], vr.at[o], peer)
        for o, peer in enumerate(all_row(p))
    ]
    for copy in vec_copies:
        copy.start()

    for copies, keep in zip(swaps, keeps):
        for copy in copies:
            copy.wait_recv()
        keep.wait()
    och = HD // cols
    for j in range(cols):
        for s in range(slots):
            base = s * CHANNELS + j * ch
            qown[:, base : base + ch] = qin[j, :, s * ch : (s + 1) * ch]
            qbias[:, base : base + ch] = bin_[j, :, s * ch : (s + 1) * ch]
            base = s * HD + j * och
            oown[:, base : base + och] = oin[j, :, s * och : (s + 1) * och]
    tail = (slots - 1) * CHANNELS // 128 * 128
    filled = (slots - 1) * cols + p.c < H
    exact = tail == (slots - 1) * CHANNELS
    ring_q = Ring(p, qown, qfull, (qs, qr), middle(tail, 0), 0, tail)
    ring_t = Ring(
        p, qown, qfull, (zs, zr), tail + 128, tail, None, filled if exact else None
    )
    if exact:

        @pl.when(jnp.logical_not(filled))
        def _():
            qfull[:, :, tail:] = jnp.zeros((rows, qfull.shape[1], CHANNELS), bf16)

    ring_o = Ring(p, oown, ofull, (os_, or_), middle(slots * HD, 1))
    ring_u = Ring(p, wu, ufull, (us, ur), middle(ffc, 0))
    ring_d = Ring(p, wd, dfull, (ds0, dr0), middle(ffc, 1))
    early = steps(rows, ring_q, ring_t, ring_o)
    late = steps(rows, ring_u, ring_d)
    serve(early, 0)
    red_tok.arrive()
    spread_x = Spread(p, tok_own, xfull, width, xs, xr)
    spread_x.start()
    serve(early, rows * 1 // 8)
    for copy in vec_copies:
        copy.wait_recv()
    keeps[3].wait()
    eye = (
        lax.broadcasted_iota(jnp.int32, (8, 8), 0) == lax.broadcasted_iota(jnp.int32, (8, 8), 1)
    ).astype(f32)
    for d in range(rows):
        vecs[d] = lax.dot_general(
            vin[d], eye, TN, precision=lax.Precision.HIGHEST, preferred_element_type=f32
        )
    serve(early, rows * 2 // 8)
    serve(early, rows * 3 // 8)
    spread_x.forward()
    spread_x.finish()
    outs = []

    def keep_out(src, dst):
        copy = pltpu.make_async_copy(src, dst, loc.at[4 + len(outs)])
        copy.start()
        outs.append(copy)

    keep_out(tok_own, tok_own_f)
    keep_out(vecs, vec_f)
    mean, scale = norm_scale(rows, L, lambda d: xfull[d].astype(f32))
    serve(early, rows * 4 // 8)

    def normal(d, carry):
        value = (xfull[d].astype(f32) - mean) * scale
        n1[d] = (value * vecs[d, :, 0:1] + vecs[d, :, 1:2]).astype(bf16)
        return carry

    lax.fori_loop(0, rows, normal, 0)
    keep_out(n1, n1_f)

    serve(early, rows - 2)
    red_cot.start()
    serve(late, 0)
    serve(early, rows)
    keep_out(qfull, wq_f)
    keep_out(ofull, wo_f)
    ones = jnp.ones((8, L), bf16)

    def project(first, size):
        total = product(qbias[:, pl.ds(first, size)], ones, TN)
        total = total + summed(qfull, n1, rows, first, size)
        qkv[pl.ds(first, size)] = total.astype(bf16)

    tiled(slots * CHANNELS, 384, project)
    keep_out(qkv, qkv_f)

    def head(s, carry):
        base = s * CHANNELS
        rows_of = lambda part: pl.ds(pl.multiple_of(base + part * HD, HD), HD)
        query, key, value = qkv[rows_of(0)], qkv[rows_of(1)], qkv[rows_of(2)]
        for first in range(0, L, QB):
            last = first + QB
            scores = masked_scores(key[:, :last], query[:, first:last], first)
            peak = jnp.max(scores, axis=0, keepdims=True)
            weights = jnp.exp(scores - peak)
            total = jnp.sum(weights, axis=0, keepdims=True)
            low = (weights * (1.0 / total)).astype(bf16)
            att[pl.ds(pl.multiple_of(s * HD, HD), HD), first:last] = product(
                value[:, :last], low, NN
            ).astype(bf16)
            logs[s, :, first:last] = peak + jnp.log(total)
        return carry

    half = slots * 5 // 7
    lax.fori_loop(0, half, head, 0)
    red_cot.arrive()
    spread_c = Spread(p, cot_own, cfull, width, ys, yr)
    spread_c.start()
    lax.fori_loop(half, slots, head, 0)
    take(late, 1)
    keep_out(att, att_f)
    keep_out(logs, logs_f)

    share = Share(p, part, core_in, side_out, side_in, share_s, share_r)
    fill_partial(part, ofull, att, cols, rows, width)
    share.start()
    take(late, 1)
    share.middle()
    spread_c.forward()
    take(late, 1)
    keep_out(cot_own, cot_own_f)
    spread_c.finish()
    keep_out(cfull, cot_f)
    take(late, 2)
    share.arrive()

    def first_pass(d, total):
        value = tok_own[d].astype(f32) + share.total(d) + vecs[d, :, 2:3]
        resid[d] = value
        return total

    lax.fori_loop(0, rows, first_pass, 0)
    keep_out(resid, resid_f)
    mean, scale = norm_scale(rows, width, lambda d: resid[d])

    def third(d, carry):
        value = (resid[d] - mean) * scale
        normed[d] = (value * vecs[d, :, 3:4] + vecs[d, :, 4:5]).astype(bf16)
        return carry

    lax.fori_loop(0, rows, third, 0)
    spread_n = Spread(p, normed, n2, width, ns, nr)
    spread_n.start()
    take(late, 3)
    spread_n.forward()
    spread_n.finish()
    keep_out(n2, n2_f)
    take(late, len(late) - 1)
    keep_out(ufull, wu_f)

    def up(first, size):
        value = summed(ufull, n2, rows, first, size) + bias_up[pl.ds(first, size)]
        cube = 0.7978845608 * (value + 0.044715 * value * value * value)
        bend = jnp.tanh(cube)
        hidden[pl.ds(first, size)] = (0.5 * value * (1.0 + bend)).astype(bf16)
        slope = 0.7978845608 * (1.0 + 3.0 * 0.044715 * value * value)
        gp[pl.ds(first, size)] = (
            0.5 * (1.0 + bend) + 0.5 * value * (1.0 - bend * bend) * slope
        ).astype(bf16)

    tiled(ffc, 256, up)
    take(late, 1)
    keep_out(dfull, wd_f)
    keep_out(hidden, hidden_f)

    def down(first, size):
        value = summed(dfull, cfull, rows, first, size)
        value = (value * gp[pl.ds(first, size)].astype(f32)).astype(bf16)
        gp[pl.ds(first, size)] = value

    tiled(ffc, 256, down)
    keep_out(gp, gp_f)
    for copies in swaps:
        for copy in copies:
            copy.wait_send()
    for copy in vec_copies:
        copy.wait_send()
    for ring in (ring_q, ring_t, ring_o, ring_u, ring_d):
        ring.finish()
    red_tok.finish()
    red_cot.finish()
    share.finish()
    for copy in outs:
        copy.wait()


def forward(rows, cols, args, shapes):
    feats, width, slots, ffc = shapes
    dma = pltpu.SemaphoreType.DMA
    big = lambda n, t=bf16: pltpu.VMEM((rows, feats, n), t)
    qn, on = slots * CHANNELS, slots * HD
    ch, och = CHANNELS // cols, HD // cols
    outs = [
        ((rows, feats, qn), bf16),
        ((rows, feats, on), bf16),
        ((rows, feats, ffc), bf16),
        ((rows, feats, ffc), bf16),
        ((rows, feats, L), bf16),
        ((qn, L), bf16),
        ((on, L), bf16),
        ((slots, 1, L), f32),
        ((rows, feats, width), f32),
        ((rows, feats, L), bf16),
        ((ffc, L), bf16),
        ((ffc, L), bf16),
        ((rows, feats, L), bf16),
        ((rows, feats, width), bf16),
        ((rows, feats, width), bf16),
        ((rows, feats, 8), f32),
    ]
    scratch = [
        big(qn), big(on), big(ffc), big(ffc),
        pltpu.VMEM((feats, qn), bf16), pltpu.VMEM((feats, on), bf16),
        pltpu.VMEM((cols, feats, slots * ch), bf16),
        pltpu.VMEM((cols, feats, slots * och), bf16),
        pltpu.VMEM((cols, feats, slots * ch), bf16),
        pltpu.VMEM((cols, feats, slots * och), bf16),
        pltpu.VMEM((cols, 8, slots * ch), bf16),
        pltpu.VMEM((8, qn), bf16),
        pltpu.VMEM((rows, 8, feats), f32),
        big(8, f32),
        big(L), big(L),
        pltpu.VMEM((qn, L), bf16), pltpu.VMEM((on, L), bf16), pltpu.VMEM((slots, 1, L), f32),
        big(width, f32), big(width), big(L),
        pltpu.VMEM((ffc, L), bf16), pltpu.VMEM((ffc, L), bf16),
        big(L), big(width), big(width),
    ]
    scratch += share_scratch(rows, cols, feats, width)
    scratch += [dma((2 * rows,))] * 10
    scratch += [dma((rows + 1,)), dma((rows,))] * 2
    scratch += spread_sems(cols) * 3
    scratch += [dma((3, cols)), dma((3, cols)), dma((rows,)), dma((rows,)), dma((24,))]
    return call(
        functools.partial(forward_kernel, rows, cols),
        outs,
        scratch,
        args,
        1,
        ANY,
        in_specs=[ANY, ANY, VMEM, VMEM, ANY, ANY, ANY, ANY, VMEM],
        out_specs=[ANY] * 16,
    )


def back_one_kernel(
    rows, cols, ready, cot, hidden, normed_mid, grad_pre, w_up, cot_own, resid, vec, w_down,
    grad_down, grad_up, grad_mid, branch, output, parts, branch_own, *scratch,
):
    p = Place(rows, cols)
    width = resid.shape[-1]
    half = grad_up.shape[1]
    share = Share(p, *scratch[:6])
    gather = Spread(p, branch_own, branch, width, *scratch[6:8])
    down = Reduce(p, cot, hidden, scratch[8:11], middle(hidden.shape[0], 0)).into(grad_down)
    up = Reduce(
        p, normed_mid, grad_pre.at[pl.ds(0, half)], scratch[11:14], middle(half, 0)
    ).into(grad_up)
    share_out = Share(p, scratch[0], scratch[14], scratch[2], *scratch[15:18])
    queue = steps(rows, down, up)
    at = lambda t: rows * t // 8
    meet(p.col_peers() + p.row_peers())
    ready("cot", "hidden", "normed_mid", "grad_pre")
    take(queue, 2)
    ready("w_up")
    fill_partial(
        share.part, w_up, grad_pre, cols, rows, width, lambda: take(queue, 1)
    )
    share.start()
    take(queue, 1)
    share.middle()
    ready("cot_own", "resid", "vec", "w_down")
    serve(queue, at(2))
    serve(queue, at(3))
    share.arrive()

    def store(d, value):
        total = cot_own[d].astype(f32) + value
        grad_mid[d] = total
        low = total.astype(bf16)
        branch_own[d] = low
        parts[d, :, 4:5] = jnp.sum(low.astype(f32), axis=1, keepdims=True)
        parts[d, :, 5:6] = jnp.sum(cot_own[d].astype(f32), axis=1, keepdims=True)

    parts[...] = jnp.zeros_like(parts)

    def put(d, gain, shift):
        parts[d, :, 2:3] = gain
        parts[d, :, 3:4] = shift

    norm_back(
        rows,
        width,
        lambda d: share.total(d),
        lambda d: resid[d],
        lambda d: vec[d, :, 3:4],
        store,
        put,
    )
    gather.start()
    share.finish()
    serve(queue, at(4))
    fill_partial(share_out.part, w_down, hidden, cols, rows, width)
    share_out.start()
    serve(queue, at(5))
    share_out.middle()
    gather.forward()
    serve(queue, rows)
    share_out.arrive()

    def result(d, carry):
        output[d] = (resid[d] + share_out.total(d) + vec[d, :, 5:6]).astype(bf16)
        return carry

    lax.fori_loop(0, rows, result, 0)
    down.finish()
    up.finish()
    share_out.finish()
    gather.finish()


def back_two_kernel(
    rows, cols, ready, output, up_one, normed_mid, grad_pre, w_out, branch, att, qkv, logs,
    vec, normed_in, w_qkv, own, grad_mid, parts,
    grad_up_all, wq_o, wo_o, bias_o, units_o, feat_o, res_out, res_f32,
    grad_up, res_tok, grad_tok, grad_qkv, grad_att, dkey, dval, lead_sum, rest_sum, last_sum, out_sum, gq, go, gb,
    units, units_in, qkv_in, feat, feat_in, feat_sum, feat_cols,
    bs, br, ts, tr, es, er, fs, fr, us, ur, ws, wr, loc, *scratch,
):
    p = Place(rows, cols)
    width = own.shape[-1]
    slots = logs.shape[0]
    ch, och = CHANNELS // cols, HD // cols
    ffc = grad_pre.shape[0]
    half = grad_up.shape[1]
    qn = slots * CHANNELS
    share = Share(p, *scratch[:6])
    lead = slots * 4 // 7
    up = Reduce(
        p, normed_mid, grad_pre.at[pl.ds(ffc - half, half)], scratch[6:9], middle(half, 0)
    ).into(grad_up)
    out = Reduce(p, branch, att, scratch[9:12], middle(slots * HD, 1)).into(out_sum)
    filled = (slots - 1) * cols + p.c < H
    wide = [
        Reduce(
            p,
            normed_in,
            grad_qkv.at[pl.ds(first * CHANNELS, count * CHANNELS)],
            scratch[i : i + 3],
            middle(count * CHANNELS, 0),
            only,
        ).into(total)
        for first, count, i, total, only in (
            (0, lead, 12, lead_sum, None),
            (lead, slots - 1 - lead, 15, rest_sum, None),
            (slots - 1, 1, 18, last_sum, filled),
        )
    ]
    last_sum[...] = jnp.zeros_like(last_sum)
    early = steps(rows, up, out)
    late = steps(rows, *wide)
    at = lambda t: rows * t // 8
    back_out = Back(p, output, res_out, (bs, br))
    back_tok = Back(p, grad_tok, res_tok, (ts, tr))
    sources = [(q, back_out.col) for q in range(rows)]
    targets = [home(p, q) for q in range(rows)]
    meet(sources + targets + all_col(p) + all_row(p))
    back_out.start()
    one_copy = pltpu.make_async_copy(
        up_one, grad_up_all.at[:, : ffc - half], loc.at[3]
    )
    one_copy.start()
    ready("normed_mid", "grad_pre", "branch", "att")
    serve(early, 0)
    ready("w_out", "qkv", "logs")
    for s in range(slots):
        total = product(w_out[0, :, s * HD : (s + 1) * HD], branch[0], TN)
        for d in range(1, rows):
            total = total + product(w_out[d, :, s * HD : (s + 1) * HD], branch[d], TN)
        grad_att[s * HD : (s + 1) * HD] = total.astype(bf16)

    def head(s, carry):
        base = pl.multiple_of(s * CHANNELS, 64)

        def store(row, first, last, value):
            grad_qkv[pl.ds(base + row, HD), first:last] = value.astype(bf16)

        attend_back(
            qkv[pl.ds(base, CHANNELS)],
            grad_att[pl.ds(pl.multiple_of(s * HD, 64), HD)],
            logs[s],
            store,
            dkey,
            dval,
        )
        return carry

    third = lead * 3 // 4
    lax.fori_loop(0, third, head, 0)
    serve(early, at(1))
    lax.fori_loop(third, lead, head, 0)
    ready("normed_in")
    take(late, 1)
    serve(early, at(2))
    most = lead + (slots - lead) // 2
    lax.fori_loop(lead, most, head, 0)
    serve(early, at(3))
    lax.fori_loop(most, slots, head, 0)
    serve(early, at(4))
    take(late, 2)
    ready("w_qkv", "own", "parts", "vec", "grad_mid")
    fill_partial(
        share.part, w_qkv, grad_qkv, cols, rows, width, lambda: serve(early, at(5))
    )
    share.start()
    serve(early, at(6))
    take(late, 1)
    share.middle()
    serve(early, rows)
    take(late, 2)
    ones = jnp.ones((8, L), bf16)
    units[:, :ffc] = product(ones, grad_pre[...], NT)[0:1]
    units[:, ffc:] = product(ones, grad_qkv[...], NT)[0:1]
    row_units = []
    for o, peer in enumerate(all_row(p)):
        row_units.append(remote(units, units_in.at[o + 1], us.at[o], ur.at[o], peer))
    for copy in row_units:
        copy.start()
    serve(late, at(2))
    serve(late, at(3))
    for j in range(cols):
        for s in range(slots):
            base = s * HD + j * och
            go[j, :, s * och : (s + 1) * och] = out_sum[:, base : base + och]
    swap_o = exchange_copies(p, go, wo_o, es.at[0], er.at[0])
    for copy in swap_o:
        copy.start()
    serve(late, at(4))
    share.arrive()

    def store_tokens(d, value):
        grad_tok[d] = (grad_mid[d] + value).astype(bf16)

    def put(d, gain, shift):
        parts[d, :, 0:1] = gain
        parts[d, :, 1:2] = shift

    norm_back(
        rows,
        width,
        lambda d: share.total(d),
        lambda d: own[d].astype(f32),
        lambda d: vec[d, :, 0:1],
        store_tokens,
        put,
    )
    eye = (
        lax.broadcasted_iota(jnp.int32, (8, 8), 0) == lax.broadcasted_iota(jnp.int32, (8, 8), 1)
    ).astype(f32)
    for d in range(rows):
        feat[d] = lax.dot_general(
            eye, parts[d], NT, precision=lax.Precision.HIGHEST, preferred_element_type=f32
        )
    feats = []
    for o in range(1, rows):
        to = lax.rem(p.r + o, rows)
        feats.append(remote(feat.at[to], feat_in.at[o], fs.at[o], fr.at[o], (to, p.c)))
    for copy in feats:
        copy.start()
    serve(late, at(5))
    serve(late, rows - 2)
    back_tok.start()
    total = units[...]
    for o, copy in enumerate(row_units):
        copy.wait_recv()
        total = total + units_in[o + 1]
    units_o[...] = total[:, :ffc]
    qkv_in[...] = total[:, ffc:]
    for j in range(cols):
        for s in range(slots):
            base = s * CHANNELS + j * ch
            gb[j, :, s * ch : (s + 1) * ch] = qkv_in[:, base : base + ch]
    swap_b = exchange_copies(p, gb, bias_o, es.at[1], er.at[1])
    for copy in swap_b:
        copy.start()
    total = feat[p.r]
    for o, copy in enumerate(feats):
        copy.wait_recv()
        total = total + feat_in[o + 1]
    feat_sum[...] = total
    sums = [
        remote(feat_sum, feat_cols.at[o + 1], ws.at[o], wr.at[o], peer)
        for o, peer in enumerate(all_col(p))
    ]
    for copy in sums:
        copy.start()
    serve(late, rows)
    for j in range(cols):
        for s in range(slots):
            source, first = lead_sum, 0
            if s >= lead:
                source, first = (rest_sum, lead) if s < slots - 1 else (last_sum, slots - 1)
            base = (s - first) * CHANNELS + j * ch
            gq[j, :, s * ch : (s + 1) * ch] = source[:, base : base + ch]
    for ring in [up, out] + wide:
        ring.finish()
    swap_q = exchange_copies(p, gq, wq_o, es.at[2], er.at[2])
    for copy in swap_q:
        copy.start()
    two_copy = pltpu.make_async_copy(
        grad_up, grad_up_all.at[:, ffc - half :], loc.at[4]
    )
    two_copy.start()
    keeps = [
        pltpu.make_async_copy(src.at[p.c], dst.at[p.c], loc.at[i])
        for i, (src, dst) in enumerate(((gq, wq_o), (go, wo_o), (gb, bias_o)))
    ]
    for copy in keeps:
        copy.start()
    for o, copy in enumerate(sums):
        copy.wait_recv()
        total = total + feat_cols[o + 1]
    feat_o[...] = total
    share.finish()
    back_out.finish()
    back_tok.finish()
    res_f32[...] = res_tok[...].astype(f32)
    one_copy.wait()
    two_copy.wait()
    for copy in swap_o + swap_b + swap_q:
        copy.wait()
    for copy in keeps:
        copy.wait()
    for copy in row_units + feats + sums:
        copy.wait_send()


RAW = ("output", "up_one")
INPUTS = {
    back_one_kernel: (
        "cot", "hidden", "normed_mid", "grad_pre", "w_up", "cot_own", "resid", "vec", "w_down",
    ),
    back_two_kernel: (
        "output", "up_one", "normed_mid", "grad_pre", "w_out", "branch", "att", "qkv", "logs",
        "vec", "normed_in", "w_qkv", "own", "grad_mid", "parts",
    ),
}


def call(kernel, outs, scratch, args, collective, spec=VMEM, in_specs=None, out_specs=None):
    return pl.pallas_call(
        kernel,
        out_shape=[jax.ShapeDtypeStruct(s, t) for s, t in outs],
        in_specs=[spec] * len(args) if in_specs is None else in_specs,
        out_specs=[spec] * len(outs) if out_specs is None else out_specs,
        scratch_shapes=scratch,
        compiler_params=pltpu.CompilerParams(
            collective_id=collective, has_side_effects=True, vmem_limit_bytes=LIMIT
        ),
    )(*args)


def staged(kernel, count, *refs):
    rows, cols, outs = count
    names = INPUTS[kernel]
    ins = len(names)
    rest = list(refs[ins + outs :])
    buffers = [refs[i] if name in RAW else rest.pop(0) for i, name in enumerate(names)]
    sem = rest.pop(0)
    copies = {
        name: pltpu.make_async_copy(refs[i], buffers[i], sem.at[i])
        for i, name in enumerate(names)
        if name not in RAW
    }
    for name in copies:
        copies[name].start()

    def ready(*names):
        for name in names:
            copies[name].wait()

    kernel(rows, cols, ready, *buffers, *refs[ins : ins + outs], *rest)


def call_staged(kernel, rows, cols, outs, scratch, args, collective, out_specs=None):
    return call(
        functools.partial(staged, kernel, (rows, cols, len(outs))),
        outs,
        [
            pltpu.VMEM(arg.shape, arg.dtype)
            for name, arg in zip(INPUTS[kernel], args)
            if name not in RAW
        ]
        + [pltpu.SemaphoreType.DMA((len(args),))]
        + scratch,
        args,
        collective,
        in_specs=[ANY] * len(args),
        out_specs=out_specs,
    )


def one_hot(target, size):
    return (target[:, None] == jnp.arange(size, dtype=jnp.int32)[None, :]).astype(bf16)


def split_matrix(channels, slots, cols):
    source = jnp.arange(channels * H, dtype=jnp.int32)
    channel, head = source // H, source % H
    return one_hot(
        ((head % cols) * slots + head // cols) * channels + channel, cols * slots * channels
    )


def to_owners(weight, matrix):
    return product(weight, matrix, NN).astype(bf16)


def from_owners(blocks, matrix):
    flat = blocks.transpose(1, 0, 2).reshape(blocks.shape[1], -1)
    return product(flat, matrix, NT)


def body(
    tokens, ln1_gain, ln1_shift, weight_qkv, bias_qkv, weight_out, bias_out, ln2_gain,
    ln2_shift, weight_up, bias_up, weight_down, bias_down, cotangent,
):
    rows, cols = lax.axis_size("row"), lax.axis_size("col")
    slots = (H + cols - 1) // cols
    ch, och = CHANNELS // cols, HD // cols
    feats = D // rows
    width = L // cols
    ffc = weight_up.shape[1]
    dma = pltpu.SemaphoreType.DMA

    qkv_split, out_split = split_matrix(ch, slots, cols), split_matrix(och, slots, cols)
    wq = to_owners(weight_qkv, qkv_split)
    wo = to_owners(weight_out, out_split)
    bias = jnp.pad(bias_qkv.reshape(ch, H), ((0, 0), (0, slots * cols - H)))
    bias = bias.reshape(ch, slots, cols).transpose(2, 1, 0).reshape(cols, 1, slots * ch)
    terms = []
    for _ in range(3):
        terms.append(lax.reduce_precision(bias, 8, 7))
        bias = bias - terms[-1]
    bias = jnp.concatenate(terms + [jnp.zeros_like(bias)] * 5, axis=1).astype(bf16)
    zero = jnp.zeros_like(ln1_gain)
    vec = jnp.stack(
        [ln1_gain, ln1_shift, bias_out, ln2_gain, ln2_shift, bias_down, zero, zero]
    )
    (
        w_qkv, w_out, w_up, w_down, normed_in, qkv, att, logs, resid, normed_mid, hidden,
        grad_pre, cot, tok_own, cot_own, vec,
    ) = forward(
        rows,
        cols,
        (tokens, cotangent, wq, wo, bias, vec, weight_up, weight_down, bias_up[:, None]),
        (feats, width, slots, ffc),
    )
    half = ffc // 2 // 128 * 128
    grad_weight_down, grad_up_one, grad_mid, branch, output, parts = call_staged(
        back_one_kernel,
        rows,
        cols,
        [
            ((feats, ffc), f32),
            ((feats, half), f32),
            ((rows, feats, width), f32),
            ((rows, feats, L), bf16),
            ((rows, feats, width), bf16),
            ((rows, feats, 8), f32),
        ],
        [pltpu.VMEM((rows, feats, width), bf16)]
        + share_scratch(rows, cols, feats, width)
        + spread_sems(cols)
        + reduce_scratch(rows, feats, ffc)
        + reduce_scratch(rows, feats, half)
        + [share_scratch(rows, cols, feats, width)[i] for i in (1, 3, 4, 5)],
        (cot, hidden, normed_mid, grad_pre, w_up, cot_own, resid, vec, w_down),
        3,
    )
    qn, on = slots * CHANNELS, slots * HD
    vm = pltpu.VMEM
    lead = slots * 4 // 7 * CHANNELS
    (
        grad_weight_up, gq, go, gb, grad_bias_up, feat, res_out, res_tok
    ) = call_staged(
        back_two_kernel,
        rows,
        cols,
        [
            ((feats, ffc), f32),
            ((cols, feats, slots * ch), bf16),
            ((cols, feats, slots * och), bf16),
            ((cols, 1, slots * ch), f32),
            ((1, ffc), f32),
            ((8, feats), f32),
            ((feats, rows * width), bf16),
            ((feats, rows * width), f32),
        ],
        [
            vm((feats, ffc - half), f32),
            vm((feats, rows * width), bf16),
            vm((rows, feats, width), bf16),
            vm((qn, L), bf16),
            vm((on, L), bf16),
            vm((HD, L), f32),
            vm((HD, L), f32),
            vm((feats, lead), bf16),
            vm((feats, qn - CHANNELS - lead), bf16),
            vm((feats, CHANNELS), bf16),
            vm((feats, on), bf16),
            vm((cols, feats, slots * ch), bf16),
            vm((cols, feats, slots * och), bf16),
            vm((cols, 1, slots * ch), f32),
            vm((1, ffc + qn), f32),
            vm((rows, 1, ffc + qn), f32),
            vm((1, qn), f32),
            vm((rows, 8, feats), f32),
            vm((rows, 8, feats), f32),
            vm((8, feats), f32),
            vm((cols, 8, feats), f32),
        ]
        + [dma((rows + 1,)), dma((rows,))] * 2
        + [dma((3, cols)), dma((3, cols))]
        + [dma((rows,))] * 4
        + [dma((cols,))] * 2
        + [dma((5,))]
        + share_scratch(rows, cols, feats, width)
        + reduce_scratch(rows, feats, ffc - half)
        + reduce_scratch(rows, feats, on)
        + reduce_scratch(rows, feats, lead)
        + reduce_scratch(rows, feats, qn - CHANNELS - lead)
        + reduce_scratch(rows, feats, CHANNELS),
        (
            output, grad_up_one, normed_mid, grad_pre, w_out, branch, att, qkv, logs,
            vec, normed_in, w_qkv, tok_own, grad_mid, parts,
        ),
        4,
        [ANY] + [VMEM] * 5 + [ANY, VMEM],
    )
    grad_weight_qkv = from_owners(gq, qkv_split)
    grad_weight_out = from_owners(go, out_split)
    grad_bias_qkv = gb.reshape(cols, slots, ch).transpose(2, 1, 0)
    grad_bias_qkv = grad_bias_qkv.reshape(ch, slots * cols)[:, :H].reshape(-1)
    return (
        res_out,
        res_tok,
        feat[0],
        feat[1],
        grad_weight_qkv,
        grad_bias_qkv,
        grad_weight_out,
        feat[4],
        feat[2],
        feat[3],
        grad_weight_up,
        grad_bias_up[0],
        grad_weight_down,
        feat[5],
    )


def solution(mesh):
    both, row, col = P("row", "col"), P("row"), P("col")
    in_specs = (both, row, row, both, col, both, row, row, row, both, col, both, row, both)
    out_specs = (both, both, row, row, both, col, both, row, row, row, both, col, both, row)
    return jax.shard_map(body, mesh=mesh, in_specs=in_specs, out_specs=out_specs, check_vma=False)
```
